32 devices in a mesh: grp: 2 (over y), smp: 4 (over z), snp: 2 (over x), pair: 2 (over core).
Axes of the slice: x: 2, y: 2, z: 4, core: 2. Of those that a mesh axis runs over, the one named last changes fastest.
Arguments:
- dosage: bfloat16 [16384, 4096], P(('grp', 'smp'), ('snp', 'pair')), parts along dimension 0, may hold values from 0 to 2
- allele_mean: float32 [8192], P('grp'), parts along dimension 0, may hold values from 0.7 to 1.3
- snp_scale: float32 [8192], P('grp'), parts along dimension 0, may hold values from 1.5 to 4.5
- band_next: int32 [128], P('grp'), parts along dimension 0, may hold values from 1 to 2
- ld_prev: float32 [8192, 320], P(('grp', 'smp')), parts along dimension 0, may hold values from -0.95 to 1, as said below
- band_prev: int32 [128], P('grp'), parts along dimension 0, may hold values from 1 to 2
- zscores: float32 [8192, 512], P(('grp', 'smp'), ('snp', 'pair')), parts along dimension 0, may hold values from -22 to 22
- observed: int32 [8192, 8], P(('grp', 'smp'), ('snp', 'pair')), parts along dimension 0, may hold values 0 or 1
Outputs:
- ld_next: float32 [8192, 320], P(('grp', 'snp', 'pair')), parts along dimension 0
- imputed: float32 [8192, 512], P(('grp', 'smp'), ('snp', 'pair')), parts along dimension 0
The draws below stay inside these ranges and needn't reach their ends.
There are 2 independent parts, one for each index of `grp`. The reference program is written for one: setup_inputs(seed, part) draws one part's arguments, and reference() takes and returns one part's arrays. A program takes and returns all parts, laid end to end along the dimension named above; each array names one. Nothing has to cross between parts.
Inputs may be any that keep to these rules, and one draw needn't show every extreme that they name: `ld_prev`: row i holds the band of a symmetric matrix with unit diagonal: entry (i, o) belongs to column 64 * (i // 64) - 128 + o. For every band mask, the masked matrix plus the identity is positive definite.
All inputs are finite; a program needn't handle non-finite values. No bound on the sum of `observed` on one device may be relied on, other than what follows from the above.
Results may differ from the reference program's by a relative error of at most 0.00049.
Values may be sent and summed in bfloat16 or wider, within the bound.
No kernel may reach another device: no remote copies, remote signals or barrier semaphores. Data moves between devices by JAX's collectives and lax.ppermute only.
A program may use at most 128 MiB of HBM per device.

```python
import math
import jax
import jax.numpy as jnp
from jax import lax

W = 4096
TILE = 64
BMAX = 2
TRAITS = 512
TBLK = 64
ITERS = 3
NT = 64
NBLK = 8
SAMPLES = 8192


def band_of(window, tile_size, span):
    local_rows = window.shape[0]
    tile_count = local_rows // tile_size
    blocks = window.reshape(tile_count, tile_size, tile_count + span - 1, tile_size)
    pieces = []
    for offset in range(span):
        diagonal = jnp.diagonal(blocks[:, :, offset:offset + tile_count, :], axis1=0, axis2=2)
        pieces.append(jnp.transpose(diagonal, (2, 0, 1)))
    return jnp.concatenate(pieces, axis=2).reshape(local_rows, span * tile_size)


def ld_dense(key):
    base_key = jax.random.fold_in(key, 11)
    sign_key, step_key, hot_key, jitter_key = jax.random.split(base_key, 4)
    allele_sign = jnp.where(jax.random.randint(sign_key, (W,), 0, 2) == 0, -1.0, 1.0).astype(jnp.float32)
    hotspot = jax.random.randint(hot_key, (W,), 0, 16) == 0
    base_step = jnp.exp(jax.random.uniform(step_key, (W,), jnp.float32, jnp.log(0.02), jnp.log(1.0)))
    step_sizes = jnp.where(hotspot, 4.0, base_step)
    jitter_raw = jax.random.uniform(jitter_key, (W, W), jnp.float32, 0.5, 1.5)
    position = jnp.cumsum(step_sizes)
    distance = jnp.abs(position[:, None] - position[None, :])
    jitter = 0.5 * (jitter_raw + jitter_raw.T)
    tile_of = jnp.arange(W, dtype=jnp.int32) // TILE
    in_band = jnp.abs(tile_of[:, None] - tile_of[None, :]) <= BMAX
    identity = jnp.eye(W, dtype=jnp.float32)
    kernel = jnp.where(in_band, jnp.exp(-distance) * jitter, 0.0) * (1.0 - identity)
    row_weight = jnp.sum(kernel, axis=1)
    balance = 1.0 / jnp.sqrt(row_weight)
    balanced = balance[:, None] * kernel * balance[None, :]
    largest = jnp.max(jnp.sum(balanced, axis=1))
    scaled = jnp.minimum(1.8 * balanced / largest, 0.95)
    return allele_sign[:, None] * scaled * allele_sign[None, :] + identity


def draw_dosage(key, part):
    block_rows = SAMPLES // 8
    hot_key = jax.random.fold_in(key, 7)
    hotspot = jax.random.randint(hot_key, (W,), 0, 8) == 0
    threshold = jnp.where(hotspot, 32, 1)
    column = lax.broadcasted_iota(jnp.int32, (block_rows, W), 1)

    def one_block(block_index):
        block_key = jax.random.fold_in(key, block_index + 100)
        summed = jnp.zeros((block_rows, W), jnp.float32)
        for haplotype in range(2):
            hap_key = jax.random.fold_in(block_key, haplotype)
            break_key, fresh_key, jitter_key = jax.random.split(hap_key, 3)
            breaks = jax.random.randint(break_key, (block_rows, W), 0, 64)
            starts = (breaks < threshold[None, :]) | (column == 0)
            source = lax.cummax(jnp.where(starts, column, 0), axis=1)
            fresh_draw = jax.random.uniform(fresh_key, (block_rows, W), jnp.float32)
            carried = jnp.take_along_axis(fresh_draw, source, axis=1)
            jitter = jax.random.uniform(jitter_key, (block_rows, W), jnp.float32)
            summed = summed + 0.8 * carried + 0.2 * jitter
        return summed.astype(jnp.bfloat16)
    blocks = lax.map(one_block, jnp.arange(8, dtype=jnp.int32))
    return blocks.reshape(SAMPLES, W)


def draw_ld_prev(key, part):
    symmetric = ld_dense(key)
    band_reach = TILE * BMAX
    padded = jnp.pad(symmetric, ((0, 0), (band_reach, band_reach)))
    return band_of(padded, TILE, 2 * BMAX + 1)


def draw_zscores(key, part):
    base_key = jax.random.fold_in(key, 13)
    column_key = jax.random.fold_in(base_key, 0)
    value_key = jax.random.fold_in(base_key, 1)
    causal_key = jax.random.fold_in(base_key, 3)
    effect_key = jax.random.fold_in(base_key, 4)
    amp_key = jax.random.fold_in(base_key, 5)
    linkage = ld_dense(key)
    positions = jnp.arange(W, dtype=jnp.float32)
    row_factor = 0.6 * jnp.exp(jnp.log(3.0) * positions / (W - 1))
    column_factor = jnp.exp(jax.random.uniform(column_key, (TRAITS,), jnp.float32, jnp.log(0.3), jnp.log(2.0)))
    amplitude = jnp.exp(jax.random.uniform(amp_key, (TRAITS,), jnp.float32, jnp.log(0.1), jnp.log(2.0)))
    causal = jax.random.randint(causal_key, (W, TRAITS), 0, 64) == 0
    effect = jnp.where(causal, jax.random.uniform(effect_key, (W, TRAITS), jnp.float32, -1.0, 1.0), 0.0)
    signal = jnp.dot(linkage, effect, precision=lax.Precision.HIGHEST)
    background = jnp.clip(jax.random.normal(value_key, (W, TRAITS), jnp.float32), -2.8, 2.8)
    values = row_factor[:, None] * background + amplitude[None, :] * signal
    return column_factor[None, :] * values


def place_ends(entries, stream_key, smallest, top_value):
    place = [jax.random.randint(jax.random.fold_in(stream_key, axis), (), 0, length) for axis, length in enumerate(entries.shape)]
    widest = entries.shape.index(max(entries.shape))
    beside = place[:widest] + [(place[widest] + 1) % entries.shape[widest]] + place[widest + 1:]
    return entries.at[tuple(place)].set(smallest).at[tuple(beside)].set(top_value)


def setup_inputs(seed: int = 0, part: int = 0) -> dict:
    arg_keys = jax.random.split(jax.random.key(seed), 9)
    own_keys = jax.random.split(jax.random.fold_in(arg_keys[8], part), 9)
    return {
        "dosage": draw_dosage(jax.random.fold_in(jax.random.fold_in(arg_keys[8], part), 71), part),
        "allele_mean": jnp.clip(jax.random.uniform(own_keys[1], (W,), jnp.float32, 0.7, 1.3), 0.7, 1.3),
        "snp_scale": jnp.clip(jnp.exp(jax.random.uniform(own_keys[2], (W,), jnp.float32, math.log(1.5), math.log(4.5))), 1.5, 4.5),
        "band_next": place_ends(jax.random.randint(own_keys[3], (NT,), 1, BMAX + 1), jax.random.fold_in(own_keys[3], 1), 1, BMAX).astype(jnp.int32),
        "ld_prev": draw_ld_prev(jax.random.fold_in(jax.random.fold_in(arg_keys[8], part), 71), part),
        "band_prev": place_ends(jax.random.randint(own_keys[5], (NT,), 1, BMAX + 1), jax.random.fold_in(own_keys[5], 1), 1, BMAX).astype(jnp.int32),
        "zscores": draw_zscores(jax.random.fold_in(jax.random.fold_in(arg_keys[8], part), 71), part),
        "observed": place_ends((jax.random.randint(own_keys[7], (W, NBLK), 0, 4) < 3).astype(jnp.int32), jax.random.fold_in(own_keys[7], 1), 0, 1),
    }


ridge_term = 1.0


def tile_table(widths, reach_tiles):
    tile_total = widths.shape[0]
    padded = jnp.pad(widths, reach_tiles)
    columns = []
    for offset in range(-reach_tiles, reach_tiles + 1):
        beside = padded[reach_tiles + offset:reach_tiles + offset + tile_total]
        columns.append(abs(offset) <= jnp.minimum(widths, beside))
    return jnp.stack(columns, axis=1).astype(jnp.float32)


def expand_table(table, tile_size):
    return jnp.repeat(jnp.repeat(table, tile_size, axis=0), tile_size, axis=1)


def reference(dosage, allele_mean, snp_scale, band_next, ld_prev, band_prev, zscores, observed):
    band_reach = TILE * BMAX
    band_cols = (2 * BMAX + 1) * TILE
    padded_dose = jnp.pad(dosage, ((0, 0), (band_reach, band_reach)))
    padded_mean = jnp.pad(allele_mean, band_reach)
    padded_scale = jnp.pad(snp_scale, band_reach)

    def tile_gram(tile_index):
        first_col = (tile_index * TILE).astype(jnp.int32)
        columns = lax.dynamic_slice_in_dim(padded_dose, first_col, band_cols, 1)
        mean_part = lax.dynamic_slice_in_dim(padded_mean, first_col, band_cols, 0)
        scale_part = lax.dynamic_slice_in_dim(padded_scale, first_col, band_cols, 0)
        normed = ((columns.astype(jnp.float32) - mean_part) * scale_part).astype(jnp.bfloat16)
        own_block = normed[:, band_reach:band_reach + TILE]
        return jnp.dot(own_block.T, normed, preferred_element_type=jnp.float32)

    gram = lax.map(tile_gram, jnp.arange(NT, dtype=jnp.int32)).reshape(W, band_cols)
    next_mask = expand_table(tile_table(band_next, BMAX), TILE)
    ld_next = next_mask * gram / SAMPLES

    band = expand_table(tile_table(band_prev, BMAX), TILE) * ld_prev
    seen = jnp.repeat(observed.astype(jnp.float32), TBLK, axis=1)
    tiles = band.reshape(NT, TILE, band_cols)

    def apply_band(vector):
        padded = jnp.pad(vector, ((band_reach, band_reach), (0, 0)))
        stacked = padded.reshape(NT + 2 * BMAX, TILE, TRAITS)
        windows = jnp.concatenate([stacked[offset:offset + NT] for offset in range(2 * BMAX + 1)], axis=1)
        result = jnp.einsum("uio,uot->uit", tiles, windows, precision=lax.Precision.HIGHEST)
        return result.reshape(W, TRAITS)

    def operate(vector):
        masked = seen * vector
        return seen * (apply_band(masked) + ridge_term * masked) + (1.0 - seen) * vector

    rhs = seen * zscores
    solution = jnp.zeros_like(rhs)
    residual = rhs
    direction = rhs
    norm_now = jnp.sum(residual * residual, axis=0)
    for turn_index in range(ITERS):
        image = operate(direction)
        step_size = norm_now / jnp.sum(direction * image, axis=0)
        solution = solution + step_size * direction
        residual = residual - step_size * image
        norm_next = jnp.sum(residual * residual, axis=0)
        direction = residual + (norm_next / norm_now) * direction
        norm_now = norm_next
    imputed = apply_band(seen * solution)
    return ld_next, imputed
```

```python
import functools
import jax
import jax.numpy as jnp
from jax import lax
from jax.experimental import pallas as pl
from jax.experimental.pallas import tpu as pltpu
from jax.sharding import PartitionSpec as P

TILE = 64
BMAX = 2
TBLK = 64
ITERS = 3
RIDGE = 1.0
SPAN = 2 * BMAX + 1
REACH = TILE * BMAX
LANE = 128
QW = 256
HZ = ITERS * REACH
HB = (ITERS - 1) * REACH
TINY = 1e-6
VMEM_LIMIT = 60 * 1024 * 1024
VMEM = pl.BlockSpec(memory_space=pltpu.VMEM)
SMEM = pl.BlockSpec(memory_space=pltpu.SMEM)


def params(**kw):
    return pltpu.CompilerParams(vmem_limit_bytes=VMEM_LIMIT, **kw)


def mask_rows(band_ref, first_tile, total):
    def width(t):
        inside = (t >= 0) & (t < total)
        return jnp.where(inside, band_ref[jnp.clip(t, 0, total - 1)], 0)

    widths = [width(first_tile + d) for d in range(-BMAX, BMAX + 2)]
    low = lax.broadcasted_iota(jnp.int32, (1, LANE), 1) < TILE
    rows = []
    for q in range(-BMAX, BMAX + 1):
        flags = [
            (abs(q) <= jnp.minimum(widths[BMAX + t], widths[BMAX + t + q])).astype(jnp.float32)
            for t in range(2)
        ]
        rows.append(jnp.where(low, flags[0], flags[1]))
    return rows


def low_lanes(shape):
    return lax.broadcasted_iota(jnp.int32, shape, 1) < TILE


def tdot(left, right):
    return lax.dot_general(
        left, right, (((0,), (0,)), ((), ())), preferred_element_type=jnp.float32
    )


def dot(left, right):
    return lax.dot_general(
        left, right, (((1,), (0,)), ((), ())), preferred_element_type=jnp.float32
    )


def gram_kernel(
    parts, rot, inv, meta, own, ahead, right, left, first, mean, scale, *rest
):
    outs = rest[:parts]
    normed, cross = rest[parts:]
    g = pl.program_id(0)
    quarter = lax.rem(g + meta[0], parts) if rot else g
    blocks = QW // LANE
    base = meta[1]
    lanes_total = mean.shape[0]

    def standard(values, block):
        row = jnp.clip(block, 0, lanes_total - 1)
        m = mean[pl.ds(row, 1), :]
        s = scale[pl.ds(row, 1), :]
        return ((values.astype(jnp.float32) - m) * s).astype(jnp.bfloat16)

    for b in range(blocks):
        cols = slice(b * LANE, (b + 1) * LANE)
        normed[:, cols] = standard(own[:, cols], base + quarter * blocks + b)
    beyond = base + (quarter + 1) * blocks
    tail = slice(QW, QW + LANE)

    @pl.when(quarter == parts - 1)
    def _():
        normed[:, tail] = standard(right[...], beyond)

    @pl.when(quarter != parts - 1)
    def _():
        normed[:, tail] = standard(ahead[...], beyond)

    @pl.when(g == 0)
    def _():
        cross[...] = inv * tdot(standard(left[...], base - 1), standard(first[...], base))

    full = tdot(normed[...], normed[:, :QW])
    rows = (BMAX + 1) * TILE
    low = low_lanes((rows, LANE))
    pieces = []
    for b in range(blocks):
        cols = slice(b * LANE, (b + 1) * LANE)
        pieces.append(
            inv
            * jnp.where(
                low,
                full[b * LANE : b * LANE + rows, cols],
                full[b * LANE + TILE : b * LANE + TILE + rows, cols],
            )
        )
    share = LANE // parts // blocks
    start = pl.multiple_of(quarter * (share * blocks), 8)
    shares = [cross[pl.ds(pl.multiple_of(start + b * share, 8), share), :] for b in range(blocks)]
    for i in range(parts):

        @pl.when(g == i)
        def _(i=i):
            for b in range(blocks):
                cols = slice(b * LANE, (b + 1) * LANE)
                outs[i][0:rows, cols] = pieces[b]
                outs[i][rows : rows + share, cols] = shares[b]


def gram_parts(dosage, left, right, mean, scale, k, column_place, rot, inv):
    samples, cols = dosage.shape
    parts = cols // QW
    blocks = QW // LANE
    total = cols // LANE
    height = (BMAX + 1) * TILE + LANE // parts // blocks
    meta = jnp.stack([k, column_place * total]).astype(jnp.int32)

    def quarter(g, m):
        return lax.rem(g + m[0], parts) if rot else g

    fixed = lambda g, m: (0, 0)
    grid_spec = pltpu.PrefetchScalarGridSpec(
        num_scalar_prefetch=1,
        grid=(parts,),
        in_specs=[
            pl.BlockSpec((samples, QW), lambda g, m: (0, quarter(g, m))),
            pl.BlockSpec(
                (samples, LANE),
                lambda g, m: (0, jnp.minimum((quarter(g, m) + 1) * blocks, total - 1)),
            ),
            pl.BlockSpec((samples, LANE), fixed),
            pl.BlockSpec((samples, LANE), fixed),
            pl.BlockSpec((samples, LANE), fixed),
            pl.BlockSpec((mean.shape[0] // LANE, LANE), fixed),
            pl.BlockSpec((mean.shape[0] // LANE, LANE), fixed),
        ],
        out_specs=[pl.BlockSpec((height, QW), fixed) for _ in range(parts)],
        scratch_shapes=[
            pltpu.VMEM((samples, QW + LANE), jnp.bfloat16),
            pltpu.VMEM((LANE, LANE), jnp.float32),
        ],
    )
    return pl.pallas_call(
        functools.partial(gram_kernel, parts, rot, inv),
        grid_spec=grid_spec,
        out_shape=[jax.ShapeDtypeStruct((height, QW), jnp.float32) for _ in range(parts)],
        compiler_params=params(dimension_semantics=("arbitrary",)),
        cost_estimate=pl.CostEstimate(
            flops=2 * samples * cols * (QW + LANE), bytes_accessed=dosage.size * 4, transcendentals=0
        ),
        name="gram",
    )(
        meta,
        dosage,
        dosage,
        right,
        left,
        dosage,
        mean.reshape(-1, LANE),
        scale.reshape(-1, LANE),
    )


def assemble_kernel(parts, rot, tile_total, meta, band, *rest):
    ins = rest[:parts]
    out = rest[parts]
    blocks = QW // LANE
    rows = (BMAX + 1) * TILE
    low = low_lanes((TILE, LANE))
    share = LANE // parts // blocks
    for quarter in range(parts):

        def fetch(row, count, b, quarter=quarter):
            cols = slice(b * LANE, (b + 1) * LANE)
            return ins[quarter][row : row + count, cols]

        for b in range(blocks):
            a = quarter * blocks + b
            cols = slice(a * LANE, (a + 1) * LANE)
            masks = mask_rows(band, meta[1] + 2 * a, tile_total)
            for q in range(BMAX + 1):
                out[(BMAX + q) * TILE : (BMAX + q + 1) * TILE, cols] = (
                    fetch(q * TILE, TILE, b) * masks[BMAX + q]
                )
            turned = fetch(TILE, 2 * TILE, b).T
            rolled = pltpu.roll(turned, TILE, axis=1)
            if a == 0:
                count = LANE // share
                cross = [
                    ins[j // blocks][
                        rows : rows + share, (j % blocks) * LANE : (j % blocks + 1) * LANE
                    ]
                    for j in range(count)
                ]
                cross = jnp.concatenate(cross, axis=0)
                one_low, two_low, two_high = cross[TILE:], cross[:TILE], cross[TILE:]
            else:
                one_low, two_low, two_high = last_turned[TILE:], last_rolled[:TILE], last_turned[TILE:]
            out[TILE : 2 * TILE, cols] = jnp.where(low, one_low, rolled[:TILE]) * masks[1]
            out[0:TILE, cols] = jnp.where(low, two_low, two_high) * masks[0]
            last_turned, last_rolled = turned, rolled


def assemble(pieces, band_next, first_tile, cols):
    parts = len(pieces)
    meta = jnp.stack([first_tile * 0, first_tile]).astype(jnp.int32)
    return pl.pallas_call(
        functools.partial(assemble_kernel, parts, False, band_next.shape[0]),
        in_specs=[SMEM, SMEM] + [VMEM] * parts,
        out_specs=VMEM,
        out_shape=jax.ShapeDtypeStruct((SPAN * TILE, cols), jnp.float32),
        compiler_params=params(),
        name="assemble",
    )(meta, band_next, *pieces)


def krylov_kernel(
    tile_total, sb, meta, band, ldt, z, obs, halo_l, halo_r, w_out, mom_out,
    dh, dl, ucat, seen, u_prev, y
):
    rows = ldt.shape[1]
    traits = z.shape[1]
    own_blocks = rows // LANE
    zb = HZ // LANE
    bb = HB // LANE
    first_tile = meta[0]
    nb = obs.shape[0]
    ld_rows = SPAN * TILE
    total_blocks = own_blocks + 2 * zb

    for c in range(total_blocks):
        if c < zb:
            vec = halo_l[c * LANE : (c + 1) * LANE, :traits]
            flags = [
                halo_l[HZ + bb * ld_rows + c * nb + i : HZ + bb * ld_rows + c * nb + i + 1, :]
                for i in range(nb)
            ]
        elif c < zb + own_blocks:
            o = c - zb
            vec = z[o * LANE : (o + 1) * LANE, :]
            flags = [
                obs[i : i + 1, o * LANE : (o + 1) * LANE].astype(jnp.float32) for i in range(nb)
            ]
        else:
            o = c - zb - own_blocks
            vec = halo_r[o * LANE : (o + 1) * LANE, :traits]
            flags = [
                halo_r[HZ + bb * ld_rows + o * nb + i : HZ + bb * ld_rows + o * nb + i + 1, :]
                for i in range(nb)
            ]
        wide = jnp.concatenate(
            [jnp.broadcast_to(f, (TBLK, LANE)) for f in flags], axis=0
        )
        mask = wide.T
        here = slice(c * LANE, (c + 1) * LANE)
        seen[here, :] = mask
        start = mask * vec
        high = start.astype(jnp.bfloat16)
        u_prev[here, :] = start
        ucat[here, :traits] = high
        ucat[here, traits:] = (start - high.astype(jnp.float32)).astype(jnp.bfloat16)

    per = sb // LANE
    low = low_lanes((TILE, LANE))
    sub = lax.broadcasted_iota(jnp.int32, (TILE, LANE), 0)
    lane = lax.broadcasted_iota(jnp.int32, (TILE, LANE), 1)
    chunks = SPAN + 1
    for c in range(own_blocks + 2 * bb):
        if c < bb:
            get = lambda q, c=c: halo_l[HZ + c * ld_rows + q * TILE : HZ + c * ld_rows + (q + 1) * TILE, :]
        elif c < bb + own_blocks:
            get = lambda q, c=c: ldt[q * TILE : (q + 1) * TILE, (c - bb) * LANE : (c - bb + 1) * LANE]
        else:
            o = c - bb - own_blocks
            get = lambda q, o=o: halo_r[HZ + o * ld_rows + q * TILE : HZ + o * ld_rows + (q + 1) * TILE, :]
        masks = mask_rows(band, first_tile + 2 * (c - bb), tile_total)
        s, h = c // per, c % per
        cols = slice(h * LANE, (h + 1) * LANE)
        parts = [get(q) * masks[q] for q in range(SPAN)]
        zero = jnp.zeros((TILE, LANE), jnp.float32)
        for j in range(chunks):
            left = parts[j] if j < SPAN else zero
            right = parts[j - 1] if j >= 1 else zero
            value = jnp.where(low, left, right)
            if BMAX <= j < BMAX + 2:
                value = value - (sub + TILE * (j - BMAX) == lane).astype(jnp.float32)
            high = value.astype(jnp.bfloat16)
            at = slice(h * LANE + j * TILE, h * LANE + (j + 1) * TILE)
            dh[s, at, cols] = high
            dl[s, at, cols] = (value - high.astype(jnp.float32)).astype(jnp.bfloat16)
        for x in range(per):
            if x < h:
                at = slice(x * LANE, (x + 1) * LANE)
            elif x > h:
                at = slice((x + 2) * LANE, (x + 3) * LANE)
            else:
                continue
            blank = jnp.zeros((LANE, LANE), jnp.bfloat16)
            dh[s, at, cols] = blank
            dl[s, at, cols] = blank

    supers = (rows + 2 * HB) // sb
    window = sb + 2 * REACH

    def product(both, rest):
        return both[:, :traits] + both[:, traits:] + rest

    def apply():
        for s in range(supers):
            vec = ucat[REACH + s * sb : REACH + (s + 1) * sb, :]
            part = product(dot(dh[s], vec), dot(dl[s], vec[:, :traits]))
            at = s * sb
            if s == 0:
                y[at : at + window, :] = part
            else:
                y[at : at + 2 * REACH, :] += part[: 2 * REACH]
                y[at + 2 * REACH : at + window, :] = part[2 * REACH :]

    own = slice(HZ, HZ + rows)
    sums = []
    for step in range(ITERS):
        apply()
        if step == 0:
            for edge_rows, edge_cols, s, target, source in (
                (slice(0, LANE), slice(0, LANE), 0, 1, 0),
                (
                    slice(window - LANE, window),
                    slice(sb - LANE, sb),
                    supers - 1,
                    total_blocks - 2,
                    total_blocks - 1,
                ),
            ):
                vec = ucat[source * LANE : (source + 1) * LANE, :]
                part = product(
                    tdot(dh[s, edge_rows, edge_cols], vec),
                    tdot(dl[s, edge_rows, edge_cols], vec[:, :traits]),
                )
                y[target * LANE : (target + 1) * LANE, :] += part
        u_own = u_prev[own, :]
        y_own = y[own, :]
        w_out[step] = u_own + y_own
        sums.append(jnp.sum(u_own * u_own, axis=0, keepdims=True))
        sums.append(jnp.sum(u_own * y_own, axis=0, keepdims=True))
        if step < ITERS - 1:
            edge = (step + 1) * REACH
            here = slice(edge, total_blocks * LANE - edge)
            nxt = seen[here, :] * y[here, :]
            high = nxt.astype(jnp.bfloat16)
            u_prev[here, :] = nxt
            ucat[here, :traits] = high
            ucat[here, traits:] = (nxt - high.astype(jnp.float32)).astype(jnp.bfloat16)
    mom_out[...] = jnp.concatenate(
        sums + [jnp.zeros((8 - len(sums), traits), jnp.float32)], axis=0
    )


def krylov(ldt, z, obs, halo_l, halo_r, band_prev, first_tile):
    rows, traits = z.shape
    wide = rows + 2 * HB
    sb = 2 * LANE if wide % (2 * LANE) == 0 else LANE
    ext = rows + 2 * HZ
    supers = wide // sb
    meta = first_tile.reshape(1).astype(jnp.int32)
    return pl.pallas_call(
        functools.partial(krylov_kernel, band_prev.shape[0], sb),
        in_specs=[SMEM, SMEM] + [VMEM] * 5,
        out_specs=[VMEM, VMEM],
        out_shape=[
            jax.ShapeDtypeStruct((ITERS, rows, traits), jnp.float32),
            jax.ShapeDtypeStruct((8, traits), jnp.float32),
        ],
        scratch_shapes=[
            pltpu.VMEM((supers, sb + 2 * REACH, sb), jnp.bfloat16),
            pltpu.VMEM((supers, sb + 2 * REACH, sb), jnp.bfloat16),
            pltpu.VMEM((ext, 2 * traits), jnp.bfloat16),
            pltpu.VMEM((ext, traits), jnp.float32),
            pltpu.VMEM((ext, traits), jnp.float32),
            pltpu.VMEM((ext, traits), jnp.float32),
        ],
        compiler_params=params(),
        cost_estimate=pl.CostEstimate(
            flops=ITERS * 6 * ext * SPAN * TILE * traits, bytes_accessed=ldt.size * 4, transcendentals=0
        ),
        name="krylov",
    )(meta, band_prev, ldt, z, obs, halo_l, halo_r)


def combine_kernel(w, mom, out):
    m = [mom[i : i + 1, :] for i in range(2 * ITERS)]
    shift = 1.0 + RIDGE
    h = [shift * m[i] + m[i + 1] for i in range(2 * ITERS - 1)]
    d0 = h[0]
    l10 = h[1] / d0
    l20 = h[2] / d0
    d1 = h[2] - l10 * h[1]
    t12 = h[3] - l20 * h[1]
    ok1 = d1 > TINY * h[2]
    r1 = jnp.where(ok1, 1.0 / jnp.where(ok1, d1, 1.0), 0.0)
    l21 = t12 * r1
    d2 = h[4] - l20 * h[2] - l21 * t12
    ok2 = ok1 & (d2 > TINY * h[4])
    r2 = jnp.where(ok2, 1.0 / jnp.where(ok2, d2, 1.0), 0.0)
    z0 = m[0]
    z1 = m[1] - l10 * z0
    z2 = m[2] - l20 * z0 - l21 * z1
    c2 = z2 * r2
    c1 = z1 * r1 - l21 * c2
    c0 = z0 / d0 - l10 * c1 - l20 * c2
    out[...] = c0 * w[0] + c1 * w[1] + c2 * w[2]


def combine(w, mom):
    return pl.pallas_call(
        combine_kernel,
        in_specs=[VMEM, VMEM],
        out_specs=VMEM,
        out_shape=jax.ShapeDtypeStruct(w.shape[1:], jnp.float32),
        compiler_params=params(),
        name="combine",
    )(w, mom)


def packed(z, ldt, obs):
    z = jnp.pad(z, ((0, 0), (0, LANE - z.shape[1])))
    obs = obs.astype(jnp.float32)
    parts = [z]
    parts += [ldt[:, i : i + LANE] for i in range(0, ldt.shape[1], LANE)]
    parts += [obs[:, i : i + LANE] for i in range(0, obs.shape[1], LANE)]
    height = sum(p.shape[0] for p in parts)
    parts.append(jnp.zeros((-height % 8, LANE), jnp.float32))
    return jnp.concatenate(parts, axis=0)


def halos(z, ldt, obs, axis):
    count = lax.axis_size(axis)
    rows = z.shape[0]

    def shifted(value, by):
        pairs = [(i, i + by) for i in range(count) if 0 <= i + by < count]
        return lax.ppermute(value, axis, pairs)

    if rows >= HZ:
        last = packed(z[rows - HZ :], ldt[:, rows - HB :], obs[:, rows - HZ :])
        head = packed(z[:HZ], ldt[:, :HB], obs[:, :HZ])
        return shifted(last, 1), shifted(head, -1)

    def gather(value, width, dim):
        lefts, rights = [], []
        hop, have = 1, 0
        while have < width:
            take = min(rows, width - have)
            lefts.insert(0, shifted(lax.slice_in_dim(value, rows - take, rows, axis=dim), hop))
            rights.append(shifted(lax.slice_in_dim(value, 0, take, axis=dim), -hop))
            have += take
            hop += 1
        return jnp.concatenate(lefts, dim), jnp.concatenate(rights, dim)

    zs = gather(z, HZ, 0)
    lds = gather(ldt, HB, 1)
    seens = gather(obs, HZ, 1)
    return packed(zs[0], lds[0], seens[0]), packed(zs[1], lds[1], seens[1])


def local(dosage, allele_mean, snp_scale, band_next, ld_prev, band_prev, zscores, observed):
    samples, cols = dosage.shape
    rows = ld_prev.shape[0]
    n_smp = lax.axis_size("smp")
    k = lax.axis_index("smp")
    snp, pair = lax.axis_index("snp"), lax.axis_index("pair")
    n_snp, n_pair = lax.axis_size("snp"), lax.axis_size("pair")
    place = snp * n_pair + pair
    count = n_snp * n_pair

    ldt = ld_prev.T
    obs = observed.T
    halo_l, halo_r = halos(zscores, ldt, obs, "smp")

    line = ("snp", "pair")
    right = lax.ppermute(dosage[:, :LANE], line, [(i + 1, i) for i in range(count - 1)])
    left = lax.ppermute(dosage[:, cols - LANE :], line, [(i, i + 1) for i in range(count - 1)])

    parts = cols // QW
    rot = parts == n_smp
    inv = 1.0 / (samples * n_smp)
    blocks = gram_parts(dosage, left, right, allele_mean, snp_scale, k, place, rot, inv)
    if rot:
        cycle = lambda value, by: lax.ppermute(
            value, "smp", [(i, (i + by) % n_smp) for i in range(n_smp)]
        )
        total = blocks[0]
        for by in range(1, n_smp):
            total = total + cycle(blocks[by].astype(jnp.float16), by).astype(jnp.float32)
        total = total.astype(jnp.float16)
        ring = [total] + [cycle(total, by) for by in range(1, n_smp)]
        stacked = jnp.stack(ring)
        pieces = [
            lax.dynamic_index_in_dim(stacked, lax.rem(k + n_smp - q, n_smp), 0, keepdims=False).astype(
                jnp.float32
            )
            for q in range(parts)
        ]
    else:
        pieces = lax.psum(tuple(blocks), "smp")
    ldn = assemble(pieces, band_next, place * (cols // TILE), cols)

    w, mom = krylov(ldt, zscores, obs, halo_l, halo_r, band_prev, k * (rows // TILE))
    imputed = combine(w, lax.psum(mom, "smp"))
    return ldn.T, imputed


def solution(mesh):
    return jax.shard_map(
        local,
        mesh=mesh,
        in_specs=(
            P(("grp", "smp"), ("snp", "pair")),
            P("grp"),
            P("grp"),
            P("grp"),
            P(("grp", "smp"), None),
            P("grp"),
            P(("grp", "smp"), ("snp", "pair")),
            P(("grp", "smp"), ("snp", "pair")),
        ),
        out_specs=(P(("grp", "snp", "pair"), None), P(("grp", "smp"), ("snp", "pair"))),
        check_vma=False,
    )
```

```python
import functools
import jax
import jax.numpy as jnp
from jax import lax
from jax.experimental import pallas as pl
from jax.experimental.pallas import tpu as pltpu
from jax.sharding import PartitionSpec as P

TILE = 64
BMAX = 2
TBLK = 64
ITERS = 3
RIDGE = 1.0
SPAN = 2 * BMAX + 1
REACH = TILE * BMAX
LANE = 128
QW = 256
HZ = ITERS * REACH
HB = (ITERS - 1) * REACH
TINY = 1e-6
VMEM_LIMIT = 28 * 1024 * 1024
VMEM = pl.BlockSpec(memory_space=pltpu.VMEM)
SMEM = pl.BlockSpec(memory_space=pltpu.SMEM)


def params(**kw):
    return pltpu.CompilerParams(vmem_limit_bytes=VMEM_LIMIT, **kw)


def mask_rows(band_ref, first_tile, total):
    def width(t):
        inside = (t >= 0) & (t < total)
        return jnp.where(inside, band_ref[jnp.clip(t, 0, total - 1)], 0)

    widths = [width(first_tile + d) for d in range(-BMAX, BMAX + 2)]
    low = lax.broadcasted_iota(jnp.int32, (1, LANE), 1) < TILE
    rows = []
    for q in range(-BMAX, BMAX + 1):
        flags = [
            (abs(q) <= jnp.minimum(widths[BMAX + t], widths[BMAX + t + q])).astype(jnp.float32)
            for t in range(2)
        ]
        rows.append(jnp.where(low, flags[0], flags[1]))
    return rows


def low_lanes(shape):
    return lax.broadcasted_iota(jnp.int32, shape, 1) < TILE


def tdot(left, right):
    return lax.dot_general(
        left, right, (((0,), (0,)), ((), ())), preferred_element_type=jnp.float32
    )


def dot(left, right):
    return lax.dot_general(
        left, right, (((1,), (0,)), ((), ())), preferred_element_type=jnp.float32
    )


def gram_kernel(
    parts, rot, inv, meta, own, ahead, right, left, first, mean, scale, *rest
):
    outs = rest[:parts]
    normed, cross = rest[parts:]
    g = pl.program_id(0)
    quarter = lax.rem(g + meta[0], parts) if rot else g
    blocks = QW // LANE
    base = meta[1]
    lanes_total = mean.shape[0]

    def standard(values, block):
        row = jnp.clip(block, 0, lanes_total - 1)
        m = mean[pl.ds(row, 1), :]
        s = scale[pl.ds(row, 1), :]
        return ((values.astype(jnp.float32) - m) * s).astype(jnp.bfloat16)

    for b in range(blocks):
        cols = slice(b * LANE, (b + 1) * LANE)
        normed[:, cols] = standard(own[:, cols], base + quarter * blocks + b)
    beyond = base + (quarter + 1) * blocks
    tail = slice(QW, QW + LANE)

    @pl.when(quarter == parts - 1)
    def _():
        normed[:, tail] = standard(right[...], beyond)

    @pl.when(quarter != parts - 1)
    def _():
        normed[:, tail] = standard(ahead[...], beyond)

    @pl.when(g == 0)
    def _():
        cross[...] = inv * tdot(standard(left[...], base - 1), standard(first[...], base))

    full = tdot(normed[...], normed[:, :QW])
    rows = (BMAX + 1) * TILE
    low = low_lanes((rows, LANE))
    pieces = []
    for b in range(blocks):
        cols = slice(b * LANE, (b + 1) * LANE)
        pieces.append(
            inv
            * jnp.where(
                low,
                full[b * LANE : b * LANE + rows, cols],
                full[b * LANE + TILE : b * LANE + TILE + rows, cols],
            )
        )
    share = LANE // parts // blocks
    start = pl.multiple_of(quarter * (share * blocks), 8)
    shares = [cross[pl.ds(pl.multiple_of(start + b * share, 8), share), :] for b in range(blocks)]
    for i in range(parts):

        @pl.when(g == i)
        def _(i=i):
            for b in range(blocks):
                cols = slice(b * LANE, (b + 1) * LANE)
                outs[i][0:rows, cols] = pieces[b]
                outs[i][rows : rows + share, cols] = shares[b]


def gram_parts(dosage, left, right, mean, scale, k, column_place, rot, inv):
    samples, cols = dosage.shape
    parts = cols // QW
    blocks = QW // LANE
    total = cols // LANE
    height = (BMAX + 1) * TILE + LANE // parts // blocks
    meta = jnp.stack([k, column_place * total]).astype(jnp.int32)

    def quarter(g, m):
        return lax.rem(g + m[0], parts) if rot else g

    fixed = lambda g, m: (0, 0)
    grid_spec = pltpu.PrefetchScalarGridSpec(
        num_scalar_prefetch=1,
        grid=(parts,),
        in_specs=[
            pl.BlockSpec((samples, QW), lambda g, m: (0, quarter(g, m))),
            pl.BlockSpec(
                (samples, LANE),
                lambda g, m: (0, jnp.minimum((quarter(g, m) + 1) * blocks, total - 1)),
            ),
            pl.BlockSpec((samples, LANE), fixed),
            pl.BlockSpec((samples, LANE), fixed),
            pl.BlockSpec((samples, LANE), fixed),
            pl.BlockSpec((mean.shape[0] // LANE, LANE), fixed),
            pl.BlockSpec((mean.shape[0] // LANE, LANE), fixed),
        ],
        out_specs=[pl.BlockSpec((height, QW), fixed) for _ in range(parts)],
        scratch_shapes=[
            pltpu.VMEM((samples, QW + LANE), jnp.bfloat16),
            pltpu.VMEM((LANE, LANE), jnp.float32),
        ],
    )
    return pl.pallas_call(
        functools.partial(gram_kernel, parts, rot, inv),
        grid_spec=grid_spec,
        out_shape=[jax.ShapeDtypeStruct((height, QW), jnp.float32) for _ in range(parts)],
        compiler_params=params(dimension_semantics=("arbitrary",)),
        cost_estimate=pl.CostEstimate(
            flops=2 * samples * cols * (QW + LANE), bytes_accessed=dosage.size * 4, transcendentals=0
        ),
        name="gram",
    )(
        meta,
        dosage,
        dosage,
        right,
        left,
        dosage,
        mean.reshape(-1, LANE),
        scale.reshape(-1, LANE),
    )


def assemble_kernel(parts, rot, tile_total, meta, band, *rest):
    ins = rest[:parts]
    out = rest[parts]
    blocks = QW // LANE
    rows = (BMAX + 1) * TILE
    low = low_lanes((TILE, LANE))
    share = LANE // parts // blocks
    for quarter in range(parts):

        def fetch(row, count, b, quarter=quarter):
            cols = slice(b * LANE, (b + 1) * LANE)
            return ins[quarter][row : row + count, cols]

        for b in range(blocks):
            a = quarter * blocks + b
            cols = slice(a * LANE, (a + 1) * LANE)
            masks = mask_rows(band, meta[1] + 2 * a, tile_total)
            for q in range(BMAX + 1):
                out[(BMAX + q) * TILE : (BMAX + q + 1) * TILE, cols] = (
                    fetch(q * TILE, TILE, b) * masks[BMAX + q]
                )
            turned = fetch(TILE, 2 * TILE, b).T
            rolled = pltpu.roll(turned, TILE, axis=1)
            if a == 0:
                count = LANE // share
                cross = [
                    ins[j // blocks][
                        rows : rows + share, (j % blocks) * LANE : (j % blocks + 1) * LANE
                    ]
                    for j in range(count)
                ]
                cross = jnp.concatenate(cross, axis=0)
                one_low, two_low, two_high = cross[TILE:], cross[:TILE], cross[TILE:]
            else:
                one_low, two_low, two_high = last_turned[TILE:], last_rolled[:TILE], last_turned[TILE:]
            out[TILE : 2 * TILE, cols] = jnp.where(low, one_low, rolled[:TILE]) * masks[1]
            out[0:TILE, cols] = jnp.where(low, two_low, two_high) * masks[0]
            last_turned, last_rolled = turned, rolled


def assemble(pieces, band_next, first_tile, cols):
    parts = len(pieces)
    meta = jnp.stack([first_tile * 0, first_tile]).astype(jnp.int32)
    return pl.pallas_call(
        functools.partial(assemble_kernel, parts, False, band_next.shape[0]),
        in_specs=[SMEM, SMEM] + [VMEM] * parts,
        out_specs=VMEM,
        out_shape=jax.ShapeDtypeStruct((SPAN * TILE, cols), jnp.float32),
        compiler_params=params(),
        name="assemble",
    )(meta, band_next, *pieces)


def krylov_kernel(
    tile_total, sb, meta, band, ldt, z, obs, halo_l, halo_r, w_out, mom_out,
    dh, dl, ucat, seen, u_prev, y
):
    rows = ldt.shape[1]
    traits = z.shape[1]
    own_blocks = rows // LANE
    zb = HZ // LANE
    bb = HB // LANE
    first_tile = meta[0]
    nb = obs.shape[0]
    ld_rows = SPAN * TILE
    total_blocks = own_blocks + 2 * zb

    for c in range(total_blocks):
        if c < zb:
            vec = halo_l[c * LANE : (c + 1) * LANE, :traits]
            flags = [
                halo_l[HZ + bb * ld_rows + c * nb + i : HZ + bb * ld_rows + c * nb + i + 1, :]
                for i in range(nb)
            ]
        elif c < zb + own_blocks:
            o = c - zb
            vec = z[o * LANE : (o + 1) * LANE, :]
            flags = [
                obs[i : i + 1, o * LANE : (o + 1) * LANE].astype(jnp.float32) for i in range(nb)
            ]
        else:
            o = c - zb - own_blocks
            vec = halo_r[o * LANE : (o + 1) * LANE, :traits]
            flags = [
                halo_r[HZ + bb * ld_rows + o * nb + i : HZ + bb * ld_rows + o * nb + i + 1, :]
                for i in range(nb)
            ]
        wide = jnp.concatenate(
            [jnp.broadcast_to(f, (TBLK, LANE)) for f in flags], axis=0
        )
        mask = wide.T
        here = slice(c * LANE, (c + 1) * LANE)
        seen[here, :] = mask
        start = mask * vec
        high = start.astype(jnp.bfloat16)
        u_prev[here, :] = start
        ucat[here, :traits] = high
        ucat[here, traits:] = (start - high.astype(jnp.float32)).astype(jnp.bfloat16)

    per = sb // LANE
    low = low_lanes((TILE, LANE))
    sub = lax.broadcasted_iota(jnp.int32, (TILE, LANE), 0)
    lane = lax.broadcasted_iota(jnp.int32, (TILE, LANE), 1)
    chunks = SPAN + 1
    for c in range(own_blocks + 2 * bb):
        if c < bb:
            get = lambda q, c=c: halo_l[HZ + c * ld_rows + q * TILE : HZ + c * ld_rows + (q + 1) * TILE, :]
        elif c < bb + own_blocks:
            get = lambda q, c=c: ldt[q * TILE : (q + 1) * TILE, (c - bb) * LANE : (c - bb + 1) * LANE]
        else:
            o = c - bb - own_blocks
            get = lambda q, o=o: halo_r[HZ + o * ld_rows + q * TILE : HZ + o * ld_rows + (q + 1) * TILE, :]
        masks = mask_rows(band, first_tile + 2 * (c - bb), tile_total)
        s, h = c // per, c % per
        cols = slice(h * LANE, (h + 1) * LANE)
        parts = [get(q) * masks[q] for q in range(SPAN)]
        zero = jnp.zeros((TILE, LANE), jnp.float32)
        for j in range(chunks):
            left = parts[j] if j < SPAN else zero
            right = parts[j - 1] if j >= 1 else zero
            value = jnp.where(low, left, right)
            if BMAX <= j < BMAX + 2:
                value = value - (sub + TILE * (j - BMAX) == lane).astype(jnp.float32)
            high = value.astype(jnp.bfloat16)
            at = slice(h * LANE + j * TILE, h * LANE + (j + 1) * TILE)
            dh[s, at, cols] = high
            dl[s, at, cols] = (value - high.astype(jnp.float32)).astype(jnp.bfloat16)
        for x in range(per):
            if x < h:
                at = slice(x * LANE, (x + 1) * LANE)
            elif x > h:
                at = slice((x + 2) * LANE, (x + 3) * LANE)
            else:
                continue
            blank = jnp.zeros((LANE, LANE), jnp.bfloat16)
            dh[s, at, cols] = blank
            dl[s, at, cols] = blank

    supers = (rows + 2 * HB) // sb
    window = sb + 2 * REACH

    def product(both, rest):
        return both[:, :traits] + both[:, traits:] + rest

    def apply():
        for s in range(supers):
            vec = ucat[REACH + s * sb : REACH + (s + 1) * sb, :]
            part = product(dot(dh[s], vec), dot(dl[s], vec[:, :traits]))
            at = s * sb
            if s == 0:
                y[at : at + window, :] = part
            else:
                y[at : at + 2 * REACH, :] += part[: 2 * REACH]
                y[at + 2 * REACH : at + window, :] = part[2 * REACH :]

    own = slice(HZ, HZ + rows)
    sums = []
    for step in range(ITERS):
        apply()
        if step == 0:
            for edge_rows, edge_cols, s, target, source in (
                (slice(0, LANE), slice(0, LANE), 0, 1, 0),
                (
                    slice(window - LANE, window),
                    slice(sb - LANE, sb),
                    supers - 1,
                    total_blocks - 2,
                    total_blocks - 1,
                ),
            ):
                vec = ucat[source * LANE : (source + 1) * LANE, :]
                part = product(
                    tdot(dh[s, edge_rows, edge_cols], vec),
                    tdot(dl[s, edge_rows, edge_cols], vec[:, :traits]),
                )
                y[target * LANE : (target + 1) * LANE, :] += part
        u_own = u_prev[own, :]
        y_own = y[own, :]
        w_out[step] = u_own + y_own
        sums.append(jnp.sum(u_own * u_own, axis=0, keepdims=True))
        sums.append(jnp.sum(u_own * y_own, axis=0, keepdims=True))
        if step < ITERS - 1:
            edge = (step + 1) * REACH
            here = slice(edge, total_blocks * LANE - edge)
            nxt = seen[here, :] * y[here, :]
            high = nxt.astype(jnp.bfloat16)
            u_prev[here, :] = nxt
            ucat[here, :traits] = high
            ucat[here, traits:] = (nxt - high.astype(jnp.float32)).astype(jnp.bfloat16)
    mom_out[...] = jnp.concatenate(
        sums + [jnp.zeros((8 - len(sums), traits), jnp.float32)], axis=0
    )


def krylov(ldt, z, obs, halo_l, halo_r, band_prev, first_tile):
    rows, traits = z.shape
    wide = rows + 2 * HB
    sb = 2 * LANE if wide % (2 * LANE) == 0 else LANE
    ext = rows + 2 * HZ
    supers = wide // sb
    meta = first_tile.reshape(1).astype(jnp.int32)
    return pl.pallas_call(
        functools.partial(krylov_kernel, band_prev.shape[0], sb),
        in_specs=[SMEM, SMEM] + [VMEM] * 5,
        out_specs=[VMEM, VMEM],
        out_shape=[
            jax.ShapeDtypeStruct((ITERS, rows, traits), jnp.float32),
            jax.ShapeDtypeStruct((8, traits), jnp.float32),
        ],
        scratch_shapes=[
            pltpu.VMEM((supers, sb + 2 * REACH, sb), jnp.bfloat16),
            pltpu.VMEM((supers, sb + 2 * REACH, sb), jnp.bfloat16),
            pltpu.VMEM((ext, 2 * traits), jnp.bfloat16),
            pltpu.VMEM((ext, traits), jnp.float32),
            pltpu.VMEM((ext, traits), jnp.float32),
            pltpu.VMEM((ext, traits), jnp.float32),
        ],
        compiler_params=params(),
        cost_estimate=pl.CostEstimate(
            flops=ITERS * 6 * ext * SPAN * TILE * traits, bytes_accessed=ldt.size * 4, transcendentals=0
        ),
        name="krylov",
    )(meta, band_prev, ldt, z, obs, halo_l, halo_r)


def combine_kernel(w, *rest):
    out = rest[-1]
    mom = rest[0][...]
    for other in rest[1:-1]:
        mom = mom + other[...]
    m = [mom[i : i + 1, :] for i in range(2 * ITERS)]
    shift = 1.0 + RIDGE
    h = [shift * m[i] + m[i + 1] for i in range(2 * ITERS - 1)]
    d0 = h[0]
    l10 = h[1] / d0
    l20 = h[2] / d0
    d1 = h[2] - l10 * h[1]
    t12 = h[3] - l20 * h[1]
    ok1 = d1 > TINY * h[2]
    r1 = jnp.where(ok1, 1.0 / jnp.where(ok1, d1, 1.0), 0.0)
    l21 = t12 * r1
    d2 = h[4] - l20 * h[2] - l21 * t12
    ok2 = ok1 & (d2 > TINY * h[4])
    r2 = jnp.where(ok2, 1.0 / jnp.where(ok2, d2, 1.0), 0.0)
    z0 = m[0]
    z1 = m[1] - l10 * z0
    z2 = m[2] - l20 * z0 - l21 * z1
    c2 = z2 * r2
    c1 = z1 * r1 - l21 * c2
    c0 = z0 / d0 - l10 * c1 - l20 * c2
    out[...] = c0 * w[0] + c1 * w[1] + c2 * w[2]


def combine(w, moments):
    return pl.pallas_call(
        combine_kernel,
        in_specs=[VMEM] * (1 + len(moments)),
        out_specs=VMEM,
        out_shape=jax.ShapeDtypeStruct(w.shape[1:], jnp.float32),
        compiler_params=params(),
        name="combine",
    )(w, *moments)


def packed(z, ldt, obs):
    z = jnp.pad(z, ((0, 0), (0, LANE - z.shape[1])))
    obs = obs.astype(jnp.float32)
    parts = [z]
    parts += [ldt[:, i : i + LANE] for i in range(0, ldt.shape[1], LANE)]
    parts += [obs[:, i : i + LANE] for i in range(0, obs.shape[1], LANE)]
    height = sum(p.shape[0] for p in parts)
    parts.append(jnp.zeros((-height % 8, LANE), jnp.float32))
    return jnp.concatenate(parts, axis=0)


def halos(z, ldt, obs, axis):
    count = lax.axis_size(axis)
    rows = z.shape[0]

    def shifted(value, by):
        pairs = [(i, i + by) for i in range(count) if 0 <= i + by < count]
        return lax.ppermute(value, axis, pairs)

    if rows >= HZ:
        last = packed(z[rows - HZ :], ldt[:, rows - HB :], obs[:, rows - HZ :])
        head = packed(z[:HZ], ldt[:, :HB], obs[:, :HZ])
        return shifted(last, 1), shifted(head, -1)

    def gather(value, width, dim):
        lefts, rights = [], []
        hop, have = 1, 0
        while have < width:
            take = min(rows, width - have)
            lefts.insert(0, shifted(lax.slice_in_dim(value, rows - take, rows, axis=dim), hop))
            rights.append(shifted(lax.slice_in_dim(value, 0, take, axis=dim), -hop))
            have += take
            hop += 1
        return jnp.concatenate(lefts, dim), jnp.concatenate(rights, dim)

    zs = gather(z, HZ, 0)
    lds = gather(ldt, HB, 1)
    seens = gather(obs, HZ, 1)
    return packed(zs[0], lds[0], seens[0]), packed(zs[1], lds[1], seens[1])


def local(dosage, allele_mean, snp_scale, band_next, ld_prev, band_prev, zscores, observed):
    samples, cols = dosage.shape
    rows = ld_prev.shape[0]
    n_smp = lax.axis_size("smp")
    k = lax.axis_index("smp")
    snp, pair = lax.axis_index("snp"), lax.axis_index("pair")
    n_snp, n_pair = lax.axis_size("snp"), lax.axis_size("pair")
    place = snp * n_pair + pair
    count = n_snp * n_pair

    ldt = ld_prev.T
    obs = observed.T
    halo_l, halo_r = halos(zscores, ldt, obs, "smp")

    line = ("snp", "pair")
    right = lax.ppermute(dosage[:, :LANE], line, [(i + 1, i) for i in range(count - 1)])
    left = lax.ppermute(dosage[:, cols - LANE :], line, [(i, i + 1) for i in range(count - 1)])

    w, mom = krylov(ldt, zscores, obs, halo_l, halo_r, band_prev, k * (rows // TILE))

    parts = cols // QW
    rot = parts == n_smp
    inv = 1.0 / (samples * n_smp)
    blocks = gram_parts(dosage, left, right, allele_mean, snp_scale, k, place, rot, inv)
    if rot:
        cycle = lambda value, by: lax.ppermute(
            value, "smp", [(i, (i + by) % n_smp) for i in range(n_smp)]
        )
        moments = [mom] + [cycle(mom, by) for by in range(1, n_smp)]
        got = [cycle(blocks[by].astype(jnp.float16), by) for by in range(1, n_smp)]
        got, moments = lax.optimization_barrier((got, moments))
        total = blocks[0]
        for g in got:
            total = total + g.astype(jnp.float32)
        total = total.astype(jnp.float16)
        ring = [total] + [cycle(total, by) for by in range(1, n_smp)]
        stacked = jnp.stack(ring)
        pieces = [
            lax.dynamic_index_in_dim(stacked, lax.rem(k + n_smp - q, n_smp), 0, keepdims=False).astype(
                jnp.float32
            )
            for q in range(parts)
        ]
    else:
        pieces = lax.psum(tuple(blocks), "smp")
        moments = [lax.psum(mom, "smp")]
    imputed = combine(w, moments)
    ldn = assemble(pieces, band_next, place * (cols // TILE), cols)
    return ldn.T, imputed


def solution(mesh):
    return jax.shard_map(
        local,
        mesh=mesh,
        in_specs=(
            P(("grp", "smp"), ("snp", "pair")),
            P("grp"),
            P("grp"),
            P("grp"),
            P(("grp", "smp"), None),
            P("grp"),
            P(("grp", "smp"), ("snp", "pair")),
            P(("grp", "smp"), ("snp", "pair")),
        ),
        out_specs=(P(("grp", "snp", "pair"), None), P(("grp", "smp"), ("snp", "pair"))),
        check_vma=False,
    )
```

```python
import functools
import jax
import jax.numpy as jnp
from jax import lax
from jax.experimental import pallas as pl
from jax.experimental.pallas import tpu as pltpu
from jax.sharding import PartitionSpec as P

TILE = 64
BMAX = 2
TBLK = 64
ITERS = 3
RIDGE = 1.0
SPAN = 2 * BMAX + 1
REACH = TILE * BMAX
LANE = 128
QW = 256
HZ = ITERS * REACH
HB = (ITERS - 1) * REACH
TINY = 1e-6
VMEM = pl.BlockSpec(memory_space=pltpu.VMEM)
SMEM = pl.BlockSpec(memory_space=pltpu.SMEM)


def params(mib):
    return pltpu.CompilerParams(vmem_limit_bytes=mib * 1024 * 1024)


def mask_rows(band_ref, first_tile, total):
    def width(t):
        inside = (t >= 0) & (t < total)
        return jnp.where(inside, band_ref[jnp.clip(t, 0, total - 1)], 0)

    widths = [width(first_tile + d) for d in range(-BMAX, BMAX + 2)]
    low = lax.broadcasted_iota(jnp.int32, (1, LANE), 1) < TILE
    rows = []
    for q in range(-BMAX, BMAX + 1):
        flags = [
            (abs(q) <= jnp.minimum(widths[BMAX + t], widths[BMAX + t + q])).astype(jnp.float32)
            for t in range(2)
        ]
        rows.append(jnp.where(low, flags[0], flags[1]))
    return rows


def low_lanes(shape):
    return lax.broadcasted_iota(jnp.int32, shape, 1) < TILE


def tdot(left, right):
    return lax.dot_general(
        left, right, (((0,), (0,)), ((), ())), preferred_element_type=jnp.float32
    )


def dot(left, right):
    return lax.dot_general(
        left, right, (((1,), (0,)), ((), ())), preferred_element_type=jnp.float32
    )


LEVELS = 32000.0
LARGEST = 36.0


def encode(value):
    size = jnp.minimum(jnp.abs(value) * (1.0 / LARGEST), 1.0) + 1e-30
    for _ in range(3):
        size = size * lax.rsqrt(size)
    code = size * LEVELS + 0.5
    return jnp.where(value < 0, -code, code).astype(jnp.int32).astype(jnp.int16)


def decode(code):
    value = code.astype(jnp.int32).astype(jnp.float32)
    power = value * (1.0 / LEVELS)
    square = power * power
    fourth = square * square
    eighth = fourth * fourth * LARGEST
    return jnp.where(value < 0, -eighth, eighth)


def encode_exact(value):
    size = jnp.maximum(jnp.abs(value), 1e-30)
    power = jnp.clip(jnp.floor(jnp.log2(size)), -100.0, 120.0)
    scaled = value * jnp.exp2(-power) * 2.0**13
    high = jnp.round(scaled)
    low = jnp.round((scaled - high) * 2.0**14)
    return power, high, low


def decode_exact(power, high, low):
    return (high * 2.0**-13 + low * 2.0**-27) * jnp.exp2(power)


def to_code(value):
    return value.astype(jnp.int32).astype(jnp.int16)


def from_code(code):
    return code.astype(jnp.int32).astype(jnp.float32)


def line_index(axes):
    place = lax.axis_index(axes[0])
    for axis in axes[1:]:
        place = place * lax.axis_size(axis) + lax.axis_index(axis)
    return place


def pack_kernel(dos, z, ldt, obs, dos_e, dos_o, *rest):
    halo, sem = rest[:-1], rest[-1]
    cols = dos.shape[1]
    rows = z.shape[0]
    copies = []

    def start(source, target):
        copy = pltpu.make_async_copy(source, target, sem.at[len(copies)])
        copy.start()
        copies.append(copy)

    even = lax.rem(line_index(("snp", "pair")), 2) == 0
    to_e = pl.multiple_of(jnp.where(even, cols - LANE, 0), LANE)
    to_o = pl.multiple_of(jnp.where(even, 0, cols - LANE), LANE)
    start(dos.at[:, pl.ds(to_e, LANE)], dos_e)
    start(dos.at[:, pl.ds(to_o, LANE)], dos_o)
    if halo:
        even = lax.rem(lax.axis_index("smp"), 2) == 0
        spots = []
        for out, last in ((halo[0], even), (halo[1], jnp.logical_not(even))):
            row = pl.multiple_of(jnp.where(last, rows - HZ, 0), LANE)
            col = pl.multiple_of(jnp.where(last, rows - HB, 0), LANE)
            spots.append(row)
            start(z.at[pl.ds(row, HZ), :], out.at[0:HZ, :])
            for i in range(HB // LANE):
                start(
                    ldt.at[:, pl.ds(pl.multiple_of(col + i * LANE, LANE), LANE)],
                    out.at[HZ + i * SPAN * TILE : HZ + (i + 1) * SPAN * TILE, :],
                )
        nb = obs.shape[0]
        base = HZ + HB // LANE * SPAN * TILE
        for out, row in zip(halo, spots):
            for i in range(HZ // LANE):
                flags = obs[:, pl.ds(pl.multiple_of(row + i * LANE, LANE), LANE)]
                out[base + i * nb : base + (i + 1) * nb, :] = flags.astype(jnp.float32)
            used = base + HZ // LANE * nb
            if used < out.shape[0]:
                out[used:, :] = jnp.zeros((out.shape[0] - used, LANE), jnp.float32)
    for copy in copies:
        copy.wait()


def pack(dosage, z, ldt, obs, with_halo):
    samples = dosage.shape[0]
    shapes = [jax.ShapeDtypeStruct((samples, LANE), dosage.dtype)] * 2
    copies = 2
    if with_halo:
        height = HZ + HB // LANE * SPAN * TILE + HZ // LANE * obs.shape[0]
        shapes += [jax.ShapeDtypeStruct((height + -height % 8, LANE), jnp.float32)] * 2
        copies += 2 * (1 + HB // LANE)
    far = pl.BlockSpec(memory_space=pltpu.HBM)
    return pl.pallas_call(
        pack_kernel,
        in_specs=[far, far, far, VMEM],
        out_specs=[VMEM] * len(shapes),
        out_shape=shapes,
        scratch_shapes=[pltpu.SemaphoreType.DMA((copies,))],
        compiler_params=params(8),
        name="pack",
    )(dosage, z, ldt, obs)


def exchange(value, axes, phase):
    count = 1
    for axis in axes:
        count *= lax.axis_size(axis)
    if phase == 0 and lax.axis_size(axes[-1]) == 2 and len(axes) > 1:
        return lax.ppermute(value, axes[-1], [(0, 1), (1, 0)])
    pairs = []
    for i in range(phase, count - 1, 2):
        pairs += [(i, i + 1), (i + 1, i)]
    return lax.ppermute(value, axes, pairs)


def gram_kernel(parts, rot, samples_total, dos, got_e, got_o, mean, scale, *rest):
    outs = rest[:parts]
    raw, normed, cross, sem = rest[parts:]
    blocks = QW // LANE
    samples, cols = dos.shape
    place = line_index(("snp", "pair"))
    base = place * (cols // LANE)
    lanes_total = mean.shape[0]
    first = lax.axis_index("smp") if rot else 0
    inv = 1.0 / (samples if rot else samples_total)

    def quarter_of(g):
        return lax.rem(g + first, parts)

    def fetch(g):
        at = pl.multiple_of(quarter_of(g) * QW, QW)
        return pltpu.make_async_copy(dos.at[:, pl.ds(at, QW)], raw.at[g], sem.at[g])

    for g in range(parts):
        fetch(g).start()

    def standard(values, block):
        row = jnp.clip(block, 0, lanes_total - 1)
        m = mean[pl.ds(row, 1), :]
        s = scale[pl.ds(row, 1), :]
        return ((values.astype(jnp.float32) - m) * s).astype(jnp.bfloat16)

    def settle(g):
        fetch(g).wait()
        block = quarter_of(g) * blocks
        for b in range(blocks):
            at = pl.multiple_of((block + b) * LANE, LANE)
            normed[:, pl.ds(at, LANE)] = standard(
                raw[g, :, b * LANE : (b + 1) * LANE], base + block + b
            )

    even = lax.rem(place, 2) == 0
    got = [got_e[...], got_o[...]]
    right = jnp.where(even, got[0], got[1])
    left = jnp.where(even, got[1], got[0])
    normed[:, cols:] = standard(right, base + cols // LANE)
    raw_left = standard(left, base - 1)
    settle(0)
    rows = (BMAX + 1) * TILE
    low = low_lanes((rows, LANE))
    share = LANE // parts // blocks

    fetch0 = pltpu.make_async_copy(dos.at[:, 0:LANE], raw.at[parts, :, 0:LANE], sem.at[parts])
    fetch0.start()
    fetch0.wait()
    cross[...] = inv * tdot(raw_left, standard(raw[parts, :, 0:LANE], base))

    def step(g, _):
        @pl.when(g < parts - 1)
        def _():
            settle(jnp.minimum(g + 1, parts - 1))

        quarter = quarter_of(g)
        at = pl.multiple_of(quarter * QW, QW)
        full = tdot(normed[:, pl.ds(at, QW + LANE)], normed[:, pl.ds(at, QW)])
        pieces = []
        for b in range(blocks):
            cut = slice(b * LANE, (b + 1) * LANE)
            pieces.append(
                inv
                * jnp.where(
                    low,
                    full[b * LANE : b * LANE + rows, cut],
                    full[b * LANE + TILE : b * LANE + TILE + rows, cut],
                )
            )
        start = quarter * (share * blocks)
        shares = [
            cross[pl.ds(pl.multiple_of(start + b * share, 8), share), :] for b in range(blocks)
        ]
        for i in range(parts):

            @pl.when(g == i)
            def _(i=i):
                for b in range(blocks):
                    cut = slice(b * LANE, (b + 1) * LANE)
                    send = encode if rot and i > 0 else (lambda v: v)
                    outs[i][0:rows, cut] = send(pieces[b])
                    outs[i][rows : rows + share, cut] = send(shares[b])

        return 0

    lax.fori_loop(0, parts, step, 0)


def gram_parts(dosage, got_e, got_o, mean, scale, rot, samples_total):
    samples, cols = dosage.shape
    parts = cols // QW
    height = (BMAX + 1) * TILE + LANE // parts // (QW // LANE)
    kinds = [jnp.float32] + [jnp.int16 if rot else jnp.float32] * (parts - 1)
    return pl.pallas_call(
        functools.partial(gram_kernel, parts, rot, samples_total),
        in_specs=[pl.BlockSpec(memory_space=pltpu.HBM)] + [VMEM] * 4,
        out_specs=[VMEM] * parts,
        out_shape=[jax.ShapeDtypeStruct((height, QW), kind) for kind in kinds],
        scratch_shapes=[
            pltpu.VMEM((parts + 1, samples, QW), jnp.bfloat16),
            pltpu.VMEM((samples, cols + LANE), jnp.bfloat16),
            pltpu.VMEM((LANE, LANE), jnp.float32),
            pltpu.SemaphoreType.DMA((parts + 1,)),
        ],
        compiler_params=params(24),
        cost_estimate=pl.CostEstimate(
            flops=2 * samples * cols * (QW + LANE), bytes_accessed=dosage.size * 4, transcendentals=0
        ),
        name="gram",
    )(dosage, got_e, got_o, mean.reshape(-1, LANE), scale.reshape(-1, LANE))


def total_kernel(count, own, *rest):
    others, mom, out = rest[:-2], rest[-2], rest[-1]
    height = own.shape[0]
    total = own[...]
    for other in others:
        total = total + decode(other[...])
    out[0:height, :] = encode(total * (1.0 / count))
    power, high, low = encode_exact(mom[...])
    lanes = mom.shape[1]
    top = jnp.concatenate([power, low], axis=1)
    bottom = jnp.concatenate([high, jnp.zeros_like(low)], axis=1)
    out[height : height + 16, :] = to_code(jnp.concatenate([top, bottom], axis=0))


def total_of(own, others, mom):
    count = 1 + len(others)
    return pl.pallas_call(
        functools.partial(total_kernel, count),
        in_specs=[VMEM] * (count + 1),
        out_specs=VMEM,
        out_shape=jax.ShapeDtypeStruct((own.shape[0] + 16, own.shape[1]), jnp.int16),
        compiler_params=params(8),
        name="total",
    )(own, *others, mom)


def final_kernel(parts, rot, moments, tile_total, band, w, *rest):
    ring = rest[:parts]
    moms = rest[parts : parts + moments]
    out, imputed, held = rest[parts + moments :]
    blocks = QW // LANE
    rows = (BMAX + 1) * TILE
    low = low_lanes((TILE, LANE))
    share = LANE // parts // blocks
    height = rows + share
    cols = out.shape[1]
    first_tile = line_index(("snp", "pair")) * (cols // TILE)
    if rot:
        k = lax.axis_index("smp")
        total = None
        for by in range(parts):
            held[lax.rem(k - by + parts, parts)] = decode(ring[by][0:height, :])
            code = from_code(ring[by][height : height + 16, :])
            lanes = code.shape[1] // 2
            mom = decode_exact(code[:8, :lanes], code[8:, :lanes], code[:8, lanes:])
            total = mom if total is None else total + mom
    else:
        for by in range(parts):
            held[by] = ring[by][...]
        total = moms[0][...]
    solve(w, total, imputed)
    for a in range(parts * blocks):
        quarter, b = a // blocks, a % blocks
        cut = slice(b * LANE, (b + 1) * LANE)
        cols_here = slice(a * LANE, (a + 1) * LANE)
        masks = mask_rows(band, first_tile + 2 * a, tile_total)
        for q in range(BMAX + 1):
            out[(BMAX + q) * TILE : (BMAX + q + 1) * TILE, cols_here] = (
                held[quarter, q * TILE : (q + 1) * TILE, cut] * masks[BMAX + q]
            )
        turned = held[quarter, TILE : 3 * TILE, cut].T
        rolled = pltpu.roll(turned, TILE, axis=1)
        if a == 0:
            cross = jnp.concatenate(
                [
                    held[j // blocks, rows:height, (j % blocks) * LANE : (j % blocks + 1) * LANE]
                    for j in range(LANE // share)
                ],
                axis=0,
            )
            one_low, two_low, two_high = cross[TILE:], cross[:TILE], cross[TILE:]
        else:
            one_low, two_low, two_high = last_turned[TILE:], last_rolled[:TILE], last_turned[TILE:]
        out[TILE : 2 * TILE, cols_here] = jnp.where(low, one_low, rolled[:TILE]) * masks[1]
        out[0:TILE, cols_here] = jnp.where(low, two_low, two_high) * masks[0]
        last_turned, last_rolled = turned, rolled


def final(ring, moms, w, band_next, cols, rot):
    parts = len(ring)
    height = (BMAX + 1) * TILE + LANE // parts // (QW // LANE)
    return pl.pallas_call(
        functools.partial(final_kernel, parts, rot, len(moms), band_next.shape[0]),
        in_specs=[SMEM] + [VMEM] * (1 + parts + len(moms)),
        out_specs=[VMEM, VMEM],
        out_shape=[
            jax.ShapeDtypeStruct((SPAN * TILE, cols), jnp.float32),
            jax.ShapeDtypeStruct(w.shape[1:], jnp.float32),
        ],
        scratch_shapes=[pltpu.VMEM((parts, height, QW), jnp.float32)],
        compiler_params=params(16),
        name="final",
    )(band_next, w, *ring, *moms)


class Side:
    def __init__(self, flag, one, two):
        self.flag, self.one, self.two = flag, one, two

    def __getitem__(self, at):
        if self.flag is None:
            return self.one[at]
        return jnp.where(self.flag, self.one[at], self.two[at])


def krylov_kernel(
    tile_total, sb, paired, band, ldt, z, obs, got_e, got_o, w_out, mom_out,
    dh, dl, ucat, seen, u_prev, y
):
    rows = ldt.shape[1]
    traits = z.shape[1]
    own_blocks = rows // LANE
    zb = HZ // LANE
    bb = HB // LANE
    first_tile = lax.axis_index("smp") * (rows // TILE)
    even = lax.rem(lax.axis_index("smp"), 2) == 0 if paired else None
    halo_r = Side(even, got_e, got_o)
    halo_l = Side(even, got_o, got_e)
    nb = obs.shape[0]
    ld_rows = SPAN * TILE
    total_blocks = own_blocks + 2 * zb

    for c in range(total_blocks):
        if c < zb:
            vec = halo_l[c * LANE : (c + 1) * LANE, :traits]
            flags = [
                halo_l[HZ + bb * ld_rows + c * nb + i : HZ + bb * ld_rows + c * nb + i + 1, :]
                for i in range(nb)
            ]
        elif c < zb + own_blocks:
            o = c - zb
            vec = z[o * LANE : (o + 1) * LANE, :]
            flags = [
                obs[i : i + 1, o * LANE : (o + 1) * LANE].astype(jnp.float32) for i in range(nb)
            ]
        else:
            o = c - zb - own_blocks
            vec = halo_r[o * LANE : (o + 1) * LANE, :traits]
            flags = [
                halo_r[HZ + bb * ld_rows + o * nb + i : HZ + bb * ld_rows + o * nb + i + 1, :]
                for i in range(nb)
            ]
        wide = jnp.concatenate(
            [jnp.broadcast_to(f, (TBLK, LANE)) for f in flags], axis=0
        )
        mask = wide.T
        here = slice(c * LANE, (c + 1) * LANE)
        seen[here, :] = mask
        start = mask * vec
        high = start.astype(jnp.bfloat16)
        u_prev[here, :] = start
        ucat[here, :traits] = high
        ucat[here, traits:] = (start - high.astype(jnp.float32)).astype(jnp.bfloat16)

    per = sb // LANE
    low = low_lanes((TILE, LANE))
    sub = lax.broadcasted_iota(jnp.int32, (TILE, LANE), 0)
    lane = lax.broadcasted_iota(jnp.int32, (TILE, LANE), 1)
    chunks = SPAN + 1
    for c in range(own_blocks + 2 * bb):
        if c < bb:
            get = lambda q, c=c: halo_l[HZ + c * ld_rows + q * TILE : HZ + c * ld_rows + (q + 1) * TILE, :]
        elif c < bb + own_blocks:
            get = lambda q, c=c: ldt[q * TILE : (q + 1) * TILE, (c - bb) * LANE : (c - bb + 1) * LANE]
        else:
            o = c - bb - own_blocks
            get = lambda q, o=o: halo_r[HZ + o * ld_rows + q * TILE : HZ + o * ld_rows + (q + 1) * TILE, :]
        masks = mask_rows(band, first_tile + 2 * (c - bb), tile_total)
        s, h = c // per, c % per
        cols = slice(h * LANE, (h + 1) * LANE)
        parts = [get(q) * masks[q] for q in range(SPAN)]
        zero = jnp.zeros((TILE, LANE), jnp.float32)
        for j in range(chunks):
            left = parts[j] if j < SPAN else zero
            right = parts[j - 1] if j >= 1 else zero
            value = jnp.where(low, left, right)
            if BMAX <= j < BMAX + 2:
                value = value - (sub + TILE * (j - BMAX) == lane).astype(jnp.float32)
            high = value.astype(jnp.bfloat16)
            at = slice(h * LANE + j * TILE, h * LANE + (j + 1) * TILE)
            dh[s, at, cols] = high
            dl[s, at, cols] = (value - high.astype(jnp.float32)).astype(jnp.bfloat16)
        for x in range(per):
            if x < h:
                at = slice(x * LANE, (x + 1) * LANE)
            elif x > h:
                at = slice((x + 2) * LANE, (x + 3) * LANE)
            else:
                continue
            blank = jnp.zeros((LANE, LANE), jnp.bfloat16)
            dh[s, at, cols] = blank
            dl[s, at, cols] = blank

    supers = (rows + 2 * HB) // sb
    window = sb + 2 * REACH

    def product(both, rest):
        return both[:, :traits] + both[:, traits:] + rest

    def apply():
        for s in range(supers):
            vec = ucat[REACH + s * sb : REACH + (s + 1) * sb, :]
            part = product(dot(dh[s], vec), dot(dl[s], vec[:, :traits]))
            at = s * sb
            if s == 0:
                y[at : at + window, :] = part
            else:
                y[at : at + 2 * REACH, :] += part[: 2 * REACH]
                y[at + 2 * REACH : at + window, :] = part[2 * REACH :]

    own = slice(HZ, HZ + rows)
    sums = []
    for step in range(ITERS):
        apply()
        if step == 0:
            for edge_rows, edge_cols, s, target, source in (
                (slice(0, LANE), slice(0, LANE), 0, 1, 0),
                (
                    slice(window - LANE, window),
                    slice(sb - LANE, sb),
                    supers - 1,
                    total_blocks - 2,
                    total_blocks - 1,
                ),
            ):
                vec = ucat[source * LANE : (source + 1) * LANE, :]
                part = product(
                    tdot(dh[s, edge_rows, edge_cols], vec),
                    tdot(dl[s, edge_rows, edge_cols], vec[:, :traits]),
                )
                y[target * LANE : (target + 1) * LANE, :] += part
        u_own = u_prev[own, :]
        y_own = y[own, :]
        w_out[step] = u_own + y_own
        sums.append(jnp.sum(u_own * u_own, axis=0, keepdims=True))
        sums.append(jnp.sum(u_own * y_own, axis=0, keepdims=True))
        if step < ITERS - 1:
            edge = (step + 1) * REACH
            here = slice(edge, total_blocks * LANE - edge)
            nxt = seen[here, :] * y[here, :]
            high = nxt.astype(jnp.bfloat16)
            u_prev[here, :] = nxt
            ucat[here, :traits] = high
            ucat[here, traits:] = (nxt - high.astype(jnp.float32)).astype(jnp.bfloat16)
    mom_out[...] = jnp.concatenate(
        sums + [jnp.zeros((8 - len(sums), traits), jnp.float32)], axis=0
    )


def krylov(ldt, z, obs, got_e, got_o, band_prev, paired):
    rows, traits = z.shape
    wide = rows + 2 * HB
    sb = 2 * LANE if wide % (2 * LANE) == 0 else LANE
    ext = rows + 2 * HZ
    supers = wide // sb
    return pl.pallas_call(
        functools.partial(krylov_kernel, band_prev.shape[0], sb, paired),
        in_specs=[SMEM] + [VMEM] * 5,
        out_specs=[VMEM, VMEM],
        out_shape=[
            jax.ShapeDtypeStruct((ITERS, rows, traits), jnp.float32),
            jax.ShapeDtypeStruct((8, traits), jnp.float32),
        ],
        scratch_shapes=[
            pltpu.VMEM((supers, sb + 2 * REACH, sb), jnp.bfloat16),
            pltpu.VMEM((supers, sb + 2 * REACH, sb), jnp.bfloat16),
            pltpu.VMEM((ext, 2 * traits), jnp.bfloat16),
            pltpu.VMEM((ext, traits), jnp.float32),
            pltpu.VMEM((ext, traits), jnp.float32),
            pltpu.VMEM((ext, traits), jnp.float32),
        ],
        compiler_params=params(28),
        cost_estimate=pl.CostEstimate(
            flops=ITERS * 6 * ext * SPAN * TILE * traits, bytes_accessed=ldt.size * 4, transcendentals=0
        ),
        name="krylov",
    )(band_prev, ldt, z, obs, got_e, got_o)


def solve(w, mom, out):
    m = [mom[i : i + 1, :] for i in range(2 * ITERS)]
    shift = 1.0 + RIDGE
    h = [shift * m[i] + m[i + 1] for i in range(2 * ITERS - 1)]
    d0 = h[0]
    l10 = h[1] / d0
    l20 = h[2] / d0
    d1 = h[2] - l10 * h[1]
    t12 = h[3] - l20 * h[1]
    ok1 = d1 > TINY * h[2]
    r1 = jnp.where(ok1, 1.0 / jnp.where(ok1, d1, 1.0), 0.0)
    l21 = t12 * r1
    d2 = h[4] - l20 * h[2] - l21 * t12
    ok2 = ok1 & (d2 > TINY * h[4])
    r2 = jnp.where(ok2, 1.0 / jnp.where(ok2, d2, 1.0), 0.0)
    z0 = m[0]
    z1 = m[1] - l10 * z0
    z2 = m[2] - l20 * z0 - l21 * z1
    c2 = z2 * r2
    c1 = z1 * r1 - l21 * c2
    c0 = z0 / d0 - l10 * c1 - l20 * c2
    out[...] = c0 * w[0] + c1 * w[1] + c2 * w[2]


def packed(z, ldt, obs):
    z = jnp.pad(z, ((0, 0), (0, LANE - z.shape[1])))
    obs = obs.astype(jnp.float32)
    parts = [z]
    parts += [ldt[:, i : i + LANE] for i in range(0, ldt.shape[1], LANE)]
    parts += [obs[:, i : i + LANE] for i in range(0, obs.shape[1], LANE)]
    height = sum(p.shape[0] for p in parts)
    parts.append(jnp.zeros((-height % 8, LANE), jnp.float32))
    return jnp.concatenate(parts, axis=0)


def halos(z, ldt, obs, axis):
    count = lax.axis_size(axis)
    rows = z.shape[0]

    def shifted(value, by):
        pairs = [(i, i + by) for i in range(count) if 0 <= i + by < count]
        return lax.ppermute(value, axis, pairs)

    def gather(value, width, dim):
        lefts, rights = [], []
        hop, have = 1, 0
        while have < width:
            take = min(rows, width - have)
            lefts.insert(0, shifted(lax.slice_in_dim(value, rows - take, rows, axis=dim), hop))
            rights.append(shifted(lax.slice_in_dim(value, 0, take, axis=dim), -hop))
            have += take
            hop += 1
        return jnp.concatenate(lefts, dim), jnp.concatenate(rights, dim)

    zs = gather(z, HZ, 0)
    lds = gather(ldt, HB, 1)
    seens = gather(obs, HZ, 1)
    return packed(zs[0], lds[0], seens[0]), packed(zs[1], lds[1], seens[1])


def local(dosage, allele_mean, snp_scale, band_next, ld_prev, band_prev, zscores, observed):
    samples, cols = dosage.shape
    rows = ld_prev.shape[0]
    n_smp = lax.axis_size("smp")
    ldt = ld_prev.T
    obs = observed.T
    line = ("snp", "pair")
    paired = rows >= HZ

    sent = pack(dosage, zscores, ldt, obs, paired)
    dos_e = exchange(sent[0], line, 0)
    dos_o = exchange(sent[1], line, 1)
    if paired:
        got_e = exchange(sent[2], ("smp",), 0)
        got_o = exchange(sent[3], ("smp",), 1)
    else:
        got_o, got_e = halos(zscores, ldt, obs, "smp")

    parts = cols // QW
    rot = parts == n_smp and zscores.shape[1] == LANE
    blocks = gram_parts(dosage, dos_e, dos_o, allele_mean, snp_scale, rot, samples * n_smp)
    if rot:

        def cycle(value, by):
            return lax.ppermute(value, "smp", [(i, (i + by) % n_smp) for i in range(n_smp)])

        got = [cycle(blocks[by], by) for by in range(1, n_smp)]
    w, mom = krylov(ldt, zscores, obs, got_e, got_o, band_prev, paired)
    if rot:
        mine = total_of(blocks[0], got, mom)
        ring = [mine] + [cycle(mine, by) for by in range(1, n_smp)]
        moms = []
    else:
        ring = list(lax.psum(tuple(blocks), "smp"))
        moms = [lax.psum(mom, "smp")]
    ldn, imputed = final(ring, moms, w, band_next, cols, rot)
    return ldn.T, imputed


def solution(mesh):
    return jax.shard_map(
        local,
        mesh=mesh,
        in_specs=(
            P(("grp", "smp"), ("snp", "pair")),
            P("grp"),
            P("grp"),
            P("grp"),
            P(("grp", "smp"), None),
            P("grp"),
            P(("grp", "smp"), ("snp", "pair")),
            P(("grp", "smp"), ("snp", "pair")),
        ),
        out_specs=(P(("grp", "snp", "pair"), None), P(("grp", "smp"), ("snp", "pair"))),
        check_vma=False,
    )
```

```python
import functools
import jax
import jax.numpy as jnp
from jax import lax
from jax.experimental import pallas as pl
from jax.experimental.pallas import tpu as pltpu
from jax.sharding import PartitionSpec as P

TILE = 64
BMAX = 2
TBLK = 64
ITERS = 3
RIDGE = 1.0
SPAN = 2 * BMAX + 1
REACH = TILE * BMAX
LANE = 128
QW = 256
HZ = ITERS * REACH
HB = (ITERS - 1) * REACH
TINY = 1e-6
VMEM = pl.BlockSpec(memory_space=pltpu.VMEM)
SMEM = pl.BlockSpec(memory_space=pltpu.SMEM)


def params(mib):
    return pltpu.CompilerParams(vmem_limit_bytes=mib * 1024 * 1024)


def mask_rows(band_ref, first_tile, total):
    def width(t):
        inside = (t >= 0) & (t < total)
        return jnp.where(inside, band_ref[jnp.clip(t, 0, total - 1)], 0)

    widths = [width(first_tile + d) for d in range(-BMAX, BMAX + 2)]
    low = lax.broadcasted_iota(jnp.int32, (1, LANE), 1) < TILE
    rows = []
    for q in range(-BMAX, BMAX + 1):
        flags = [
            (abs(q) <= jnp.minimum(widths[BMAX + t], widths[BMAX + t + q])).astype(jnp.float32)
            for t in range(2)
        ]
        rows.append(jnp.where(low, flags[0], flags[1]))
    return rows


def low_lanes(shape):
    return lax.broadcasted_iota(jnp.int32, shape, 1) < TILE


def tdot(left, right):
    return lax.dot_general(
        left, right, (((0,), (0,)), ((), ())), preferred_element_type=jnp.float32
    )


def dot(left, right):
    return lax.dot_general(
        left, right, (((1,), (0,)), ((), ())), preferred_element_type=jnp.float32
    )


LEVELS = 32000.0
Z_LARGEST = 22.0
Z_ROOTS = 2
LARGEST = 36.0


def encode(value, largest=LARGEST, roots=3):
    size = jnp.minimum(jnp.abs(value) * (1.0 / largest), 1.0) + 1e-30
    for _ in range(roots):
        size = size * lax.rsqrt(size)
    code = size * LEVELS + 0.5
    return to_code(jnp.where(value < 0, -code, code))


def decode(code, largest=LARGEST, roots=3):
    value = from_code(code)
    size = value * (1.0 / LEVELS)
    for _ in range(roots):
        size = size * size
    size = size * largest
    return jnp.where(value < 0, -size, size)


def encode_exact(value):
    size = jnp.maximum(jnp.abs(value), 1e-30)
    power = jnp.clip(jnp.floor(jnp.log2(size)), -100.0, 120.0)
    scaled = value * jnp.exp2(-power) * 2.0**13
    high = jnp.round(scaled)
    low = jnp.round((scaled - high) * 2.0**14)
    return power, high, low


def decode_exact(power, high, low):
    return (high * 2.0**-13 + low * 2.0**-27) * jnp.exp2(power)


def to_code(value):
    return value.astype(jnp.int32).astype(jnp.int16)


def from_code(code):
    return code.astype(jnp.int32).astype(jnp.float32)


def line_index(axes):
    place = lax.axis_index(axes[0])
    for axis in axes[1:]:
        place = place * lax.axis_size(axis) + lax.axis_index(axis)
    return place


def in_hbm(value):
    return pltpu.with_memory_space_constraint(value, pltpu.HBM)


def halo_height(nb):
    height = HZ + HB // LANE * SPAN * TILE + HZ // LANE * nb
    return height + -height % 16


def pack_kernel(dos, z, ldt, obs, dos_e, dos_o, *rest):
    cols = dos.shape[1]
    rows = z.shape[0]
    sem = rest[-1]
    copies = []

    def start(source, target):
        copy = pltpu.make_async_copy(source, target, sem.at[len(copies)])
        copy.start()
        copies.append(copy)

    even = lax.rem(line_index(("snp", "pair")), 2) == 0
    to_e = pl.multiple_of(jnp.where(even, cols - LANE, 0), LANE)
    to_o = pl.multiple_of(jnp.where(even, 0, cols - LANE), LANE)
    halo = ()
    if len(rest) > 1:
        halo, (zs, lds, flags) = rest[:2], rest[2:5]
        even = lax.rem(lax.axis_index("smp"), 2) == 0
        for i, last in enumerate((even, jnp.logical_not(even))):
            row = pl.multiple_of(jnp.where(last, rows - HZ, 0), LANE)
            col = pl.multiple_of(jnp.where(last, rows - HB, 0), LANE)
            start(z.at[pl.ds(row, HZ), :], zs.at[i])
            start(ldt.at[:, pl.ds(col, HB)], lds.at[i])
            start(obs.at[:, pl.ds(row, HZ)], flags.at[i])
    start(dos.at[:, pl.ds(to_e, LANE)], dos_e)
    start(dos.at[:, pl.ds(to_o, LANE)], dos_o)
    for i, out in enumerate(halo):
        nb = obs.shape[0]
        for copy in copies[3 * i : 3 * i + 3]:
            copy.wait()
        out[0:HZ, : z.shape[1]] = encode(zs[i], Z_LARGEST, Z_ROOTS)
        base = HZ
        for j in range(HB // LANE):
            out[base : base + SPAN * TILE, :] = to_code(
                jnp.round(lds[i, :, j * LANE : (j + 1) * LANE] * LEVELS)
            )
            base += SPAN * TILE
        bits = [flags[i, :, j * LANE : (j + 1) * LANE] for j in range(HZ // LANE)]
        blank = out.shape[0] - base - nb * len(bits)
        bits.append(jnp.zeros((blank, LANE), jnp.int32))
        out[base:, :] = jnp.concatenate(bits, axis=0).astype(jnp.int16)
    for copy in copies[3 * len(halo) :]:
        copy.wait()


def pack(dosage, z, ldt, obs, with_halo):
    samples = dosage.shape[0]
    shapes = [jax.ShapeDtypeStruct((samples, LANE), dosage.dtype)] * 2
    copies = 2
    scratch = []
    if with_halo:
        shapes += [jax.ShapeDtypeStruct((halo_height(obs.shape[0]), LANE), jnp.int16)] * 2
        copies += 6
        scratch = [
            pltpu.VMEM((2, HZ, z.shape[1]), z.dtype),
            pltpu.VMEM((2, SPAN * TILE, HB), ldt.dtype),
            pltpu.VMEM((2, obs.shape[0], HZ), obs.dtype),
        ]
    far = pl.BlockSpec(memory_space=pltpu.HBM)
    return pl.pallas_call(
        pack_kernel,
        in_specs=[far] * 4,
        out_specs=[VMEM] * len(shapes),
        out_shape=shapes,
        scratch_shapes=scratch + [pltpu.SemaphoreType.DMA((copies,))],
        compiler_params=params(8),
        name="pack",
    )(in_hbm(dosage), in_hbm(z), in_hbm(ldt), in_hbm(obs))


def exchange(value, axes, phase):
    count = 1
    for axis in axes:
        count *= lax.axis_size(axis)
    if phase == 0 and lax.axis_size(axes[-1]) == 2 and len(axes) > 1:
        return lax.ppermute(value, axes[-1], [(0, 1), (1, 0)])
    pairs = []
    for i in range(phase, count - 1, 2):
        pairs += [(i, i + 1), (i + 1, i)]
    return lax.ppermute(value, axes, pairs)


def standard(values, mean, scale, block):
    row = jnp.clip(block, 0, mean.shape[0] - 1)
    m = mean[pl.ds(row, 1), :]
    s = scale[pl.ds(row, 1), :]
    return ((values.astype(jnp.float32) - m) * s).astype(jnp.bfloat16)


def gram_kernel(parts, rot, inv, dos, mean, scale, *rest):
    outs = rest[:parts]
    raw, normed, sem = rest[parts:]
    blocks = QW // LANE
    samples, cols = dos.shape
    base = line_index(("snp", "pair")) * (cols // LANE)
    first = lax.axis_index("smp") if rot else 0

    def quarter_of(g):
        return lax.rem(g + first, parts)

    def fetch(g):
        at = pl.multiple_of(quarter_of(g) * QW, QW)
        return pltpu.make_async_copy(dos.at[:, pl.ds(at, QW)], raw.at[g], sem.at[g])

    for g in range(parts):
        fetch(g).start()

    def settle(g):
        fetch(g).wait()
        block = quarter_of(g) * blocks
        for b in range(blocks):
            at = pl.multiple_of((block + b) * LANE, LANE)
            normed[:, pl.ds(at, LANE)] = standard(
                raw[g, :, b * LANE : (b + 1) * LANE], mean, scale, base + block + b
            )

    normed[:, cols:] = jnp.zeros((samples, LANE), jnp.bfloat16)
    settle(0)
    rows = (BMAX + 1) * TILE
    low = low_lanes((rows, LANE))

    def step(g, _):
        @pl.when(g < parts - 1)
        def _():
            settle(jnp.minimum(g + 1, parts - 1))

        at = pl.multiple_of(quarter_of(g) * QW, QW)
        full = tdot(normed[:, pl.ds(at, QW + LANE)], normed[:, pl.ds(at, QW)])
        pieces = []
        for b in range(blocks):
            cut = slice(b * LANE, (b + 1) * LANE)
            pieces.append(
                inv
                * jnp.where(
                    low,
                    full[b * LANE : b * LANE + rows, cut],
                    full[b * LANE + TILE : b * LANE + TILE + rows, cut],
                )
            )
        for i in range(parts):

            @pl.when(g == i)
            def _(i=i):
                for b in range(blocks):
                    cut = slice(b * LANE, (b + 1) * LANE)
                    outs[i][:, cut] = encode(pieces[b]) if rot and i > 0 else pieces[b]

        return 0

    lax.fori_loop(0, parts, step, 0)


def gram_parts(dosage, mean, scale, rot, inv):
    samples, cols = dosage.shape
    parts = cols // QW
    rows = (BMAX + 1) * TILE
    kinds = [jnp.float32] + [jnp.int16 if rot else jnp.float32] * (parts - 1)
    return pl.pallas_call(
        functools.partial(gram_kernel, parts, rot, inv),
        in_specs=[pl.BlockSpec(memory_space=pltpu.HBM)] + [VMEM] * 2,
        out_specs=[VMEM] * parts,
        out_shape=[jax.ShapeDtypeStruct((rows, QW), kind) for kind in kinds],
        scratch_shapes=[
            pltpu.VMEM((parts, samples, QW), jnp.bfloat16),
            pltpu.VMEM((samples, cols + LANE), jnp.bfloat16),
            pltpu.SemaphoreType.DMA((parts,)),
        ],
        compiler_params=params(24),
        cost_estimate=pl.CostEstimate(
            flops=2 * samples * cols * (QW + LANE), bytes_accessed=dosage.size * 4, transcendentals=0
        ),
        name="gram",
    )(in_hbm(dosage), mean, scale)


def cross_kernel(parts, rot, inv, cols, sent_e, sent_o, got_e, got_o, mean, scale, *rest):
    ins, outs, cross = rest[:parts], rest[parts : 2 * parts], rest[-1]
    blocks = QW // LANE
    rows = (BMAX + 1) * TILE
    share = LANE // parts // blocks
    place = line_index(("snp", "pair"))
    base = place * (cols // LANE)
    end = base + cols // LANE
    even = lax.rem(place, 2) == 0
    pick = lambda one, two: jnp.where(even, one[...], two[...])
    right = standard(pick(got_e, got_o), mean, scale, end)
    left = standard(pick(got_o, got_e), mean, scale, base - 1)
    last = standard(pick(sent_e, sent_o), mean, scale, end - 1)
    head = standard(pick(sent_o, sent_e), mean, scale, base)
    ahead = inv * tdot(right, last)
    cross[...] = inv * tdot(left, head)
    low = low_lanes((TILE, LANE))
    far = slice((blocks - 1) * LANE, blocks * LANE)
    first = lax.axis_index("smp") if rot else 0
    for i in range(parts):
        send = encode if rot and i > 0 else (lambda v: v)
        wide = (lambda v: v.astype(jnp.int32)) if rot and i > 0 else (lambda v: v)
        outs[i][0:rows, :] = ins[i][...]
        quarter = lax.rem(i + first, parts)
        for b in range(blocks):
            at = pl.multiple_of((quarter * blocks + b) * share, 8)
            outs[i][rows : rows + share, b * LANE : (b + 1) * LANE] = send(
                cross[pl.ds(at, share), :]
            )

        @pl.when(quarter == parts - 1)
        def _(i=i, send=send, wide=wide):
            old = wide(ins[i][TILE : 2 * TILE, far])
            outs[i][TILE : 2 * TILE, far] = jnp.where(low, old, wide(send(ahead[:TILE]))).astype(
                outs[i].dtype
            )
            outs[i][2 * TILE : rows, far] = send(jnp.where(low, ahead[:TILE], ahead[TILE:]))


def cross_parts(sent_e, sent_o, got_e, got_o, mean, scale, blocks, cols, rot, inv):
    parts = len(blocks)
    height = (BMAX + 1) * TILE + LANE // parts // (QW // LANE)
    return pl.pallas_call(
        functools.partial(cross_kernel, parts, rot, inv, cols),
        in_specs=[VMEM] * (6 + parts),
        out_specs=[VMEM] * parts,
        out_shape=[jax.ShapeDtypeStruct((height, QW), b.dtype) for b in blocks],
        scratch_shapes=[pltpu.VMEM((LANE, LANE), jnp.float32)],
        compiler_params=params(12),
        name="cross",
    )(sent_e, sent_o, got_e, got_o, mean, scale, *blocks)


def total_kernel(count, own, *rest):
    others, mom, out = rest[:-2], rest[-2], rest[-1]
    height = own.shape[0]
    total = own[...]
    for other in others:
        total = total + decode(other[...])
    out[0:height, :] = encode(total * (1.0 / count))
    power, high, low = encode_exact(mom[...])
    lanes = mom.shape[1]
    top = jnp.concatenate([power, low], axis=1)
    bottom = jnp.concatenate([high, jnp.zeros_like(low)], axis=1)
    out[height : height + 16, :] = to_code(jnp.concatenate([top, bottom], axis=0))


def total_of(own, others, mom):
    count = 1 + len(others)
    return pl.pallas_call(
        functools.partial(total_kernel, count),
        in_specs=[VMEM] * (count + 1),
        out_specs=VMEM,
        out_shape=jax.ShapeDtypeStruct((own.shape[0] + 16, own.shape[1]), jnp.int16),
        compiler_params=params(8),
        name="total",
    )(own, *others, mom)


def final_kernel(parts, rot, moments, tile_total, band, w, *rest):
    ring = rest[:parts]
    moms = rest[parts : parts + moments]
    out, imputed, held = rest[parts + moments :]
    blocks = QW // LANE
    rows = (BMAX + 1) * TILE
    low = low_lanes((TILE, LANE))
    share = LANE // parts // blocks
    height = rows + share
    cols = out.shape[1]
    first_tile = line_index(("snp", "pair")) * (cols // TILE)
    if rot:
        k = lax.axis_index("smp")
        total = None
        for by in range(parts):
            held[lax.rem(k - by + parts, parts)] = decode(ring[by][0:height, :])
            code = from_code(ring[by][height : height + 16, :])
            lanes = code.shape[1] // 2
            mom = decode_exact(code[:8, :lanes], code[8:, :lanes], code[:8, lanes:])
            total = mom if total is None else total + mom
    else:
        for by in range(parts):
            held[by] = ring[by][...]
        total = moms[0][...]
    solve(w, total, imputed)
    for a in range(parts * blocks):
        quarter, b = a // blocks, a % blocks
        cut = slice(b * LANE, (b + 1) * LANE)
        cols_here = slice(a * LANE, (a + 1) * LANE)
        masks = mask_rows(band, first_tile + 2 * a, tile_total)
        for q in range(BMAX + 1):
            out[(BMAX + q) * TILE : (BMAX + q + 1) * TILE, cols_here] = (
                held[quarter, q * TILE : (q + 1) * TILE, cut] * masks[BMAX + q]
            )
        turned = held[quarter, TILE : 3 * TILE, cut].T
        rolled = pltpu.roll(turned, TILE, axis=1)
        if a == 0:
            cross = jnp.concatenate(
                [
                    held[j // blocks, rows:height, (j % blocks) * LANE : (j % blocks + 1) * LANE]
                    for j in range(LANE // share)
                ],
                axis=0,
            )
            one_low, two_low, two_high = cross[TILE:], cross[:TILE], cross[TILE:]
        else:
            one_low, two_low, two_high = last_turned[TILE:], last_rolled[:TILE], last_turned[TILE:]
        out[TILE : 2 * TILE, cols_here] = jnp.where(low, one_low, rolled[:TILE]) * masks[1]
        out[0:TILE, cols_here] = jnp.where(low, two_low, two_high) * masks[0]
        last_turned, last_rolled = turned, rolled


def final(ring, moms, w, band_next, cols, rot):
    parts = len(ring)
    height = (BMAX + 1) * TILE + LANE // parts // (QW // LANE)
    return pl.pallas_call(
        functools.partial(final_kernel, parts, rot, len(moms), band_next.shape[0]),
        in_specs=[SMEM] + [VMEM] * (1 + parts + len(moms)),
        out_specs=[VMEM, VMEM],
        out_shape=[
            jax.ShapeDtypeStruct((SPAN * TILE, cols), jnp.float32),
            jax.ShapeDtypeStruct(w.shape[1:], jnp.float32),
        ],
        scratch_shapes=[pltpu.VMEM((parts, height, QW), jnp.float32)],
        compiler_params=params(16),
        name="final",
    )(band_next, w, *ring, *moms)


class Side:
    def __init__(self, flag, one, two):
        self.flag, self.one, self.two = flag, one, two

    def pick(self, at, convert):
        if self.flag is None:
            return self.one[at]
        return jnp.where(self.flag, convert(self.one[at]), convert(self.two[at]))

    def vector(self, at):
        return self.pick(at, lambda code: decode(code, Z_LARGEST, Z_ROOTS))

    def band(self, at):
        return self.pick(at, lambda code: from_code(code) * (1.0 / LEVELS))

    def flags(self, at):
        return self.pick(at, from_code)


def krylov_kernel(
    tile_total, sb, paired, band, ldt, z, obs, got_e, got_o, w_out, mom_out,
    dh, dl, ucat, seen, u_prev, y
):
    rows = ldt.shape[1]
    traits = z.shape[1]
    own_blocks = rows // LANE
    zb = HZ // LANE
    bb = HB // LANE
    first_tile = lax.axis_index("smp") * (rows // TILE)
    even = lax.rem(lax.axis_index("smp"), 2) == 0 if paired else None
    halo_r = Side(even, got_e, got_o)
    halo_l = Side(even, got_o, got_e)
    nb = obs.shape[0]
    ld_rows = SPAN * TILE
    total_blocks = own_blocks + 2 * zb

    tail = (slice(HZ + bb * ld_rows, got_e.shape[0]), slice(None))
    flags_l, flags_r = halo_l.flags(tail), halo_r.flags(tail)

    for c in range(total_blocks):
        if c < zb:
            vec = halo_l.vector((slice(c * LANE, (c + 1) * LANE), slice(0, traits)))
            flags = [flags_l[c * nb + i : c * nb + i + 1, :] for i in range(nb)]
        elif c < zb + own_blocks:
            o = c - zb
            vec = z[o * LANE : (o + 1) * LANE, :]
            flags = [
                obs[i : i + 1, o * LANE : (o + 1) * LANE].astype(jnp.float32) for i in range(nb)
            ]
        else:
            o = c - zb - own_blocks
            vec = halo_r.vector((slice(o * LANE, (o + 1) * LANE), slice(0, traits)))
            flags = [flags_r[o * nb + i : o * nb + i + 1, :] for i in range(nb)]
        wide = jnp.concatenate(
            [jnp.broadcast_to(f, (TBLK, LANE)) for f in flags], axis=0
        )
        mask = wide.T
        here = slice(c * LANE, (c + 1) * LANE)
        seen[here, :] = mask
        start = mask * vec
        high = start.astype(jnp.bfloat16)
        u_prev[here, :] = start
        ucat[here, :traits] = high
        ucat[here, traits:] = (start - high.astype(jnp.float32)).astype(jnp.bfloat16)

    per = sb // LANE
    low = low_lanes((TILE, LANE))
    sub = lax.broadcasted_iota(jnp.int32, (TILE, LANE), 0)
    lane = lax.broadcasted_iota(jnp.int32, (TILE, LANE), 1)
    chunks = SPAN + 1
    for c in range(own_blocks + 2 * bb):
        if c < bb:
            full = halo_l.band((slice(HZ + c * ld_rows, HZ + (c + 1) * ld_rows), slice(None)))
            get = lambda q, full=full: full[q * TILE : (q + 1) * TILE]
        elif c < bb + own_blocks:
            get = lambda q, c=c: ldt[q * TILE : (q + 1) * TILE, (c - bb) * LANE : (c - bb + 1) * LANE]
        else:
            o = c - bb - own_blocks
            full = halo_r.band((slice(HZ + o * ld_rows, HZ + (o + 1) * ld_rows), slice(None)))
            get = lambda q, full=full: full[q * TILE : (q + 1) * TILE]
        masks = mask_rows(band, first_tile + 2 * (c - bb), tile_total)
        s, h = c // per, c % per
        cols = slice(h * LANE, (h + 1) * LANE)
        parts = [get(q) * masks[q] for q in range(SPAN)]
        zero = jnp.zeros((TILE, LANE), jnp.float32)
        for j in range(chunks):
            left = parts[j] if j < SPAN else zero
            right = parts[j - 1] if j >= 1 else zero
            value = jnp.where(low, left, right)
            if BMAX <= j < BMAX + 2:
                value = value - (sub + TILE * (j - BMAX) == lane).astype(jnp.float32)
            high = value.astype(jnp.bfloat16)
            at = slice(h * LANE + j * TILE, h * LANE + (j + 1) * TILE)
            dh[s, at, cols] = high
            dl[s, at, cols] = (value - high.astype(jnp.float32)).astype(jnp.bfloat16)
        for x in range(per):
            if x < h:
                at = slice(x * LANE, (x + 1) * LANE)
            elif x > h:
                at = slice((x + 2) * LANE, (x + 3) * LANE)
            else:
                continue
            blank = jnp.zeros((LANE, LANE), jnp.bfloat16)
            dh[s, at, cols] = blank
            dl[s, at, cols] = blank

    supers = (rows + 2 * HB) // sb
    window = sb + 2 * REACH

    def product(both, rest):
        return both[:, :traits] + both[:, traits:] + rest

    def apply():
        for s in range(supers):
            vec = ucat[REACH + s * sb : REACH + (s + 1) * sb, :]
            part = product(dot(dh[s], vec), dot(dl[s], vec[:, :traits]))
            at = s * sb
            if s == 0:
                y[at : at + window, :] = part
            else:
                y[at : at + 2 * REACH, :] += part[: 2 * REACH]
                y[at + 2 * REACH : at + window, :] = part[2 * REACH :]

    own = slice(HZ, HZ + rows)
    sums = []
    for step in range(ITERS):
        apply()
        if step == 0:
            for edge_rows, edge_cols, s, target, source in (
                (slice(0, LANE), slice(0, LANE), 0, 1, 0),
                (
                    slice(window - LANE, window),
                    slice(sb - LANE, sb),
                    supers - 1,
                    total_blocks - 2,
                    total_blocks - 1,
                ),
            ):
                vec = ucat[source * LANE : (source + 1) * LANE, :]
                part = product(
                    tdot(dh[s, edge_rows, edge_cols], vec),
                    tdot(dl[s, edge_rows, edge_cols], vec[:, :traits]),
                )
                y[target * LANE : (target + 1) * LANE, :] += part
        u_own = u_prev[own, :]
        y_own = y[own, :]
        w_out[step] = u_own + y_own
        sums.append(jnp.sum(u_own * u_own, axis=0, keepdims=True))
        sums.append(jnp.sum(u_own * y_own, axis=0, keepdims=True))
        if step < ITERS - 1:
            edge = (step + 1) * REACH
            here = slice(edge, total_blocks * LANE - edge)
            nxt = seen[here, :] * y[here, :]
            high = nxt.astype(jnp.bfloat16)
            u_prev[here, :] = nxt
            ucat[here, :traits] = high
            ucat[here, traits:] = (nxt - high.astype(jnp.float32)).astype(jnp.bfloat16)
    mom_out[...] = jnp.concatenate(
        sums + [jnp.zeros((8 - len(sums), traits), jnp.float32)], axis=0
    )


def krylov(ldt, z, obs, got_e, got_o, band_prev, paired):
    rows, traits = z.shape
    wide = rows + 2 * HB
    sb = 2 * LANE if wide % (2 * LANE) == 0 else LANE
    ext = rows + 2 * HZ
    supers = wide // sb
    return pl.pallas_call(
        functools.partial(krylov_kernel, band_prev.shape[0], sb, paired),
        in_specs=[SMEM] + [VMEM] * 5,
        out_specs=[VMEM, VMEM],
        out_shape=[
            jax.ShapeDtypeStruct((ITERS, rows, traits), jnp.float32),
            jax.ShapeDtypeStruct((8, traits), jnp.float32),
        ],
        scratch_shapes=[
            pltpu.VMEM((supers, sb + 2 * REACH, sb), jnp.bfloat16),
            pltpu.VMEM((supers, sb + 2 * REACH, sb), jnp.bfloat16),
            pltpu.VMEM((ext, 2 * traits), jnp.bfloat16),
            pltpu.VMEM((ext, traits), jnp.float32),
            pltpu.VMEM((ext, traits), jnp.float32),
            pltpu.VMEM((ext, traits), jnp.float32),
        ],
        compiler_params=params(28),
        cost_estimate=pl.CostEstimate(
            flops=ITERS * 6 * ext * SPAN * TILE * traits, bytes_accessed=ldt.size * 4, transcendentals=0
        ),
        name="krylov",
    )(band_prev, ldt, z, obs, got_e, got_o)


def solve(w, mom, out):
    m = [mom[i : i + 1, :] for i in range(2 * ITERS)]
    shift = 1.0 + RIDGE
    h = [shift * m[i] + m[i + 1] for i in range(2 * ITERS - 1)]
    d0 = h[0]
    l10 = h[1] / d0
    l20 = h[2] / d0
    d1 = h[2] - l10 * h[1]
    t12 = h[3] - l20 * h[1]
    ok1 = d1 > TINY * h[2]
    r1 = jnp.where(ok1, 1.0 / jnp.where(ok1, d1, 1.0), 0.0)
    l21 = t12 * r1
    d2 = h[4] - l20 * h[2] - l21 * t12
    ok2 = ok1 & (d2 > TINY * h[4])
    r2 = jnp.where(ok2, 1.0 / jnp.where(ok2, d2, 1.0), 0.0)
    z0 = m[0]
    z1 = m[1] - l10 * z0
    z2 = m[2] - l20 * z0 - l21 * z1
    c2 = z2 * r2
    c1 = z1 * r1 - l21 * c2
    c0 = z0 / d0 - l10 * c1 - l20 * c2
    out[...] = c0 * w[0] + c1 * w[1] + c2 * w[2]


def packed(z, ldt, obs):
    z = jnp.pad(z, ((0, 0), (0, LANE - z.shape[1])))
    obs = obs.astype(jnp.float32)
    parts = [z]
    parts += [ldt[:, i : i + LANE] for i in range(0, ldt.shape[1], LANE)]
    parts += [obs[:, i : i + LANE] for i in range(0, obs.shape[1], LANE)]
    height = sum(p.shape[0] for p in parts)
    parts.append(jnp.zeros((-height % 16, LANE), jnp.float32))
    return jnp.concatenate(parts, axis=0)


def halos(z, ldt, obs, axis):
    count = lax.axis_size(axis)
    rows = z.shape[0]

    def shifted(value, by):
        pairs = [(i, i + by) for i in range(count) if 0 <= i + by < count]
        return lax.ppermute(value, axis, pairs)

    def gather(value, width, dim):
        lefts, rights = [], []
        hop, have = 1, 0
        while have < width:
            take = min(rows, width - have)
            lefts.insert(0, shifted(lax.slice_in_dim(value, rows - take, rows, axis=dim), hop))
            rights.append(shifted(lax.slice_in_dim(value, 0, take, axis=dim), -hop))
            have += take
            hop += 1
        return jnp.concatenate(lefts, dim), jnp.concatenate(rights, dim)

    zs = gather(z, HZ, 0)
    lds = gather(ldt, HB, 1)
    seens = gather(obs, HZ, 1)
    return packed(zs[0], lds[0], seens[0]), packed(zs[1], lds[1], seens[1])


def local(dosage, allele_mean, snp_scale, band_next, ld_prev, band_prev, zscores, observed):
    samples, cols = dosage.shape
    rows = ld_prev.shape[0]
    n_smp = lax.axis_size("smp")
    ldt = ld_prev.T
    obs = observed.T
    line = ("snp", "pair")
    paired = rows >= HZ

    sent = pack(dosage, zscores, ldt, obs, paired)
    dos_e = exchange(sent[0], line, 0)
    dos_o = exchange(sent[1], line, 1)
    if paired:
        got_e = exchange(sent[2], ("smp",), 0)
        got_o = exchange(sent[3], ("smp",), 1)
    else:
        got_o, got_e = halos(zscores, ldt, obs, "smp")

    parts = cols // QW
    rot = parts == n_smp and zscores.shape[1] == LANE
    inv = 1.0 / (samples if rot else samples * n_smp)
    mean = allele_mean.reshape(-1, LANE)
    scale = snp_scale.reshape(-1, LANE)
    blocks = gram_parts(dosage, mean, scale, rot, inv)
    blocks = cross_parts(sent[0], sent[1], dos_e, dos_o, mean, scale, blocks, cols, rot, inv)
    if rot:

        def cycle(value, by):
            return lax.ppermute(value, "smp", [(i, (i + by) % n_smp) for i in range(n_smp)])

        got = [cycle(blocks[by], by) for by in range(1, n_smp)]
    w, mom = krylov(ldt, zscores, obs, got_e, got_o, band_prev, paired)
    if rot:
        mine = total_of(blocks[0], got, mom)
        ring = [mine] + [cycle(mine, by) for by in range(1, n_smp)]
        moms = []
    else:
        ring = list(lax.psum(tuple(blocks), "smp"))
        moms = [lax.psum(mom, "smp")]
    ldn, imputed = final(ring, moms, w, band_next, cols, rot)
    return ldn.T, imputed


def solution(mesh):
    return jax.shard_map(
        local,
        mesh=mesh,
        in_specs=(
            P(("grp", "smp"), ("snp", "pair")),
            P("grp"),
            P("grp"),
            P("grp"),
            P(("grp", "smp"), None),
            P("grp"),
            P(("grp", "smp"), ("snp", "pair")),
            P(("grp", "smp"), ("snp", "pair")),
        ),
        out_specs=(P(("grp", "snp", "pair"), None), P(("grp", "smp"), ("snp", "pair"))),
        check_vma=False,
    )
```

```python
import functools
import jax
import jax.numpy as jnp
from jax import lax
from jax.experimental import pallas as pl
from jax.experimental.pallas import tpu as pltpu
from jax.sharding import PartitionSpec as P

TILE = 64
BMAX = 2
TBLK = 64
ITERS = 3
RIDGE = 1.0
SPAN = 2 * BMAX + 1
REACH = TILE * BMAX
LANE = 128
QW = 256
HZ = ITERS * REACH
HB = (ITERS - 1) * REACH
TINY = 1e-6
VMEM = pl.BlockSpec(memory_space=pltpu.VMEM)
SMEM = pl.BlockSpec(memory_space=pltpu.SMEM)


def params(mib):
    return pltpu.CompilerParams(vmem_limit_bytes=mib * 1024 * 1024)


def mask_rows(band_ref, first_tile, total):
    def width(t):
        inside = (t >= 0) & (t < total)
        return jnp.where(inside, band_ref[jnp.clip(t, 0, total - 1)], 0)

    widths = [width(first_tile + d) for d in range(-BMAX, BMAX + 2)]
    low = lax.broadcasted_iota(jnp.int32, (1, LANE), 1) < TILE
    rows = []
    for q in range(-BMAX, BMAX + 1):
        flags = [
            (abs(q) <= jnp.minimum(widths[BMAX + t], widths[BMAX + t + q])).astype(jnp.float32)
            for t in range(2)
        ]
        rows.append(jnp.where(low, flags[0], flags[1]))
    return rows


def low_lanes(shape):
    return lax.broadcasted_iota(jnp.int32, shape, 1) < TILE


def tdot(left, right):
    return lax.dot_general(
        left, right, (((0,), (0,)), ((), ())), preferred_element_type=jnp.float32
    )


def dot(left, right):
    return lax.dot_general(
        left, right, (((1,), (0,)), ((), ())), preferred_element_type=jnp.float32
    )


LEVELS = 32000.0
Z_LARGEST = 22.0
Z_ROOTS = 2
LARGEST = 36.0


def encode(value, largest=LARGEST, roots=3):
    size = jnp.minimum(jnp.abs(value) * (1.0 / largest), 1.0) + 1e-30
    for _ in range(roots):
        size = size * lax.rsqrt(size)
    code = size * LEVELS + 0.5
    return to_code(jnp.where(value < 0, -code, code))


def decode(code, largest=LARGEST, roots=3):
    value = from_code(code)
    size = value * (1.0 / LEVELS)
    for _ in range(roots):
        size = size * size
    size = size * largest
    return jnp.where(value < 0, -size, size)


def encode_exact(value):
    size = jnp.maximum(jnp.abs(value), 1e-30)
    power = jnp.clip(jnp.floor(jnp.log2(size)), -100.0, 120.0)
    scaled = value * jnp.exp2(-power) * 2.0**13
    high = jnp.round(scaled)
    low = jnp.round((scaled - high) * 2.0**14)
    return power, high, low


def decode_exact(power, high, low):
    return (high * 2.0**-13 + low * 2.0**-27) * jnp.exp2(power)


def to_code(value):
    return value.astype(jnp.int32).astype(jnp.int16)


def from_code(code):
    return code.astype(jnp.int32).astype(jnp.float32)


def line_index(axes):
    place = lax.axis_index(axes[0])
    for axis in axes[1:]:
        place = place * lax.axis_size(axis) + lax.axis_index(axis)
    return place


def in_hbm(value):
    return pltpu.with_memory_space_constraint(value, pltpu.HBM)


def halo_height(nb):
    height = HZ + HB // LANE * SPAN * TILE + HZ // LANE * nb
    return height + -height % 16


def pack_kernel(dos, z, ldt, obs, dos_e, dos_o, *rest):
    cols = dos.shape[1]
    rows = z.shape[0]
    sem = rest[-1]
    copies = []

    def start(source, target):
        copy = pltpu.make_async_copy(source, target, sem.at[len(copies)])
        copy.start()
        copies.append(copy)

    even = lax.rem(line_index(("snp", "pair")), 2) == 0
    to_e = pl.multiple_of(jnp.where(even, cols - LANE, 0), LANE)
    to_o = pl.multiple_of(jnp.where(even, 0, cols - LANE), LANE)
    halo = ()
    if len(rest) > 1:
        halo, (zs, lds, flags) = rest[:2], rest[2:5]
        even = lax.rem(lax.axis_index("smp"), 2) == 0
        for i, last in enumerate((even, jnp.logical_not(even))):
            row = pl.multiple_of(jnp.where(last, rows - HZ, 0), LANE)
            col = pl.multiple_of(jnp.where(last, rows - HB, 0), LANE)
            start(z.at[pl.ds(row, HZ), :], zs.at[i])
            start(ldt.at[:, pl.ds(col, HB)], lds.at[i])
            start(obs.at[:, pl.ds(row, HZ)], flags.at[i])
    start(dos.at[:, pl.ds(to_e, LANE)], dos_e)
    start(dos.at[:, pl.ds(to_o, LANE)], dos_o)
    for i, out in enumerate(halo):
        nb = obs.shape[0]
        for copy in copies[3 * i : 3 * i + 3]:
            copy.wait()
        out[0:HZ, : z.shape[1]] = encode(zs[i], Z_LARGEST, Z_ROOTS)
        base = HZ
        for j in range(HB // LANE):
            out[base : base + SPAN * TILE, :] = to_code(
                jnp.round(lds[i, :, j * LANE : (j + 1) * LANE] * LEVELS)
            )
            base += SPAN * TILE
        bits = [flags[i, :, j * LANE : (j + 1) * LANE] for j in range(HZ // LANE)]
        blank = out.shape[0] - base - nb * len(bits)
        bits.append(jnp.zeros((blank, LANE), jnp.int32))
        out[base:, :] = jnp.concatenate(bits, axis=0).astype(jnp.int16)
    for copy in copies[3 * len(halo) :]:
        copy.wait()


def pack(dosage, z, ldt, obs, with_halo):
    samples = dosage.shape[0]
    shapes = [jax.ShapeDtypeStruct((samples, LANE), dosage.dtype)] * 2
    copies = 2
    scratch = []
    if with_halo:
        shapes += [jax.ShapeDtypeStruct((halo_height(obs.shape[0]), LANE), jnp.int16)] * 2
        copies += 6
        scratch = [
            pltpu.VMEM((2, HZ, z.shape[1]), z.dtype),
            pltpu.VMEM((2, SPAN * TILE, HB), ldt.dtype),
            pltpu.VMEM((2, obs.shape[0], HZ), obs.dtype),
        ]
    far = pl.BlockSpec(memory_space=pltpu.HBM)
    return pl.pallas_call(
        pack_kernel,
        in_specs=[far] * 4,
        out_specs=[VMEM] * len(shapes),
        out_shape=shapes,
        scratch_shapes=scratch + [pltpu.SemaphoreType.DMA((copies,))],
        compiler_params=params(8),
        name="pack",
    )(in_hbm(dosage), in_hbm(z), in_hbm(ldt), in_hbm(obs))


def exchange(value, axes, phase):
    count = 1
    for axis in axes:
        count *= lax.axis_size(axis)
    if phase == 0 and lax.axis_size(axes[-1]) == 2 and len(axes) > 1:
        return lax.ppermute(value, axes[-1], [(0, 1), (1, 0)])
    pairs = []
    for i in range(phase, count - 1, 2):
        pairs += [(i, i + 1), (i + 1, i)]
    return lax.ppermute(value, axes, pairs)


DIAG = TILE // 2
RING = (0, 2, 3, 1)
NEAR = DIAG + BMAX * TILE


def quarter_at(step, first, parts):
    return jnp.bitwise_xor(step, first)


def tail_rows(parts):
    return TILE // parts


def standard(values, mean, scale, block):
    row = jnp.clip(block, 0, mean.shape[0] - 1)
    m = mean[pl.ds(row, 1), :]
    s = scale[pl.ds(row, 1), :]
    return ((values.astype(jnp.float32) - m) * s).astype(jnp.bfloat16)


def gram_kernel(parts, rot, inv, dos, mean, scale, *rest):
    outs = rest[:parts]
    raw, normed, sem = rest[parts:]
    blocks = QW // LANE
    samples, cols = dos.shape
    base = line_index(("snp", "pair")) * (cols // LANE)
    first = lax.axis_index("smp") if rot else 0

    def quarter_of(g):
        return lax.rem(g + first, parts)

    def fetch(g):
        at = pl.multiple_of(quarter_of(g) * QW, QW)
        return pltpu.make_async_copy(dos.at[:, pl.ds(at, QW)], raw.at[g], sem.at[g])

    for g in range(parts):
        fetch(g).start()

    def settle(g):
        fetch(g).wait()
        block = quarter_of(g) * blocks
        for b in range(blocks):
            at = pl.multiple_of((block + b) * LANE, LANE)
            normed[:, pl.ds(at, LANE)] = standard(
                raw[g, :, b * LANE : (b + 1) * LANE], mean, scale, base + block + b
            )

    normed[:, cols:] = jnp.zeros((samples, LANE), jnp.bfloat16)
    settle(0)
    rows = (BMAX + 1) * TILE
    tail = tail_rows(parts)
    low = low_lanes((rows, LANE))
    sub = lax.broadcasted_iota(jnp.int32, (TILE, LANE), 0)
    lane = lax.broadcasted_iota(jnp.int32, (TILE, LANE), 1)
    spot = lax.broadcasted_iota(jnp.int32, (tail, LANE), 0)

    def step(g, _):
        @pl.when(g < parts - 1)
        def _():
            settle(jnp.minimum(g + 1, parts - 1))

        at = pl.multiple_of(quarter_of(g) * QW, QW)
        full = tdot(normed[:, pl.ds(at, QW + LANE)], normed[:, pl.ds(at, QW)])
        pieces = []
        for b in range(blocks):
            cut = slice(b * LANE, (b + 1) * LANE)
            pieces.append(
                inv
                * jnp.where(
                    low,
                    full[b * LANE : b * LANE + rows, cut],
                    full[b * LANE + TILE : b * LANE + TILE + rows, cut],
                )
            )
        folded = [
            jnp.where(sub <= lane, p[:TILE], pltpu.roll(p[:TILE], TILE, axis=1)) for p in pieces
        ]
        folded = jnp.where(lane < TILE, folded[0], pltpu.roll(folded[1], TILE, axis=1))
        diagonals = [
            jnp.sum(jnp.where(sub == lane - TILE, p[:TILE], 0.0), axis=0, keepdims=True)
            for p in pieces
        ]
        ends = jnp.where(spot == 0, diagonals[0], jnp.where(spot == 1, diagonals[1], 0.0))
        slot = quarter_at(quarter_of(g), first, parts)
        for i in range(parts):

            @pl.when(slot == i)
            def _(i=i):
                send = encode if rot and i > 0 else (lambda v: v)
                for b in range(blocks):
                    cut = slice(b * LANE, (b + 1) * LANE)
                    outs[i][:DIAG, cut] = send(folded[b * DIAG : (b + 1) * DIAG])
                    outs[i][DIAG:NEAR, cut] = send(pieces[b][TILE:])
                outs[i][NEAR:, :LANE] = jnp.zeros((tail, LANE), outs[i].dtype)
                outs[i][NEAR:, LANE:] = send(ends)

        return 0

    lax.fori_loop(0, parts, step, 0)


def gram_parts(dosage, mean, scale, rot, inv):
    samples, cols = dosage.shape
    parts = cols // QW
    rows = NEAR + tail_rows(parts)
    kinds = [jnp.float32] + [jnp.int16 if rot else jnp.float32] * (parts - 1)
    return pl.pallas_call(
        functools.partial(gram_kernel, parts, rot, inv),
        in_specs=[pl.BlockSpec(memory_space=pltpu.HBM)] + [VMEM] * 2,
        out_specs=[VMEM] * parts,
        out_shape=[jax.ShapeDtypeStruct((rows, QW), kind) for kind in kinds],
        scratch_shapes=[
            pltpu.VMEM((parts, samples, QW), jnp.bfloat16),
            pltpu.VMEM((samples, cols + LANE), jnp.bfloat16),
            pltpu.SemaphoreType.DMA((parts,)),
        ],
        compiler_params=params(24),
        cost_estimate=pl.CostEstimate(
            flops=2 * samples * cols * (QW + LANE), bytes_accessed=dosage.size * 4, transcendentals=0
        ),
        name="gram",
    )(in_hbm(dosage), mean, scale)


def cross_kernel(parts, rot, inv, cols, sent_e, sent_o, got_e, got_o, mean, scale, *rest):
    ins, outs, (zero, one) = rest[:parts], rest[parts : 2 * parts], rest[-2:]
    blocks = QW // LANE
    tail = tail_rows(parts)
    place = line_index(("snp", "pair"))
    base = place * (cols // LANE)
    end = base + cols // LANE
    even = lax.rem(place, 2) == 0
    pick = lambda one, two: jnp.where(even, one[...], two[...])
    right = standard(pick(got_e, got_o), mean, scale, end)
    left = standard(pick(got_o, got_e), mean, scale, base - 1)
    last = standard(pick(sent_e, sent_o), mean, scale, end - 1)
    head = standard(pick(sent_o, sent_e), mean, scale, base)
    ahead = inv * tdot(right, last)
    behind = inv * tdot(left, head)
    low = low_lanes((TILE, LANE))
    turned = pltpu.roll(behind[TILE:], TILE, axis=1)
    zero[...] = jnp.where(low, behind[:TILE], turned)
    one[...] = turned
    far = slice((blocks - 1) * LANE, blocks * LANE)
    first = lax.axis_index("smp") if rot else 0
    for i in range(parts):
        send = encode if rot and i > 0 else (lambda v: v)
        wide = (lambda v: v.astype(jnp.int32)) if rot and i > 0 else (lambda v: v)
        kind = outs[i].dtype
        outs[i][:NEAR, :] = ins[i][:NEAR, :]
        quarter = quarter_at(i, first, parts)
        share = pl.ds(pl.multiple_of(quarter * tail, 8), tail)
        outs[i][NEAR:, :LANE] = send(zero[share, :])
        outs[i][NEAR:, LANE:] = jnp.where(
            low_lanes((tail, LANE)), wide(send(one[share, :])), wide(ins[i][NEAR:, LANE:])
        ).astype(kind)

        @pl.when(quarter == parts - 1)
        def _(i=i, send=send, wide=wide, kind=kind):
            next_one = slice(DIAG, DIAG + TILE)
            outs[i][next_one, far] = jnp.where(
                low, wide(ins[i][next_one, far]), wide(send(ahead[:TILE]))
            ).astype(kind)
            outs[i][DIAG + TILE : NEAR, far] = send(jnp.where(low, ahead[:TILE], ahead[TILE:]))


def cross_parts(sent_e, sent_o, got_e, got_o, mean, scale, blocks, cols, rot, inv):
    parts = len(blocks)
    height = NEAR + tail_rows(parts)
    return pl.pallas_call(
        functools.partial(cross_kernel, parts, rot, inv, cols),
        in_specs=[VMEM] * (6 + parts),
        out_specs=[VMEM] * parts,
        out_shape=[jax.ShapeDtypeStruct((height, QW), b.dtype) for b in blocks],
        scratch_shapes=[pltpu.VMEM((TILE, LANE), jnp.float32)] * 2,
        compiler_params=params(12),
        name="cross",
    )(sent_e, sent_o, got_e, got_o, mean, scale, *blocks)


def total_kernel(count, own, *rest):
    others, mom, out = rest[:-2], rest[-2], rest[-1]
    height = own.shape[0]
    total = own[...]
    for other in others:
        total = total + decode(other[...])
    out[0:height, :] = encode(total * (1.0 / count))
    power, high, low = encode_exact(mom[...])
    lanes = mom.shape[1]
    top = jnp.concatenate([power, low], axis=1)
    bottom = jnp.concatenate([high, jnp.zeros_like(low)], axis=1)
    out[height : height + 16, :] = to_code(jnp.concatenate([top, bottom], axis=0))


def total_of(own, others, mom):
    count = 1 + len(others)
    return pl.pallas_call(
        functools.partial(total_kernel, count),
        in_specs=[VMEM] * (count + 1),
        out_specs=VMEM,
        out_shape=jax.ShapeDtypeStruct((own.shape[0] + 16, own.shape[1]), jnp.int16),
        compiler_params=params(8),
        name="total",
    )(own, *others, mom)


def final_kernel(parts, rot, moments, tile_total, band, w, *rest):
    ring = rest[:parts]
    moms = rest[parts : parts + moments]
    out_far, imputed_far, held, out, imputed, sem = rest[parts + moments :]
    blocks = QW // LANE
    tail = tail_rows(parts)
    height = NEAR + tail
    low = low_lanes((TILE, LANE))
    sub = lax.broadcasted_iota(jnp.int32, (TILE, LANE), 0)
    lane = lax.broadcasted_iota(jnp.int32, (TILE, LANE), 1)
    cols = out.shape[1]
    first_tile = line_index(("snp", "pair")) * (cols // TILE)
    copies = []

    def ship(source, target):
        copy = pltpu.make_async_copy(source, target, sem.at[len(copies)])
        copy.start()
        copies.append(copy)

    def swap(value):
        return pltpu.roll(value, TILE, axis=1)

    if rot:
        k = lax.axis_index("smp")
        total = None
        for piece, by in zip(ring, RING):
            held[quarter_at(by, k, parts)] = decode(piece[0:height, :])
            code = from_code(piece[height : height + 16, :])
            lanes = code.shape[1] // 2
            mom = decode_exact(code[:8, :lanes], code[8:, :lanes], code[:8, lanes:])
            total = mom if total is None else total + mom
    else:
        for by in range(parts):
            held[by] = ring[by][...]
        total = moms[0][...]
    solve(w, total, imputed)
    ship(imputed, imputed_far)
    for quarter in range(parts):
        fold = jnp.concatenate(
            [held[quarter, :DIAG, b * LANE : (b + 1) * LANE] for b in range(blocks)], axis=0
        )
        mirror = jnp.concatenate([fold, swap(fold)], axis=0).T[:TILE]
        for b in range(blocks):
            a = quarter * blocks + b
            cut = slice(b * LANE, (b + 1) * LANE)
            cols_here = slice(a * LANE, (a + 1) * LANE)
            masks = mask_rows(band, first_tile + 2 * a, tile_total)
            here, there = (fold, mirror) if b == 0 else (swap(fold), swap(mirror))
            second = jnp.where(
                sub == lane - TILE,
                held[quarter, NEAR + b : NEAR + b + 1, LANE : 2 * LANE],
                swap(jnp.where(lane < sub, here, there)),
            )
            centre = jnp.where(low, jnp.where(sub <= lane, here, there), second)
            out[BMAX * TILE : (BMAX + 1) * TILE, cols_here] = centre * masks[BMAX]
            for q in range(1, BMAX + 1):
                out[(BMAX + q) * TILE : (BMAX + q + 1) * TILE, cols_here] = (
                    held[quarter, DIAG + (q - 1) * TILE : DIAG + q * TILE, cut] * masks[BMAX + q]
                )
            turned = held[quarter, DIAG:NEAR, cut].T
            rolled = swap(turned)
            if a == 0:
                cross = [
                    jnp.concatenate(
                        [held[j, NEAR:height, c * LANE : (c + 1) * LANE] for j in range(parts)],
                        axis=0,
                    )
                    for c in range(2)
                ]
                one_low, two_low, two_high = swap(cross[0]), cross[0], swap(cross[1])
            else:
                one_low, two_low, two_high = (
                    last_turned[TILE:], last_rolled[:TILE], last_turned[TILE:]
                )
            out[TILE : 2 * TILE, cols_here] = jnp.where(low, one_low, rolled[:TILE]) * masks[1]
            out[0:TILE, cols_here] = jnp.where(low, two_low, two_high) * masks[0]
            last_turned, last_rolled = turned, rolled
        block = slice(quarter * QW, (quarter + 1) * QW)
        ship(out.at[:, block], out_far.at[:, block])
    for copy in copies:
        copy.wait()


def final(ring, moms, w, band_next, cols, rot):
    parts = len(ring)
    shapes = [
        jax.ShapeDtypeStruct((SPAN * TILE, cols), jnp.float32),
        jax.ShapeDtypeStruct(w.shape[1:], jnp.float32),
    ]
    return pl.pallas_call(
        functools.partial(final_kernel, parts, rot, len(moms), band_next.shape[0]),
        in_specs=[SMEM] + [VMEM] * (1 + parts + len(moms)),
        out_specs=[pl.BlockSpec(memory_space=pltpu.HBM)] * 2,
        out_shape=shapes,
        scratch_shapes=[
            pltpu.VMEM((parts, NEAR + tail_rows(parts), QW), jnp.float32),
            pltpu.VMEM(shapes[0].shape, jnp.float32),
            pltpu.VMEM(shapes[1].shape, jnp.float32),
            pltpu.SemaphoreType.DMA((parts + 1,)),
        ],
        compiler_params=params(16),
        name="final",
    )(band_next, w, *ring, *moms)


class Side:
    def __init__(self, flag, one, two):
        self.flag, self.one, self.two = flag, one, two

    def pick(self, at, convert):
        if self.flag is None:
            return self.one[at]
        return jnp.where(self.flag, convert(self.one[at]), convert(self.two[at]))

    def vector(self, at):
        return self.pick(at, lambda code: decode(code, Z_LARGEST, Z_ROOTS))

    def band(self, at):
        return self.pick(at, lambda code: from_code(code) * (1.0 / LEVELS))

    def flags(self, at):
        return self.pick(at, from_code)


def krylov_kernel(
    tile_total, sb, paired, band, ldt, z, obs, got_e, got_o, w_out, mom_out,
    dh, dl, ucat, seen, u_prev, y
):
    rows = ldt.shape[1]
    traits = z.shape[1]
    own_blocks = rows // LANE
    zb = HZ // LANE
    bb = HB // LANE
    first_tile = lax.axis_index("smp") * (rows // TILE)
    even = lax.rem(lax.axis_index("smp"), 2) == 0 if paired else None
    halo_r = Side(even, got_e, got_o)
    halo_l = Side(even, got_o, got_e)
    nb = obs.shape[0]
    ld_rows = SPAN * TILE
    total_blocks = own_blocks + 2 * zb

    tail = (slice(HZ + bb * ld_rows, got_e.shape[0]), slice(None))
    flags_l, flags_r = halo_l.flags(tail), halo_r.flags(tail)

    for c in range(total_blocks):
        if c < zb:
            vec = halo_l.vector((slice(c * LANE, (c + 1) * LANE), slice(0, traits)))
            flags = [flags_l[c * nb + i : c * nb + i + 1, :] for i in range(nb)]
        elif c < zb + own_blocks:
            o = c - zb
            vec = z[o * LANE : (o + 1) * LANE, :]
            flags = [
                obs[i : i + 1, o * LANE : (o + 1) * LANE].astype(jnp.float32) for i in range(nb)
            ]
        else:
            o = c - zb - own_blocks
            vec = halo_r.vector((slice(o * LANE, (o + 1) * LANE), slice(0, traits)))
            flags = [flags_r[o * nb + i : o * nb + i + 1, :] for i in range(nb)]
        wide = jnp.concatenate(
            [jnp.broadcast_to(f, (TBLK, LANE)) for f in flags], axis=0
        )
        mask = wide.T
        here = slice(c * LANE, (c + 1) * LANE)
        seen[here, :] = mask
        start = mask * vec
        high = start.astype(jnp.bfloat16)
        u_prev[here, :] = start
        ucat[here, :traits] = high
        ucat[here, traits:] = (start - high.astype(jnp.float32)).astype(jnp.bfloat16)

    per = sb // LANE
    low = low_lanes((TILE, LANE))
    sub = lax.broadcasted_iota(jnp.int32, (TILE, LANE), 0)
    lane = lax.broadcasted_iota(jnp.int32, (TILE, LANE), 1)
    chunks = SPAN + 1
    for c in range(own_blocks + 2 * bb):
        if c < bb:
            full = halo_l.band((slice(HZ + c * ld_rows, HZ + (c + 1) * ld_rows), slice(None)))
            get = lambda q, full=full: full[q * TILE : (q + 1) * TILE]
        elif c < bb + own_blocks:
            get = lambda q, c=c: ldt[q * TILE : (q + 1) * TILE, (c - bb) * LANE : (c - bb + 1) * LANE]
        else:
            o = c - bb - own_blocks
            full = halo_r.band((slice(HZ + o * ld_rows, HZ + (o + 1) * ld_rows), slice(None)))
            get = lambda q, full=full: full[q * TILE : (q + 1) * TILE]
        masks = mask_rows(band, first_tile + 2 * (c - bb), tile_total)
        s, h = c // per, c % per
        cols = slice(h * LANE, (h + 1) * LANE)
        parts = [get(q) * masks[q] for q in range(SPAN)]
        zero = jnp.zeros((TILE, LANE), jnp.float32)
        for j in range(chunks):
            left = parts[j] if j < SPAN else zero
            right = parts[j - 1] if j >= 1 else zero
            value = jnp.where(low, left, right)
            if BMAX <= j < BMAX + 2:
                value = value - (sub + TILE * (j - BMAX) == lane).astype(jnp.float32)
            high = value.astype(jnp.bfloat16)
            at = slice(h * LANE + j * TILE, h * LANE + (j + 1) * TILE)
            dh[s, at, cols] = high
            dl[s, at, cols] = (value - high.astype(jnp.float32)).astype(jnp.bfloat16)
        for x in range(per):
            if x < h:
                at = slice(x * LANE, (x + 1) * LANE)
            elif x > h:
                at = slice((x + 2) * LANE, (x + 3) * LANE)
            else:
                continue
            blank = jnp.zeros((LANE, LANE), jnp.bfloat16)
            dh[s, at, cols] = blank
            dl[s, at, cols] = blank

    supers = (rows + 2 * HB) // sb
    window = sb + 2 * REACH

    def product(both, rest):
        return both[:, :traits] + both[:, traits:] + rest

    def apply():
        for s in range(supers):
            vec = ucat[REACH + s * sb : REACH + (s + 1) * sb, :]
            part = product(dot(dh[s], vec), dot(dl[s], vec[:, :traits]))
            at = s * sb
            if s == 0:
                y[at : at + window, :] = part
            else:
                y[at : at + 2 * REACH, :] += part[: 2 * REACH]
                y[at + 2 * REACH : at + window, :] = part[2 * REACH :]

    own = slice(HZ, HZ + rows)
    sums = []
    for step in range(ITERS):
        apply()
        if step == 0:
            for edge_rows, edge_cols, s, target, source in (
                (slice(0, LANE), slice(0, LANE), 0, 1, 0),
                (
                    slice(window - LANE, window),
                    slice(sb - LANE, sb),
                    supers - 1,
                    total_blocks - 2,
                    total_blocks - 1,
                ),
            ):
                vec = ucat[source * LANE : (source + 1) * LANE, :]
                part = product(
                    tdot(dh[s, edge_rows, edge_cols], vec),
                    tdot(dl[s, edge_rows, edge_cols], vec[:, :traits]),
                )
                y[target * LANE : (target + 1) * LANE, :] += part
        u_own = u_prev[own, :]
        y_own = y[own, :]
        w_out[step] = u_own + y_own
        sums.append(jnp.sum(u_own * u_own, axis=0, keepdims=True))
        sums.append(jnp.sum(u_own * y_own, axis=0, keepdims=True))
        if step < ITERS - 1:
            edge = (step + 1) * REACH
            here = slice(edge, total_blocks * LANE - edge)
            nxt = seen[here, :] * y[here, :]
            high = nxt.astype(jnp.bfloat16)
            u_prev[here, :] = nxt
            ucat[here, :traits] = high
            ucat[here, traits:] = (nxt - high.astype(jnp.float32)).astype(jnp.bfloat16)
    mom_out[...] = jnp.concatenate(
        sums + [jnp.zeros((8 - len(sums), traits), jnp.float32)], axis=0
    )


def krylov(ldt, z, obs, got_e, got_o, band_prev, paired):
    rows, traits = z.shape
    wide = rows + 2 * HB
    sb = 2 * LANE if wide % (2 * LANE) == 0 else LANE
    ext = rows + 2 * HZ
    supers = wide // sb
    return pl.pallas_call(
        functools.partial(krylov_kernel, band_prev.shape[0], sb, paired),
        in_specs=[SMEM] + [VMEM] * 5,
        out_specs=[VMEM, VMEM],
        out_shape=[
            jax.ShapeDtypeStruct((ITERS, rows, traits), jnp.float32),
            jax.ShapeDtypeStruct((8, traits), jnp.float32),
        ],
        scratch_shapes=[
            pltpu.VMEM((supers, sb + 2 * REACH, sb), jnp.bfloat16),
            pltpu.VMEM((supers, sb + 2 * REACH, sb), jnp.bfloat16),
            pltpu.VMEM((ext, 2 * traits), jnp.bfloat16),
            pltpu.VMEM((ext, traits), jnp.float32),
            pltpu.VMEM((ext, traits), jnp.float32),
            pltpu.VMEM((ext, traits), jnp.float32),
        ],
        compiler_params=params(28),
        cost_estimate=pl.CostEstimate(
            flops=ITERS * 6 * ext * SPAN * TILE * traits, bytes_accessed=ldt.size * 4, transcendentals=0
        ),
        name="krylov",
    )(band_prev, ldt, z, obs, got_e, got_o)


def solve(w, mom, out):
    m = [mom[i : i + 1, :] for i in range(2 * ITERS)]
    shift = 1.0 + RIDGE
    h = [shift * m[i] + m[i + 1] for i in range(2 * ITERS - 1)]
    d0 = h[0]
    l10 = h[1] / d0
    l20 = h[2] / d0
    d1 = h[2] - l10 * h[1]
    t12 = h[3] - l20 * h[1]
    ok1 = d1 > TINY * h[2]
    r1 = jnp.where(ok1, 1.0 / jnp.where(ok1, d1, 1.0), 0.0)
    l21 = t12 * r1
    d2 = h[4] - l20 * h[2] - l21 * t12
    ok2 = ok1 & (d2 > TINY * h[4])
    r2 = jnp.where(ok2, 1.0 / jnp.where(ok2, d2, 1.0), 0.0)
    z0 = m[0]
    z1 = m[1] - l10 * z0
    z2 = m[2] - l20 * z0 - l21 * z1
    c2 = z2 * r2
    c1 = z1 * r1 - l21 * c2
    c0 = z0 / d0 - l10 * c1 - l20 * c2
    out[...] = c0 * w[0] + c1 * w[1] + c2 * w[2]


def packed(z, ldt, obs):
    z = jnp.pad(z, ((0, 0), (0, LANE - z.shape[1])))
    obs = obs.astype(jnp.float32)
    parts = [z]
    parts += [ldt[:, i : i + LANE] for i in range(0, ldt.shape[1], LANE)]
    parts += [obs[:, i : i + LANE] for i in range(0, obs.shape[1], LANE)]
    height = sum(p.shape[0] for p in parts)
    parts.append(jnp.zeros((-height % 16, LANE), jnp.float32))
    return jnp.concatenate(parts, axis=0)


def halos(z, ldt, obs, axis):
    count = lax.axis_size(axis)
    rows = z.shape[0]

    def shifted(value, by):
        pairs = [(i, i + by) for i in range(count) if 0 <= i + by < count]
        return lax.ppermute(value, axis, pairs)

    def gather(value, width, dim):
        lefts, rights = [], []
        hop, have = 1, 0
        while have < width:
            take = min(rows, width - have)
            lefts.insert(0, shifted(lax.slice_in_dim(value, rows - take, rows, axis=dim), hop))
            rights.append(shifted(lax.slice_in_dim(value, 0, take, axis=dim), -hop))
            have += take
            hop += 1
        return jnp.concatenate(lefts, dim), jnp.concatenate(rights, dim)

    zs = gather(z, HZ, 0)
    lds = gather(ldt, HB, 1)
    seens = gather(obs, HZ, 1)
    return packed(zs[0], lds[0], seens[0]), packed(zs[1], lds[1], seens[1])


def local(dosage, allele_mean, snp_scale, band_next, ld_prev, band_prev, zscores, observed):
    samples, cols = dosage.shape
    rows = ld_prev.shape[0]
    n_smp = lax.axis_size("smp")
    ldt = ld_prev.T
    obs = observed.T
    line = ("snp", "pair")
    paired = rows >= HZ

    sent = pack(dosage, zscores, ldt, obs, paired)
    dos_e = exchange(sent[0], line, 0)
    dos_o = exchange(sent[1], line, 1)
    if paired:
        got_e = exchange(sent[2], ("smp",), 0)
        got_o = exchange(sent[3], ("smp",), 1)
    else:
        got_o, got_e = halos(zscores, ldt, obs, "smp")

    parts = cols // QW
    rot = parts == n_smp == 4 and zscores.shape[1] == LANE
    inv = 1.0 / (samples if rot else samples * n_smp)
    mean = allele_mean.reshape(-1, LANE)
    scale = snp_scale.reshape(-1, LANE)
    blocks = gram_parts(dosage, mean, scale, rot, inv)
    blocks = cross_parts(sent[0], sent[1], dos_e, dos_o, mean, scale, blocks, cols, rot, inv)
    if rot:

        def swap(value, by):
            return lax.ppermute(value, "smp", [(i, i ^ by) for i in range(n_smp)])

        got = [swap(blocks[by], by) for by in (1, 3, 2)]
    w, mom = krylov(ldt, zscores, obs, got_e, got_o, band_prev, paired)
    if rot:
        mine = total_of(blocks[0], got, mom)
        ring = [swap(mine, by) if by else mine for by in RING]
        moms = []
    else:
        ring = list(lax.psum(tuple(blocks), "smp"))
        moms = [lax.psum(mom, "smp")]
    ldn, imputed = final(ring, moms, w, band_next, cols, rot)
    return ldn.T, imputed


def solution(mesh):
    return jax.shard_map(
        local,
        mesh=mesh,
        in_specs=(
            P(("grp", "smp"), ("snp", "pair")),
            P("grp"),
            P("grp"),
            P("grp"),
            P(("grp", "smp"), None),
            P("grp"),
            P(("grp", "smp"), ("snp", "pair")),
            P(("grp", "smp"), ("snp", "pair")),
        ),
        out_specs=(P(("grp", "snp", "pair"), None), P(("grp", "smp"), ("snp", "pair"))),
        check_vma=False,
    )
```

```python
import functools
import jax
import jax.numpy as jnp
from jax import lax
from jax.experimental import pallas as pl
from jax.experimental.pallas import tpu as pltpu
from jax.sharding import PartitionSpec as P

TILE = 64
BMAX = 2
TBLK = 64
ITERS = 3
RIDGE = 1.0
SPAN = 2 * BMAX + 1
REACH = TILE * BMAX
LANE = 128
QW = 256
HZ = ITERS * REACH
HB = (ITERS - 1) * REACH
TINY = 1e-6
VMEM = pl.BlockSpec(memory_space=pltpu.VMEM)
SMEM = pl.BlockSpec(memory_space=pltpu.SMEM)


def params(mib):
    return pltpu.CompilerParams(vmem_limit_bytes=mib * 1024 * 1024)


def mask_rows(band_ref, first_tile, total):
    def width(t):
        inside = (t >= 0) & (t < total)
        return jnp.where(inside, band_ref[jnp.clip(t, 0, total - 1)], 0)

    widths = [width(first_tile + d) for d in range(-BMAX, BMAX + 2)]
    low = lax.broadcasted_iota(jnp.int32, (1, LANE), 1) < TILE
    rows = []
    for q in range(-BMAX, BMAX + 1):
        flags = [
            (abs(q) <= jnp.minimum(widths[BMAX + t], widths[BMAX + t + q])).astype(jnp.float32)
            for t in range(2)
        ]
        rows.append(jnp.where(low, flags[0], flags[1]))
    return rows


def low_lanes(shape):
    return lax.broadcasted_iota(jnp.int32, shape, 1) < TILE


def tdot(left, right):
    return lax.dot_general(
        left, right, (((0,), (0,)), ((), ())), preferred_element_type=jnp.float32
    )


def dot(left, right):
    return lax.dot_general(
        left, right, (((1,), (0,)), ((), ())), preferred_element_type=jnp.float32
    )


LEVELS = 32000.0
Z_LARGEST = 22.0
Z_ROOTS = 2
LARGEST = 36.0


def encode(value, largest=LARGEST, roots=3):
    size = jnp.minimum(jnp.abs(value) * (1.0 / largest), 1.0) + 1e-30
    for _ in range(roots):
        size = size * lax.rsqrt(size)
    code = size * LEVELS + 0.5
    return to_code(jnp.where(value < 0, -code, code))


def decode(code, largest=LARGEST, roots=3):
    value = from_code(code)
    size = value * (1.0 / LEVELS)
    for _ in range(roots):
        size = size * size
    size = size * largest
    return jnp.where(value < 0, -size, size)


def encode_exact(value):
    size = jnp.maximum(jnp.abs(value), 1e-30)
    power = jnp.clip(jnp.floor(jnp.log2(size)), -100.0, 120.0)
    scaled = value * jnp.exp2(-power) * 2.0**13
    high = jnp.round(scaled)
    low = jnp.round((scaled - high) * 2.0**14)
    return power, high, low


def decode_exact(power, high, low):
    return (high * 2.0**-13 + low * 2.0**-27) * jnp.exp2(power)


def to_code(value):
    return value.astype(jnp.int32).astype(jnp.int16)


def from_code(code):
    return code.astype(jnp.int32).astype(jnp.float32)


def line_index(axes):
    place = lax.axis_index(axes[0])
    for axis in axes[1:]:
        place = place * lax.axis_size(axis) + lax.axis_index(axis)
    return place


def in_hbm(value):
    return pltpu.with_memory_space_constraint(value, pltpu.HBM)


def halo_height(nb):
    height = HZ + HB // LANE * SPAN * TILE + HZ // LANE * nb
    return height + -height % 16


def pack_kernel(dos, z, ldt, obs, dos_e, dos_o, *rest):
    cols = dos.shape[1]
    rows = z.shape[0]
    sem = rest[-1]
    copies = []

    def start(source, target):
        copy = pltpu.make_async_copy(source, target, sem.at[len(copies)])
        copy.start()
        copies.append(copy)

    even = lax.rem(line_index(("snp", "pair")), 2) == 0
    to_e = pl.multiple_of(jnp.where(even, cols - LANE, 0), LANE)
    to_o = pl.multiple_of(jnp.where(even, 0, cols - LANE), LANE)
    halo = ()
    if len(rest) > 1:
        halo, (zs, lds, flags) = rest[:2], rest[2:5]
        even = lax.rem(lax.axis_index("smp"), 2) == 0
        for i, last in enumerate((even, jnp.logical_not(even))):
            row = pl.multiple_of(jnp.where(last, rows - HZ, 0), LANE)
            col = pl.multiple_of(jnp.where(last, rows - HB, 0), LANE)
            start(z.at[pl.ds(row, HZ), :], zs.at[i])
            start(ldt.at[:, pl.ds(col, HB)], lds.at[i])
            start(obs.at[:, pl.ds(row, HZ)], flags.at[i])
    start(dos.at[:, pl.ds(to_e, LANE)], dos_e)
    start(dos.at[:, pl.ds(to_o, LANE)], dos_o)
    for i, out in enumerate(halo):
        nb = obs.shape[0]
        for copy in copies[3 * i : 3 * i + 3]:
            copy.wait()
        out[0:HZ, : z.shape[1]] = encode(zs[i], Z_LARGEST, Z_ROOTS)
        base = HZ
        for j in range(HB // LANE):
            out[base : base + SPAN * TILE, :] = to_code(
                jnp.round(lds[i, :, j * LANE : (j + 1) * LANE] * LEVELS)
            )
            base += SPAN * TILE
        bits = [flags[i, :, j * LANE : (j + 1) * LANE] for j in range(HZ // LANE)]
        blank = out.shape[0] - base - nb * len(bits)
        bits.append(jnp.zeros((blank, LANE), jnp.int32))
        out[base:, :] = jnp.concatenate(bits, axis=0).astype(jnp.int16)
    for copy in copies[3 * len(halo) :]:
        copy.wait()


def pack(dosage, z, ldt, obs, with_halo):
    samples = dosage.shape[0]
    shapes = [jax.ShapeDtypeStruct((samples, LANE), dosage.dtype)] * 2
    copies = 2
    scratch = []
    if with_halo:
        shapes += [jax.ShapeDtypeStruct((halo_height(obs.shape[0]), LANE), jnp.int16)] * 2
        copies += 6
        scratch = [
            pltpu.VMEM((2, HZ, z.shape[1]), z.dtype),
            pltpu.VMEM((2, SPAN * TILE, HB), ldt.dtype),
            pltpu.VMEM((2, obs.shape[0], HZ), obs.dtype),
        ]
    far = pl.BlockSpec(memory_space=pltpu.HBM)
    return pl.pallas_call(
        pack_kernel,
        in_specs=[far] * 4,
        out_specs=[VMEM] * len(shapes),
        out_shape=shapes,
        scratch_shapes=scratch + [pltpu.SemaphoreType.DMA((copies,))],
        compiler_params=params(8),
        name="pack",
    )(in_hbm(dosage), in_hbm(z), in_hbm(ldt), in_hbm(obs))


def exchange(value, axes, phase):
    count = 1
    for axis in axes:
        count *= lax.axis_size(axis)
    if phase == 0 and lax.axis_size(axes[-1]) == 2 and len(axes) > 1:
        return lax.ppermute(value, axes[-1], [(0, 1), (1, 0)])
    pairs = []
    for i in range(phase, count - 1, 2):
        pairs += [(i, i + 1), (i + 1, i)]
    return lax.ppermute(value, axes, pairs)


DIAG = TILE // 2
RING = (0, 2, 3, 1)
NEAR = DIAG + BMAX * TILE


def quarter_at(step, first, parts):
    return jnp.bitwise_xor(step, first)


def tail_rows(parts):
    return TILE // parts


def standard(values, mean, scale, block):
    row = jnp.clip(block, 0, mean.shape[0] - 1)
    m = mean[pl.ds(row, 1), :]
    s = scale[pl.ds(row, 1), :]
    return ((values.astype(jnp.float32) - m) * s).astype(jnp.bfloat16)


def gram_kernel(parts, rot, inv, dos, mean, scale, *rest):
    outs = rest[:parts]
    raw, normed, sem = rest[parts:]
    blocks = QW // LANE
    samples, cols = dos.shape
    base = line_index(("snp", "pair")) * (cols // LANE)
    first = lax.axis_index("smp") if rot else 0

    def quarter_of(g):
        return lax.rem(g + first, parts)

    def fetch(g):
        at = pl.multiple_of(quarter_of(g) * QW, QW)
        return pltpu.make_async_copy(dos.at[:, pl.ds(at, QW)], raw.at[g], sem.at[g])

    for g in range(parts):
        fetch(g).start()

    def settle(g):
        fetch(g).wait()
        block = quarter_of(g) * blocks
        for b in range(blocks):
            at = pl.multiple_of((block + b) * LANE, LANE)
            normed[:, pl.ds(at, LANE)] = standard(
                raw[g, :, b * LANE : (b + 1) * LANE], mean, scale, base + block + b
            )

    normed[:, cols:] = jnp.zeros((samples, LANE), jnp.bfloat16)
    settle(0)
    rows = (BMAX + 1) * TILE
    tail = tail_rows(parts)
    low = low_lanes((rows, LANE))
    sub = lax.broadcasted_iota(jnp.int32, (TILE, LANE), 0)
    lane = lax.broadcasted_iota(jnp.int32, (TILE, LANE), 1)
    spot = lax.broadcasted_iota(jnp.int32, (tail, LANE), 0)

    def step(g, _):
        @pl.when(g < parts - 1)
        def _():
            settle(jnp.minimum(g + 1, parts - 1))

        at = pl.multiple_of(quarter_of(g) * QW, QW)
        full = tdot(normed[:, pl.ds(at, QW + LANE)], normed[:, pl.ds(at, QW)])
        pieces = []
        for b in range(blocks):
            cut = slice(b * LANE, (b + 1) * LANE)
            pieces.append(
                inv
                * jnp.where(
                    low,
                    full[b * LANE : b * LANE + rows, cut],
                    full[b * LANE + TILE : b * LANE + TILE + rows, cut],
                )
            )
        folded = [
            jnp.where(sub <= lane, p[:TILE], pltpu.roll(p[:TILE], TILE, axis=1)) for p in pieces
        ]
        folded = jnp.where(lane < TILE, folded[0], pltpu.roll(folded[1], TILE, axis=1))
        diagonals = [
            jnp.sum(jnp.where(sub == lane - TILE, p[:TILE], 0.0), axis=0, keepdims=True)
            for p in pieces
        ]
        ends = jnp.where(spot == 0, diagonals[0], jnp.where(spot == 1, diagonals[1], 0.0))
        slot = quarter_at(quarter_of(g), first, parts)
        for i in range(parts):

            @pl.when(slot == i)
            def _(i=i):
                send = encode if rot and i > 0 else (lambda v: v)
                for b in range(blocks):
                    cut = slice(b * LANE, (b + 1) * LANE)
                    outs[i][:DIAG, cut] = send(folded[b * DIAG : (b + 1) * DIAG])
                    outs[i][DIAG:NEAR, cut] = send(pieces[b][TILE:])
                outs[i][NEAR:, :LANE] = jnp.zeros((tail, LANE), outs[i].dtype)
                outs[i][NEAR:, LANE:] = send(ends)

        return 0

    lax.fori_loop(0, parts, step, 0)


def gram_parts(dosage, mean, scale, rot, inv):
    samples, cols = dosage.shape
    parts = cols // QW
    rows = NEAR + tail_rows(parts)
    kinds = [jnp.float32] + [jnp.int16 if rot else jnp.float32] * (parts - 1)
    return pl.pallas_call(
        functools.partial(gram_kernel, parts, rot, inv),
        in_specs=[pl.BlockSpec(memory_space=pltpu.HBM)] + [VMEM] * 2,
        out_specs=[VMEM] * parts,
        out_shape=[jax.ShapeDtypeStruct((rows, QW), kind) for kind in kinds],
        scratch_shapes=[
            pltpu.VMEM((parts, samples, QW), jnp.bfloat16),
            pltpu.VMEM((samples, cols + LANE), jnp.bfloat16),
            pltpu.SemaphoreType.DMA((parts,)),
        ],
        compiler_params=params(24),
        cost_estimate=pl.CostEstimate(
            flops=2 * samples * cols * (QW + LANE), bytes_accessed=dosage.size * 4, transcendentals=0
        ),
        name="gram",
    )(in_hbm(dosage), mean, scale)


def cross_kernel(parts, rot, inv, cols, sent_e, sent_o, got_o, got_e, mean, scale, *rest):
    ins, outs, (zero, one) = rest[:parts], rest[parts : 2 * parts], rest[-2:]
    blocks = QW // LANE
    tail = tail_rows(parts)
    place = line_index(("snp", "pair"))
    base = place * (cols // LANE)
    end = base + cols // LANE
    even = lax.rem(place, 2) == 0
    pick = lambda one, two: jnp.where(even, one[...], two[...])
    right = standard(pick(got_e, got_o), mean, scale, end)
    left = standard(pick(got_o, got_e), mean, scale, base - 1)
    last = standard(pick(sent_e, sent_o), mean, scale, end - 1)
    head = standard(pick(sent_o, sent_e), mean, scale, base)
    ahead = inv * tdot(right, last)
    behind = inv * tdot(left, head)
    low = low_lanes((TILE, LANE))
    turned = pltpu.roll(behind[TILE:], TILE, axis=1)
    zero[...] = jnp.where(low, behind[:TILE], turned)
    one[...] = turned
    far = slice((blocks - 1) * LANE, blocks * LANE)
    first = lax.axis_index("smp") if rot else 0
    for i in range(parts):
        send = encode if rot and i > 0 else (lambda v: v)
        wide = (lambda v: v.astype(jnp.int32)) if rot and i > 0 else (lambda v: v)
        kind = outs[i].dtype
        outs[i][:NEAR, :] = ins[i][:NEAR, :]
        quarter = quarter_at(i, first, parts)
        share = pl.ds(pl.multiple_of(quarter * tail, 8), tail)
        outs[i][NEAR:, :LANE] = send(zero[share, :])
        outs[i][NEAR:, LANE:] = jnp.where(
            low_lanes((tail, LANE)), wide(send(one[share, :])), wide(ins[i][NEAR:, LANE:])
        ).astype(kind)

        @pl.when(quarter == parts - 1)
        def _(i=i, send=send, wide=wide, kind=kind):
            next_one = slice(DIAG, DIAG + TILE)
            outs[i][next_one, far] = jnp.where(
                low, wide(ins[i][next_one, far]), wide(send(ahead[:TILE]))
            ).astype(kind)
            outs[i][DIAG + TILE : NEAR, far] = send(jnp.where(low, ahead[:TILE], ahead[TILE:]))


def cross_parts(sent_e, sent_o, got_e, got_o, mean, scale, blocks, cols, rot, inv):
    parts = len(blocks)
    height = NEAR + tail_rows(parts)
    return pl.pallas_call(
        functools.partial(cross_kernel, parts, rot, inv, cols),
        in_specs=[VMEM] * (6 + parts),
        out_specs=[VMEM] * parts,
        out_shape=[jax.ShapeDtypeStruct((height, QW), b.dtype) for b in blocks],
        scratch_shapes=[pltpu.VMEM((TILE, LANE), jnp.float32)] * 2,
        compiler_params=params(12),
        name="cross",
    )(sent_e, sent_o, got_o, got_e, mean, scale, *blocks)


def total_kernel(count, own, *rest):
    others, mom, out = rest[:-2], rest[-2], rest[-1]
    height = own.shape[0]
    total = own[...]
    for other in others:
        total = total + decode(other[...])
    out[0:height, :] = encode(total * (1.0 / count))
    power, high, low = encode_exact(mom[...])
    lanes = mom.shape[1]
    top = jnp.concatenate([power, low], axis=1)
    bottom = jnp.concatenate([high, jnp.zeros_like(low)], axis=1)
    out[height : height + 16, :] = to_code(jnp.concatenate([top, bottom], axis=0))


def total_of(own, others, mom):
    count = 1 + len(others)
    return pl.pallas_call(
        functools.partial(total_kernel, count),
        in_specs=[VMEM] * (count + 1),
        out_specs=VMEM,
        out_shape=jax.ShapeDtypeStruct((own.shape[0] + 16, own.shape[1]), jnp.int16),
        compiler_params=params(8),
        name="total",
    )(own, *others, mom)


def final_kernel(parts, rot, moments, tile_total, band, w, *rest):
    ring = rest[:parts]
    moms = rest[parts : parts + moments]
    out_far, imputed_far, held, out, imputed, sem = rest[parts + moments :]
    blocks = QW // LANE
    tail = tail_rows(parts)
    height = NEAR + tail
    low = low_lanes((TILE, LANE))
    sub = lax.broadcasted_iota(jnp.int32, (TILE, LANE), 0)
    lane = lax.broadcasted_iota(jnp.int32, (TILE, LANE), 1)
    cols = out.shape[1]
    first_tile = line_index(("snp", "pair")) * (cols // TILE)
    copies = []

    def ship(source, target):
        copy = pltpu.make_async_copy(source, target, sem.at[len(copies)])
        copy.start()
        copies.append(copy)

    def swap(value):
        return pltpu.roll(value, TILE, axis=1)

    if rot:
        k = lax.axis_index("smp")
        total = None
        for piece, by in zip(ring, RING):
            held[quarter_at(by, k, parts)] = decode(piece[0:height, :])
            code = from_code(piece[height : height + 16, :])
            lanes = code.shape[1] // 2
            mom = decode_exact(code[:8, :lanes], code[8:, :lanes], code[:8, lanes:])
            total = mom if total is None else total + mom
    else:
        for by in range(parts):
            held[by] = ring[by][...]
        total = moms[0][...]
    solve(w, total, imputed)
    ship(imputed, imputed_far)
    for quarter in range(parts):
        fold = jnp.concatenate(
            [held[quarter, :DIAG, b * LANE : (b + 1) * LANE] for b in range(blocks)], axis=0
        )
        mirror = jnp.concatenate([fold, swap(fold)], axis=0).T[:TILE]
        for b in range(blocks):
            a = quarter * blocks + b
            cut = slice(b * LANE, (b + 1) * LANE)
            cols_here = slice(a * LANE, (a + 1) * LANE)
            masks = mask_rows(band, first_tile + 2 * a, tile_total)
            here, there = (fold, mirror) if b == 0 else (swap(fold), swap(mirror))
            second = jnp.where(
                sub == lane - TILE,
                held[quarter, NEAR + b : NEAR + b + 1, LANE : 2 * LANE],
                swap(jnp.where(lane < sub, here, there)),
            )
            centre = jnp.where(low, jnp.where(sub <= lane, here, there), second)
            out[BMAX * TILE : (BMAX + 1) * TILE, cols_here] = centre * masks[BMAX]
            for q in range(1, BMAX + 1):
                out[(BMAX + q) * TILE : (BMAX + q + 1) * TILE, cols_here] = (
                    held[quarter, DIAG + (q - 1) * TILE : DIAG + q * TILE, cut] * masks[BMAX + q]
                )
            turned = held[quarter, DIAG:NEAR, cut].T
            rolled = swap(turned)
            if a == 0:
                cross = [
                    jnp.concatenate(
                        [held[j, NEAR:height, c * LANE : (c + 1) * LANE] for j in range(parts)],
                        axis=0,
                    )
                    for c in range(2)
                ]
                one_low, two_low, two_high = swap(cross[0]), cross[0], swap(cross[1])
            else:
                one_low, two_low, two_high = (
                    last_turned[TILE:], last_rolled[:TILE], last_turned[TILE:]
                )
            out[TILE : 2 * TILE, cols_here] = jnp.where(low, one_low, rolled[:TILE]) * masks[1]
            out[0:TILE, cols_here] = jnp.where(low, two_low, two_high) * masks[0]
            last_turned, last_rolled = turned, rolled
        block = slice(quarter * QW, (quarter + 1) * QW)
        ship(out.at[:, block], out_far.at[:, block])
    for copy in copies:
        copy.wait()


def final(ring, moms, w, band_next, cols, rot):
    parts = len(ring)
    shapes = [
        jax.ShapeDtypeStruct((SPAN * TILE, cols), jnp.float32),
        jax.ShapeDtypeStruct(w.shape[1:], jnp.float32),
    ]
    return pl.pallas_call(
        functools.partial(final_kernel, parts, rot, len(moms), band_next.shape[0]),
        in_specs=[SMEM] + [VMEM] * (1 + parts + len(moms)),
        out_specs=[pl.BlockSpec(memory_space=pltpu.HBM)] * 2,
        out_shape=shapes,
        scratch_shapes=[
            pltpu.VMEM((parts, NEAR + tail_rows(parts), QW), jnp.float32),
            pltpu.VMEM(shapes[0].shape, jnp.float32),
            pltpu.VMEM(shapes[1].shape, jnp.float32),
            pltpu.SemaphoreType.DMA((parts + 1,)),
        ],
        compiler_params=params(16),
        name="final",
    )(band_next, w, *ring, *moms)


class Side:
    def __init__(self, flag, one, two):
        self.flag, self.one, self.two = flag, one, two

    def pick(self, at, convert):
        if self.flag is None:
            return self.one[at]
        return jnp.where(self.flag, convert(self.one[at]), convert(self.two[at]))

    def vector(self, at):
        return self.pick(at, lambda code: decode(code, Z_LARGEST, Z_ROOTS))

    def band(self, at):
        return self.pick(at, lambda code: from_code(code) * (1.0 / LEVELS))

    def flags(self, at):
        return self.pick(at, from_code)


def krylov_kernel(
    tile_total, sb, paired, band, ldt, z, obs, got_o, got_e, w_out, mom_out,
    dh, dl, ucat, seen, u_prev, y
):
    rows = ldt.shape[1]
    traits = z.shape[1]
    own_blocks = rows // LANE
    zb = HZ // LANE
    bb = HB // LANE
    first_tile = lax.axis_index("smp") * (rows // TILE)
    even = lax.rem(lax.axis_index("smp"), 2) == 0 if paired else None
    halo_r = Side(even, got_e, got_o)
    halo_l = Side(even, got_o, got_e)
    nb = obs.shape[0]
    ld_rows = SPAN * TILE
    total_blocks = own_blocks + 2 * zb

    tail = (slice(HZ + bb * ld_rows, got_e.shape[0]), slice(None))
    flags_l, flags_r = halo_l.flags(tail), halo_r.flags(tail)

    for c in range(total_blocks):
        if c < zb:
            vec = halo_l.vector((slice(c * LANE, (c + 1) * LANE), slice(0, traits)))
            flags = [flags_l[c * nb + i : c * nb + i + 1, :] for i in range(nb)]
        elif c < zb + own_blocks:
            o = c - zb
            vec = z[o * LANE : (o + 1) * LANE, :]
            flags = [
                obs[i : i + 1, o * LANE : (o + 1) * LANE].astype(jnp.float32) for i in range(nb)
            ]
        else:
            o = c - zb - own_blocks
            vec = halo_r.vector((slice(o * LANE, (o + 1) * LANE), slice(0, traits)))
            flags = [flags_r[o * nb + i : o * nb + i + 1, :] for i in range(nb)]
        wide = jnp.concatenate(
            [jnp.broadcast_to(f, (TBLK, LANE)) for f in flags], axis=0
        )
        mask = wide.T
        here = slice(c * LANE, (c + 1) * LANE)
        seen[here, :] = mask
        start = mask * vec
        high = start.astype(jnp.bfloat16)
        u_prev[here, :] = start
        ucat[here, :traits] = high
        ucat[here, traits:] = (start - high.astype(jnp.float32)).astype(jnp.bfloat16)

    per = sb // LANE
    low = low_lanes((TILE, LANE))
    sub = lax.broadcasted_iota(jnp.int32, (TILE, LANE), 0)
    lane = lax.broadcasted_iota(jnp.int32, (TILE, LANE), 1)
    chunks = SPAN + 1
    for c in range(own_blocks + 2 * bb):
        if c < bb:
            full = halo_l.band((slice(HZ + c * ld_rows, HZ + (c + 1) * ld_rows), slice(None)))
            get = lambda q, full=full: full[q * TILE : (q + 1) * TILE]
        elif c < bb + own_blocks:
            get = lambda q, c=c: ldt[q * TILE : (q + 1) * TILE, (c - bb) * LANE : (c - bb + 1) * LANE]
        else:
            o = c - bb - own_blocks
            full = halo_r.band((slice(HZ + o * ld_rows, HZ + (o + 1) * ld_rows), slice(None)))
            get = lambda q, full=full: full[q * TILE : (q + 1) * TILE]
        masks = mask_rows(band, first_tile + 2 * (c - bb), tile_total)
        s, h = c // per, c % per
        cols = slice(h * LANE, (h + 1) * LANE)
        parts = [get(q) * masks[q] for q in range(SPAN)]
        zero = jnp.zeros((TILE, LANE), jnp.float32)
        for j in range(chunks):
            left = parts[j] if j < SPAN else zero
            right = parts[j - 1] if j >= 1 else zero
            value = jnp.where(low, left, right)
            if BMAX <= j < BMAX + 2:
                value = value - (sub + TILE * (j - BMAX) == lane).astype(jnp.float32)
            high = value.astype(jnp.bfloat16)
            at = slice(h * LANE + j * TILE, h * LANE + (j + 1) * TILE)
            dh[s, at, cols] = high
            dl[s, at, cols] = (value - high.astype(jnp.float32)).astype(jnp.bfloat16)
        for x in range(per):
            if x < h:
                at = slice(x * LANE, (x + 1) * LANE)
            elif x > h:
                at = slice((x + 2) * LANE, (x + 3) * LANE)
            else:
                continue
            blank = jnp.zeros((LANE, LANE), jnp.bfloat16)
            dh[s, at, cols] = blank
            dl[s, at, cols] = blank

    supers = (rows + 2 * HB) // sb
    window = sb + 2 * REACH

    def product(both, rest):
        return both[:, :traits] + both[:, traits:] + rest

    def apply():
        for s in range(supers):
            vec = ucat[REACH + s * sb : REACH + (s + 1) * sb, :]
            part = product(dot(dh[s], vec), dot(dl[s], vec[:, :traits]))
            at = s * sb
            if s == 0:
                y[at : at + window, :] = part
            else:
                y[at : at + 2 * REACH, :] += part[: 2 * REACH]
                y[at + 2 * REACH : at + window, :] = part[2 * REACH :]

    own = slice(HZ, HZ + rows)
    sums = []
    for step in range(ITERS):
        apply()
        if step == 0:
            for edge_rows, edge_cols, s, target, source in (
                (slice(0, LANE), slice(0, LANE), 0, 1, 0),
                (
                    slice(window - LANE, window),
                    slice(sb - LANE, sb),
                    supers - 1,
                    total_blocks - 2,
                    total_blocks - 1,
                ),
            ):
                vec = ucat[source * LANE : (source + 1) * LANE, :]
                part = product(
                    tdot(dh[s, edge_rows, edge_cols], vec),
                    tdot(dl[s, edge_rows, edge_cols], vec[:, :traits]),
                )
                y[target * LANE : (target + 1) * LANE, :] += part
        u_own = u_prev[own, :]
        y_own = y[own, :]
        w_out[step] = u_own + y_own
        sums.append(jnp.sum(u_own * u_own, axis=0, keepdims=True))
        sums.append(jnp.sum(u_own * y_own, axis=0, keepdims=True))
        if step < ITERS - 1:
            edge = (step + 1) * REACH
            here = slice(edge, total_blocks * LANE - edge)
            nxt = seen[here, :] * y[here, :]
            high = nxt.astype(jnp.bfloat16)
            u_prev[here, :] = nxt
            ucat[here, :traits] = high
            ucat[here, traits:] = (nxt - high.astype(jnp.float32)).astype(jnp.bfloat16)
    mom_out[...] = jnp.concatenate(
        sums + [jnp.zeros((8 - len(sums), traits), jnp.float32)], axis=0
    )


def krylov(ldt, z, obs, got_e, got_o, band_prev, paired):
    rows, traits = z.shape
    wide = rows + 2 * HB
    sb = 2 * LANE if wide % (2 * LANE) == 0 else LANE
    ext = rows + 2 * HZ
    supers = wide // sb
    return pl.pallas_call(
        functools.partial(krylov_kernel, band_prev.shape[0], sb, paired),
        in_specs=[SMEM] + [VMEM] * 5,
        out_specs=[VMEM, VMEM],
        out_shape=[
            jax.ShapeDtypeStruct((ITERS, rows, traits), jnp.float32),
            jax.ShapeDtypeStruct((8, traits), jnp.float32),
        ],
        scratch_shapes=[
            pltpu.VMEM((supers, sb + 2 * REACH, sb), jnp.bfloat16),
            pltpu.VMEM((supers, sb + 2 * REACH, sb), jnp.bfloat16),
            pltpu.VMEM((ext, 2 * traits), jnp.bfloat16),
            pltpu.VMEM((ext, traits), jnp.float32),
            pltpu.VMEM((ext, traits), jnp.float32),
            pltpu.VMEM((ext, traits), jnp.float32),
        ],
        compiler_params=params(28),
        cost_estimate=pl.CostEstimate(
            flops=ITERS * 6 * ext * SPAN * TILE * traits, bytes_accessed=ldt.size * 4, transcendentals=0
        ),
        name="krylov",
    )(band_prev, ldt, z, obs, got_o, got_e)


def solve(w, mom, out):
    m = [mom[i : i + 1, :] for i in range(2 * ITERS)]
    shift = 1.0 + RIDGE
    h = [shift * m[i] + m[i + 1] for i in range(2 * ITERS - 1)]
    d0 = h[0]
    l10 = h[1] / d0
    l20 = h[2] / d0
    d1 = h[2] - l10 * h[1]
    t12 = h[3] - l20 * h[1]
    ok1 = d1 > TINY * h[2]
    r1 = jnp.where(ok1, 1.0 / jnp.where(ok1, d1, 1.0), 0.0)
    l21 = t12 * r1
    d2 = h[4] - l20 * h[2] - l21 * t12
    ok2 = ok1 & (d2 > TINY * h[4])
    r2 = jnp.where(ok2, 1.0 / jnp.where(ok2, d2, 1.0), 0.0)
    z0 = m[0]
    z1 = m[1] - l10 * z0
    z2 = m[2] - l20 * z0 - l21 * z1
    c2 = z2 * r2
    c1 = z1 * r1 - l21 * c2
    c0 = z0 / d0 - l10 * c1 - l20 * c2
    out[...] = c0 * w[0] + c1 * w[1] + c2 * w[2]


def packed(z, ldt, obs):
    z = jnp.pad(z, ((0, 0), (0, LANE - z.shape[1])))
    obs = obs.astype(jnp.float32)
    parts = [z]
    parts += [ldt[:, i : i + LANE] for i in range(0, ldt.shape[1], LANE)]
    parts += [obs[:, i : i + LANE] for i in range(0, obs.shape[1], LANE)]
    height = sum(p.shape[0] for p in parts)
    parts.append(jnp.zeros((-height % 16, LANE), jnp.float32))
    return jnp.concatenate(parts, axis=0)


def halos(z, ldt, obs, axis):
    count = lax.axis_size(axis)
    rows = z.shape[0]

    def shifted(value, by):
        pairs = [(i, i + by) for i in range(count) if 0 <= i + by < count]
        return lax.ppermute(value, axis, pairs)

    def gather(value, width, dim):
        lefts, rights = [], []
        hop, have = 1, 0
        while have < width:
            take = min(rows, width - have)
            lefts.insert(0, shifted(lax.slice_in_dim(value, rows - take, rows, axis=dim), hop))
            rights.append(shifted(lax.slice_in_dim(value, 0, take, axis=dim), -hop))
            have += take
            hop += 1
        return jnp.concatenate(lefts, dim), jnp.concatenate(rights, dim)

    zs = gather(z, HZ, 0)
    lds = gather(ldt, HB, 1)
    seens = gather(obs, HZ, 1)
    return packed(zs[0], lds[0], seens[0]), packed(zs[1], lds[1], seens[1])


def local(dosage, allele_mean, snp_scale, band_next, ld_prev, band_prev, zscores, observed):
    samples, cols = dosage.shape
    rows = ld_prev.shape[0]
    n_smp = lax.axis_size("smp")
    ldt = ld_prev.T
    obs = observed.T
    line = ("snp", "pair")
    paired = rows >= HZ

    sent = pack(dosage, zscores, ldt, obs, paired)
    dos_o = exchange(sent[1], line, 1)
    dos_e = exchange(sent[0], line, 0)
    if paired:
        got_o = exchange(sent[3], ("smp",), 1)
        got_e = exchange(sent[2], ("smp",), 0)
    else:
        got_o, got_e = halos(zscores, ldt, obs, "smp")

    parts = cols // QW
    rot = parts == n_smp == 4 and zscores.shape[1] == LANE
    inv = 1.0 / (samples if rot else samples * n_smp)
    mean = allele_mean.reshape(-1, LANE)
    scale = snp_scale.reshape(-1, LANE)
    blocks = gram_parts(dosage, mean, scale, rot, inv)
    blocks = cross_parts(sent[0], sent[1], dos_e, dos_o, mean, scale, blocks, cols, rot, inv)
    if rot:

        def swap(value, by):
            return lax.ppermute(value, "smp", [(i, i ^ by) for i in range(n_smp)])

        got = [swap(blocks[by], by) for by in (1, 3, 2)]
    w, mom = krylov(ldt, zscores, obs, got_e, got_o, band_prev, paired)
    if rot:
        mine = total_of(blocks[0], got, mom)
        ring = [swap(mine, by) if by else mine for by in RING]
        moms = []
    else:
        ring = list(lax.psum(tuple(blocks), "smp"))
        moms = [lax.psum(mom, "smp")]
    ldn, imputed = final(ring, moms, w, band_next, cols, rot)
    return ldn.T, imputed


def solution(mesh):
    return jax.shard_map(
        local,
        mesh=mesh,
        in_specs=(
            P(("grp", "smp"), ("snp", "pair")),
            P("grp"),
            P("grp"),
            P("grp"),
            P(("grp", "smp"), None),
            P("grp"),
            P(("grp", "smp"), ("snp", "pair")),
            P(("grp", "smp"), ("snp", "pair")),
        ),
        out_specs=(P(("grp", "snp", "pair"), None), P(("grp", "smp"), ("snp", "pair"))),
        check_vma=False,
    )
```

```python
import functools
import jax
import jax.numpy as jnp
from jax import lax
from jax.experimental import pallas as pl
from jax.experimental.pallas import tpu as pltpu
from jax.sharding import PartitionSpec as P

TILE = 64
BMAX = 2
TBLK = 64
ITERS = 3
RIDGE = 1.0
SPAN = 2 * BMAX + 1
REACH = TILE * BMAX
LANE = 128
QW = 256
HZ = ITERS * REACH
HB = (ITERS - 1) * REACH
TINY = 1e-6
VMEM = pl.BlockSpec(memory_space=pltpu.VMEM)
SMEM = pl.BlockSpec(memory_space=pltpu.SMEM)


def params(mib):
    return pltpu.CompilerParams(vmem_limit_bytes=mib * 1024 * 1024)


def mask_rows(band_ref, first_tile, total):
    def width(t):
        inside = (t >= 0) & (t < total)
        return jnp.where(inside, band_ref[jnp.clip(t, 0, total - 1)], 0)

    widths = [width(first_tile + d) for d in range(-BMAX, BMAX + 2)]
    low = lax.broadcasted_iota(jnp.int32, (1, LANE), 1) < TILE
    rows = []
    for q in range(-BMAX, BMAX + 1):
        flags = [
            (abs(q) <= jnp.minimum(widths[BMAX + t], widths[BMAX + t + q])).astype(jnp.float32)
            for t in range(2)
        ]
        rows.append(jnp.where(low, flags[0], flags[1]))
    return rows


def low_lanes(shape):
    return lax.broadcasted_iota(jnp.int32, shape, 1) < TILE


def tdot(left, right):
    return lax.dot_general(
        left, right, (((0,), (0,)), ((), ())), preferred_element_type=jnp.float32
    )


def dot(left, right):
    return lax.dot_general(
        left, right, (((1,), (0,)), ((), ())), preferred_element_type=jnp.float32
    )


LEVELS = 32000.0
Z_LARGEST = 22.0
Z_ROOTS = 2
LARGEST = 36.0


def encode(value, largest=LARGEST, roots=3):
    size = jnp.minimum(jnp.abs(value) * (1.0 / largest), 1.0) + 1e-30
    for _ in range(roots):
        size = size * lax.rsqrt(size)
    code = size * LEVELS + 0.5
    return to_code(jnp.where(value < 0, -code, code))


def decode(code, largest=LARGEST, roots=3):
    value = from_code(code)
    size = value * (1.0 / LEVELS)
    for _ in range(roots):
        size = size * size
    size = size * largest
    return jnp.where(value < 0, -size, size)


def encode_exact(value):
    size = jnp.maximum(jnp.abs(value), 1e-30)
    power = jnp.clip(jnp.floor(jnp.log2(size)), -100.0, 120.0)
    scaled = value * jnp.exp2(-power) * 2.0**13
    high = jnp.round(scaled)
    low = jnp.round((scaled - high) * 2.0**14)
    return power, high, low


def decode_exact(power, high, low):
    return (high * 2.0**-13 + low * 2.0**-27) * jnp.exp2(power)


def to_code(value):
    return value.astype(jnp.int32).astype(jnp.int16)


def from_code(code):
    return code.astype(jnp.int32).astype(jnp.float32)


def line_index(axes):
    place = lax.axis_index(axes[0])
    for axis in axes[1:]:
        place = place * lax.axis_size(axis) + lax.axis_index(axis)
    return place


def in_hbm(value):
    return pltpu.with_memory_space_constraint(value, pltpu.HBM)


def halo_height(nb):
    height = HZ + HB // LANE * SPAN * TILE + HZ // LANE * nb
    return height + -height % 16


def pack_kernel(dos, z, ldt, obs, dos_e, dos_o, *rest):
    cols = dos.shape[1]
    rows = z.shape[0]
    sem = rest[-1]
    copies = []

    def start(source, target):
        copy = pltpu.make_async_copy(source, target, sem.at[len(copies)])
        copy.start()
        copies.append(copy)

    even = lax.rem(line_index(("snp", "pair")), 2) == 0
    to_e = pl.multiple_of(jnp.where(even, cols - LANE, 0), LANE)
    to_o = pl.multiple_of(jnp.where(even, 0, cols - LANE), LANE)
    halo = ()
    if len(rest) > 1:
        halo, (zs, lds, flags) = rest[:2], rest[2:5]
        even = lax.rem(lax.axis_index("smp"), 2) == 0
        for i, last in enumerate((even, jnp.logical_not(even))):
            row = pl.multiple_of(jnp.where(last, rows - HZ, 0), LANE)
            col = pl.multiple_of(jnp.where(last, rows - HB, 0), LANE)
            start(z.at[pl.ds(row, HZ), :], zs.at[i])
            start(ldt.at[:, pl.ds(col, HB)], lds.at[i])
            start(obs.at[:, pl.ds(row, HZ)], flags.at[i])
    start(dos.at[:, pl.ds(to_e, LANE)], dos_e)
    start(dos.at[:, pl.ds(to_o, LANE)], dos_o)
    for i, out in enumerate(halo):
        nb = obs.shape[0]
        for copy in copies[3 * i : 3 * i + 3]:
            copy.wait()
        out[0:HZ, : z.shape[1]] = encode(zs[i], Z_LARGEST, Z_ROOTS)
        base = HZ
        for j in range(HB // LANE):
            out[base : base + SPAN * TILE, :] = to_code(
                jnp.round(lds[i, :, j * LANE : (j + 1) * LANE] * LEVELS)
            )
            base += SPAN * TILE
        bits = [flags[i, :, j * LANE : (j + 1) * LANE] for j in range(HZ // LANE)]
        blank = out.shape[0] - base - nb * len(bits)
        bits.append(jnp.zeros((blank, LANE), jnp.int32))
        out[base:, :] = jnp.concatenate(bits, axis=0).astype(jnp.int16)
    for copy in copies[3 * len(halo) :]:
        copy.wait()


def pack(dosage, z, ldt, obs, with_halo):
    samples = dosage.shape[0]
    shapes = [jax.ShapeDtypeStruct((samples, LANE), dosage.dtype)] * 2
    copies = 2
    scratch = []
    if with_halo:
        shapes += [jax.ShapeDtypeStruct((halo_height(obs.shape[0]), LANE), jnp.int16)] * 2
        copies += 6
        scratch = [
            pltpu.VMEM((2, HZ, z.shape[1]), z.dtype),
            pltpu.VMEM((2, SPAN * TILE, HB), ldt.dtype),
            pltpu.VMEM((2, obs.shape[0], HZ), obs.dtype),
        ]
    far = pl.BlockSpec(memory_space=pltpu.HBM)
    return pl.pallas_call(
        pack_kernel,
        in_specs=[far] * 4,
        out_specs=[VMEM] * len(shapes),
        out_shape=shapes,
        scratch_shapes=scratch + [pltpu.SemaphoreType.DMA((copies,))],
        compiler_params=params(8),
        name="pack",
    )(in_hbm(dosage), in_hbm(z), in_hbm(ldt), in_hbm(obs))


def exchange(value, axes, phase):
    count = 1
    for axis in axes:
        count *= lax.axis_size(axis)
    if phase == 0 and lax.axis_size(axes[-1]) == 2 and len(axes) > 1:
        return lax.ppermute(value, axes[-1], [(0, 1), (1, 0)])
    pairs = []
    for i in range(phase, count - 1, 2):
        pairs += [(i, i + 1), (i + 1, i)]
    return lax.ppermute(value, axes, pairs)


DIAG = TILE // 2
RING = (0, 2, 3, 1)
NEAR = DIAG + BMAX * TILE


def quarter_at(step, first, parts):
    if isinstance(first, int):
        return (step + first) % parts
    return lax.rem(step + first, parts)


def tail_rows(parts):
    return TILE // parts


def standard(values, mean, scale, block):
    row = jnp.clip(block, 0, mean.shape[0] - 1)
    m = mean[pl.ds(row, 1), :]
    s = scale[pl.ds(row, 1), :]
    return ((values.astype(jnp.float32) - m) * s).astype(jnp.bfloat16)


def gram_kernel(parts, rot, inv, dos, mean, scale, *rest):
    outs, (head, last), normed = rest[:parts], rest[parts : parts + 2], rest[parts + 2]
    blocks = QW // LANE
    samples, cols = dos.shape
    base = line_index(("snp", "pair")) * (cols // LANE)
    first = lax.axis_index("smp") if rot else 0
    tail = tail_rows(parts)
    sub = lax.broadcasted_iota(jnp.int32, (TILE, LANE), 0)
    lane = lax.broadcasted_iota(jnp.int32, (TILE, LANE), 1)
    spot = lax.broadcasted_iota(jnp.int32, (tail, LANE), 0)
    low = low_lanes(((BMAX + 1) * TILE, LANE))

    def settle(g):
        block = quarter_at(g, first, parts) * blocks
        for b in range(blocks):
            at = block + b
            if rot:
                at = pl.multiple_of(at * LANE, LANE)
                values = dos[:, pl.ds(at, LANE)]
            else:
                values = dos[:, at * LANE : (at + 1) * LANE]
            normed[g, :, b * LANE : (b + 1) * LANE] = standard(
                values, mean, scale, base + block + b
            )

    settle(0)
    for g in range(parts):
        if g + 1 < parts:
            settle(g + 1)
        own = normed[g]
        top = tdot(own, own)
        bottom = tdot(normed[(g + 1) % parts, :, :LANE], own)
        pieces = []
        for b in range(blocks):
            cut = slice(b * LANE, (b + 1) * LANE)
            full = jnp.concatenate([top[b * LANE :, cut], bottom[:, cut]], axis=0)
            pieces.append(
                inv * jnp.where(low, full[: low.shape[0]], full[TILE : TILE + low.shape[0]])
            )
        folded = [
            jnp.where(sub <= lane, p[:TILE], pltpu.roll(p[:TILE], TILE, axis=1)) for p in pieces
        ]
        folded = jnp.where(lane < TILE, folded[0], pltpu.roll(folded[1], TILE, axis=1))
        diagonals = [
            jnp.sum(jnp.where(sub == lane - TILE, p[:TILE], 0.0), axis=0, keepdims=True)
            for p in pieces
        ]
        ends = jnp.where(spot == 0, diagonals[0], jnp.where(spot == 1, diagonals[1], 0.0))
        send = encode if rot and g > 0 else (lambda v: v)
        for b in range(blocks):
            cut = slice(b * LANE, (b + 1) * LANE)
            outs[g][:DIAG, cut] = send(folded[b * DIAG : (b + 1) * DIAG])
            outs[g][DIAG:NEAR, cut] = send(pieces[b][TILE:])
        outs[g][NEAR:, :LANE] = jnp.zeros((tail, LANE), outs[g].dtype)
        outs[g][NEAR:, LANE:] = send(ends)
    head[...] = normed[lax.rem(parts - first, parts), :, :LANE]
    last[...] = normed[parts - 1 - first, :, (blocks - 1) * LANE :]


def gram_parts(dosage, mean, scale, rot, inv):
    samples, cols = dosage.shape
    parts = cols // QW
    rows = NEAR + tail_rows(parts)
    kinds = [jnp.float32] + [jnp.int16 if rot else jnp.float32] * (parts - 1)
    shapes = [jax.ShapeDtypeStruct((rows, QW), kind) for kind in kinds]
    shapes += [jax.ShapeDtypeStruct((samples, LANE), jnp.bfloat16)] * 2
    return pl.pallas_call(
        functools.partial(gram_kernel, parts, rot, inv),
        in_specs=[VMEM] * 3,
        out_specs=[VMEM] * len(shapes),
        out_shape=shapes,
        scratch_shapes=[pltpu.VMEM((parts, samples, QW), jnp.bfloat16)],
        compiler_params=params(24),
        cost_estimate=pl.CostEstimate(
            flops=2 * samples * cols * (QW + LANE), bytes_accessed=dosage.size * 4, transcendentals=0
        ),
        name="gram",
    )(dosage, mean, scale)


def cross_kernel(parts, rot, inv, cols, head, last, got_o, got_e, mean, scale, *rest):
    ins, outs, (zero, one) = rest[:parts], rest[parts : 2 * parts], rest[-2:]
    blocks = QW // LANE
    tail = tail_rows(parts)
    place = line_index(("snp", "pair"))
    base = place * (cols // LANE)
    end = base + cols // LANE
    even = lax.rem(place, 2) == 0
    pick = lambda one, two: jnp.where(even, one[...], two[...])
    right = standard(pick(got_e, got_o), mean, scale, end)
    left = standard(pick(got_o, got_e), mean, scale, base - 1)
    ahead = inv * tdot(right, last[...])
    behind = inv * tdot(left, head[...])
    low = low_lanes((TILE, LANE))
    turned = pltpu.roll(behind[TILE:], TILE, axis=1)
    zero[...] = jnp.where(low, behind[:TILE], turned)
    one[...] = turned
    far = slice((blocks - 1) * LANE, blocks * LANE)
    first = lax.axis_index("smp") if rot else 0
    for i in range(parts):
        send = encode if rot and i > 0 else (lambda v: v)
        wide = (lambda v: v.astype(jnp.int32)) if rot and i > 0 else (lambda v: v)
        kind = outs[i].dtype
        outs[i][:NEAR, :] = ins[i][:NEAR, :]
        quarter = quarter_at(i, first, parts)
        share = pl.ds(pl.multiple_of(quarter * tail, 8) if rot else quarter * tail, tail)
        outs[i][NEAR:, :LANE] = send(zero[share, :])
        outs[i][NEAR:, LANE:] = jnp.where(
            low_lanes((tail, LANE)), wide(send(one[share, :])), wide(ins[i][NEAR:, LANE:])
        ).astype(kind)

        def join(i=i, send=send, wide=wide, kind=kind):
            next_one = slice(DIAG, DIAG + TILE)
            outs[i][next_one, far] = jnp.where(
                low, wide(ins[i][next_one, far]), wide(send(ahead[:TILE]))
            ).astype(kind)
            outs[i][DIAG + TILE : NEAR, far] = send(jnp.where(low, ahead[:TILE], ahead[TILE:]))

        if rot:
            pl.when(quarter == parts - 1)(join)
        elif i == parts - 1:
            join()


def cross_parts(got_e, got_o, mean, scale, made, cols, rot, inv):
    *blocks, head, last = made
    parts = len(blocks)
    height = NEAR + tail_rows(parts)
    return pl.pallas_call(
        functools.partial(cross_kernel, parts, rot, inv, cols),
        in_specs=[VMEM] * (6 + parts),
        out_specs=[VMEM] * parts,
        out_shape=[jax.ShapeDtypeStruct((height, QW), b.dtype) for b in blocks],
        scratch_shapes=[pltpu.VMEM((TILE, LANE), jnp.float32)] * 2,
        compiler_params=params(12),
        name="cross",
    )(head, last, got_o, got_e, mean, scale, *blocks)


def total_kernel(count, own, *rest):
    others, mom, out = rest[:-2], rest[-2], rest[-1]
    height = own.shape[0]
    total = own[...]
    for other in others:
        total = total + decode(other[...])
    out[0:height, :] = encode(total * (1.0 / count))
    power, high, low = encode_exact(mom[...])
    lanes = mom.shape[1]
    top = jnp.concatenate([power, low], axis=1)
    bottom = jnp.concatenate([high, jnp.zeros_like(low)], axis=1)
    out[height : height + 16, :] = to_code(jnp.concatenate([top, bottom], axis=0))


def total_of(own, others, mom):
    count = 1 + len(others)
    return pl.pallas_call(
        functools.partial(total_kernel, count),
        in_specs=[VMEM] * (count + 1),
        out_specs=VMEM,
        out_shape=jax.ShapeDtypeStruct((own.shape[0] + 16, own.shape[1]), jnp.int16),
        compiler_params=params(8),
        name="total",
    )(own, *others, mom)


def final_kernel(parts, rot, moments, tile_total, band, w, *rest):
    ring = rest[:parts]
    moms = rest[parts : parts + moments]
    out_far, imputed_far, held, out, imputed, sem = rest[parts + moments :]
    blocks = QW // LANE
    tail = tail_rows(parts)
    height = NEAR + tail
    low = low_lanes((TILE, LANE))
    sub = lax.broadcasted_iota(jnp.int32, (TILE, LANE), 0)
    lane = lax.broadcasted_iota(jnp.int32, (TILE, LANE), 1)
    cols = out.shape[1]
    first_tile = line_index(("snp", "pair")) * (cols // TILE)
    copies = []

    def ship(source, target):
        copy = pltpu.make_async_copy(source, target, sem.at[len(copies)])
        copy.start()
        copies.append(copy)

    def swap(value):
        return pltpu.roll(value, TILE, axis=1)

    if rot:
        k = lax.axis_index("smp")
        total = None
        for piece, by in zip(ring, RING):
            held[jnp.bitwise_xor(k, by)] = decode(piece[0:height, :])
            code = from_code(piece[height : height + 16, :])
            lanes = code.shape[1] // 2
            mom = decode_exact(code[:8, :lanes], code[8:, :lanes], code[:8, lanes:])
            total = mom if total is None else total + mom
    else:
        for by in range(parts):
            held[by] = ring[by][...]
        total = moms[0][...]
    solve(w, total, imputed)
    ship(imputed, imputed_far)
    for quarter in range(parts):
        fold = jnp.concatenate(
            [held[quarter, :DIAG, b * LANE : (b + 1) * LANE] for b in range(blocks)], axis=0
        )
        mirror = jnp.concatenate([fold, swap(fold)], axis=0).T[:TILE]
        for b in range(blocks):
            a = quarter * blocks + b
            cut = slice(b * LANE, (b + 1) * LANE)
            cols_here = slice(a * LANE, (a + 1) * LANE)
            masks = mask_rows(band, first_tile + 2 * a, tile_total)
            here, there = (fold, mirror) if b == 0 else (swap(fold), swap(mirror))
            second = jnp.where(
                sub == lane - TILE,
                held[quarter, NEAR + b : NEAR + b + 1, LANE : 2 * LANE],
                swap(jnp.where(lane < sub, here, there)),
            )
            centre = jnp.where(low, jnp.where(sub <= lane, here, there), second)
            out[BMAX * TILE : (BMAX + 1) * TILE, cols_here] = centre * masks[BMAX]
            for q in range(1, BMAX + 1):
                out[(BMAX + q) * TILE : (BMAX + q + 1) * TILE, cols_here] = (
                    held[quarter, DIAG + (q - 1) * TILE : DIAG + q * TILE, cut] * masks[BMAX + q]
                )
            turned = held[quarter, DIAG:NEAR, cut].T
            rolled = swap(turned)
            if a == 0:
                cross = [
                    jnp.concatenate(
                        [held[j, NEAR:height, c * LANE : (c + 1) * LANE] for j in range(parts)],
                        axis=0,
                    )
                    for c in range(2)
                ]
                one_low, two_low, two_high = swap(cross[0]), cross[0], swap(cross[1])
            else:
                one_low, two_low, two_high = (
                    last_turned[TILE:], last_rolled[:TILE], last_turned[TILE:]
                )
            out[TILE : 2 * TILE, cols_here] = jnp.where(low, one_low, rolled[:TILE]) * masks[1]
            out[0:TILE, cols_here] = jnp.where(low, two_low, two_high) * masks[0]
            last_turned, last_rolled = turned, rolled
        block = slice(quarter * QW, (quarter + 1) * QW)
        ship(out.at[:, block], out_far.at[:, block])
    for copy in copies:
        copy.wait()


def final(ring, moms, w, band_next, cols, rot):
    parts = len(ring)
    shapes = [
        jax.ShapeDtypeStruct((SPAN * TILE, cols), jnp.float32),
        jax.ShapeDtypeStruct(w.shape[1:], jnp.float32),
    ]
    return pl.pallas_call(
        functools.partial(final_kernel, parts, rot, len(moms), band_next.shape[0]),
        in_specs=[SMEM] + [VMEM] * (1 + parts + len(moms)),
        out_specs=[pl.BlockSpec(memory_space=pltpu.HBM)] * 2,
        out_shape=shapes,
        scratch_shapes=[
            pltpu.VMEM((parts, NEAR + tail_rows(parts), QW), jnp.float32),
            pltpu.VMEM(shapes[0].shape, jnp.float32),
            pltpu.VMEM(shapes[1].shape, jnp.float32),
            pltpu.SemaphoreType.DMA((parts + 1,)),
        ],
        compiler_params=params(16),
        name="final",
    )(band_next, w, *ring, *moms)


class Side:
    def __init__(self, flag, one, two):
        self.flag, self.one, self.two = flag, one, two

    def pick(self, at, convert):
        if self.flag is None:
            return self.one[at]
        return jnp.where(self.flag, convert(self.one[at]), convert(self.two[at]))

    def vector(self, at):
        return self.pick(at, lambda code: decode(code, Z_LARGEST, Z_ROOTS))

    def band(self, at):
        return self.pick(at, lambda code: from_code(code) * (1.0 / LEVELS))

    def flags(self, at):
        return self.pick(at, from_code)


def krylov_kernel(
    tile_total, sb, paired, band, ldt, z, obs, got_o, got_e, w_out, mom_out,
    dh, dl, ucat, seen, u_prev, y
):
    rows = ldt.shape[1]
    traits = z.shape[1]
    own_blocks = rows // LANE
    zb = HZ // LANE
    bb = HB // LANE
    first_tile = lax.axis_index("smp") * (rows // TILE)
    even = lax.rem(lax.axis_index("smp"), 2) == 0 if paired else None
    halo_r = Side(even, got_e, got_o)
    halo_l = Side(even, got_o, got_e)
    nb = obs.shape[0]
    ld_rows = SPAN * TILE
    total_blocks = own_blocks + 2 * zb

    tail = (slice(HZ + bb * ld_rows, got_e.shape[0]), slice(None))
    flags_l, flags_r = halo_l.flags(tail), halo_r.flags(tail)

    for c in range(total_blocks):
        if c < zb:
            vec = halo_l.vector((slice(c * LANE, (c + 1) * LANE), slice(0, traits)))
            flags = [flags_l[c * nb + i : c * nb + i + 1, :] for i in range(nb)]
        elif c < zb + own_blocks:
            o = c - zb
            vec = z[o * LANE : (o + 1) * LANE, :]
            flags = [
                obs[i : i + 1, o * LANE : (o + 1) * LANE].astype(jnp.float32) for i in range(nb)
            ]
        else:
            o = c - zb - own_blocks
            vec = halo_r.vector((slice(o * LANE, (o + 1) * LANE), slice(0, traits)))
            flags = [flags_r[o * nb + i : o * nb + i + 1, :] for i in range(nb)]
        wide = jnp.concatenate(
            [jnp.broadcast_to(f, (TBLK, LANE)) for f in flags], axis=0
        )
        mask = wide.T
        here = slice(c * LANE, (c + 1) * LANE)
        seen[here, :] = mask
        start = mask * vec
        high = start.astype(jnp.bfloat16)
        u_prev[here, :] = start
        ucat[here, :traits] = high
        ucat[here, traits:] = (start - high.astype(jnp.float32)).astype(jnp.bfloat16)

    per = sb // LANE
    low = low_lanes((TILE, LANE))
    sub = lax.broadcasted_iota(jnp.int32, (TILE, LANE), 0)
    lane = lax.broadcasted_iota(jnp.int32, (TILE, LANE), 1)
    chunks = SPAN + 1
    for c in range(own_blocks + 2 * bb):
        if c < bb:
            full = halo_l.band((slice(HZ + c * ld_rows, HZ + (c + 1) * ld_rows), slice(None)))
            get = lambda q, full=full: full[q * TILE : (q + 1) * TILE]
        elif c < bb + own_blocks:
            get = lambda q, c=c: ldt[q * TILE : (q + 1) * TILE, (c - bb) * LANE : (c - bb + 1) * LANE]
        else:
            o = c - bb - own_blocks
            full = halo_r.band((slice(HZ + o * ld_rows, HZ + (o + 1) * ld_rows), slice(None)))
            get = lambda q, full=full: full[q * TILE : (q + 1) * TILE]
        masks = mask_rows(band, first_tile + 2 * (c - bb), tile_total)
        s, h = c // per, c % per
        cols = slice(h * LANE, (h + 1) * LANE)
        parts = [get(q) * masks[q] for q in range(SPAN)]
        zero = jnp.zeros((TILE, LANE), jnp.float32)
        for j in range(chunks):
            left = parts[j] if j < SPAN else zero
            right = parts[j - 1] if j >= 1 else zero
            value = jnp.where(low, left, right)
            if BMAX <= j < BMAX + 2:
                value = value - (sub + TILE * (j - BMAX) == lane).astype(jnp.float32)
            high = value.astype(jnp.bfloat16)
            at = slice(h * LANE + j * TILE, h * LANE + (j + 1) * TILE)
            dh[s, at, cols] = high
            dl[s, at, cols] = (value - high.astype(jnp.float32)).astype(jnp.bfloat16)
        for x in range(per):
            if x < h:
                at = slice(x * LANE, (x + 1) * LANE)
            elif x > h:
                at = slice((x + 2) * LANE, (x + 3) * LANE)
            else:
                continue
            blank = jnp.zeros((LANE, LANE), jnp.bfloat16)
            dh[s, at, cols] = blank
            dl[s, at, cols] = blank

    supers = (rows + 2 * HB) // sb
    window = sb + 2 * REACH

    def product(both, rest):
        return both[:, :traits] + both[:, traits:] + rest

    ext = total_blocks * LANE

    def apply(step):
        lo, hi = (step + 1) * REACH, ext - (step + 1) * REACH
        done = 0
        for s in range(supers):
            at = s * sb
            begin = max(REACH + at, lo - REACH)
            end = min(REACH + at + sb, hi + REACH)
            top, bottom = max(at, lo), min(at + window, hi)
            if begin >= end or top >= bottom:
                continue
            r = slice(top - at, bottom - at)
            c = slice(begin - at - REACH, end - at - REACH)
            vec = ucat[begin:end, :]
            part = product(dot(dh[s, r, c], vec), dot(dl[s, r, c], vec[:, :traits]))
            both = min(max(done - top, 0), bottom - top)
            if both:
                y[top : top + both, :] += part[:both]
            if both < bottom - top:
                y[top + both : bottom, :] = part[both:]
            done = max(done, bottom)

    own = slice(HZ, HZ + rows)
    sums = []
    for step in range(ITERS):
        apply(step)
        if step == 0:
            for edge_rows, edge_cols, s, target, source in (
                (slice(0, LANE), slice(0, LANE), 0, 1, 0),
                (
                    slice(window - LANE, window),
                    slice(sb - LANE, sb),
                    supers - 1,
                    total_blocks - 2,
                    total_blocks - 1,
                ),
            ):
                vec = ucat[source * LANE : (source + 1) * LANE, :]
                part = product(
                    tdot(dh[s, edge_rows, edge_cols], vec),
                    tdot(dl[s, edge_rows, edge_cols], vec[:, :traits]),
                )
                y[target * LANE : (target + 1) * LANE, :] += part
        u_own = u_prev[own, :]
        y_own = y[own, :]
        w_out[step] = u_own + y_own
        sums.append(jnp.sum(u_own * u_own, axis=0, keepdims=True))
        sums.append(jnp.sum(u_own * y_own, axis=0, keepdims=True))
        if step < ITERS - 1:
            edge = (step + 1) * REACH
            here = slice(edge, total_blocks * LANE - edge)
            nxt = seen[here, :] * y[here, :]
            high = nxt.astype(jnp.bfloat16)
            u_prev[here, :] = nxt
            ucat[here, :traits] = high
            ucat[here, traits:] = (nxt - high.astype(jnp.float32)).astype(jnp.bfloat16)
    mom_out[...] = jnp.concatenate(
        sums + [jnp.zeros((8 - len(sums), traits), jnp.float32)], axis=0
    )


def krylov(ldt, z, obs, got_e, got_o, band_prev, paired):
    rows, traits = z.shape
    wide = rows + 2 * HB
    sb = 2 * LANE if wide % (2 * LANE) == 0 else LANE
    ext = rows + 2 * HZ
    supers = wide // sb
    return pl.pallas_call(
        functools.partial(krylov_kernel, band_prev.shape[0], sb, paired),
        in_specs=[SMEM] + [VMEM] * 5,
        out_specs=[VMEM, VMEM],
        out_shape=[
            jax.ShapeDtypeStruct((ITERS, rows, traits), jnp.float32),
            jax.ShapeDtypeStruct((8, traits), jnp.float32),
        ],
        scratch_shapes=[
            pltpu.VMEM((supers, sb + 2 * REACH, sb), jnp.bfloat16),
            pltpu.VMEM((supers, sb + 2 * REACH, sb), jnp.bfloat16),
            pltpu.VMEM((ext, 2 * traits), jnp.bfloat16),
            pltpu.VMEM((ext, traits), jnp.float32),
            pltpu.VMEM((ext, traits), jnp.float32),
            pltpu.VMEM((ext, traits), jnp.float32),
        ],
        compiler_params=params(28),
        cost_estimate=pl.CostEstimate(
            flops=ITERS * 6 * ext * SPAN * TILE * traits, bytes_accessed=ldt.size * 4, transcendentals=0
        ),
        name="krylov",
    )(band_prev, ldt, z, obs, got_o, got_e)


def solve(w, mom, out):
    m = [mom[i : i + 1, :] for i in range(2 * ITERS)]
    shift = 1.0 + RIDGE
    h = [shift * m[i] + m[i + 1] for i in range(2 * ITERS - 1)]
    d0 = h[0]
    l10 = h[1] / d0
    l20 = h[2] / d0
    d1 = h[2] - l10 * h[1]
    t12 = h[3] - l20 * h[1]
    ok1 = d1 > TINY * h[2]
    r1 = jnp.where(ok1, 1.0 / jnp.where(ok1, d1, 1.0), 0.0)
    l21 = t12 * r1
    d2 = h[4] - l20 * h[2] - l21 * t12
    ok2 = ok1 & (d2 > TINY * h[4])
    r2 = jnp.where(ok2, 1.0 / jnp.where(ok2, d2, 1.0), 0.0)
    z0 = m[0]
    z1 = m[1] - l10 * z0
    z2 = m[2] - l20 * z0 - l21 * z1
    c2 = z2 * r2
    c1 = z1 * r1 - l21 * c2
    c0 = z0 / d0 - l10 * c1 - l20 * c2
    out[...] = c0 * w[0] + c1 * w[1] + c2 * w[2]


def packed(z, ldt, obs):
    z = jnp.pad(z, ((0, 0), (0, LANE - z.shape[1])))
    obs = obs.astype(jnp.float32)
    parts = [z]
    parts += [ldt[:, i : i + LANE] for i in range(0, ldt.shape[1], LANE)]
    parts += [obs[:, i : i + LANE] for i in range(0, obs.shape[1], LANE)]
    height = sum(p.shape[0] for p in parts)
    parts.append(jnp.zeros((-height % 16, LANE), jnp.float32))
    return jnp.concatenate(parts, axis=0)


def halos(z, ldt, obs, axis):
    count = lax.axis_size(axis)
    rows = z.shape[0]

    def shifted(value, by):
        pairs = [(i, i + by) for i in range(count) if 0 <= i + by < count]
        return lax.ppermute(value, axis, pairs)

    def gather(value, width, dim):
        lefts, rights = [], []
        hop, have = 1, 0
        while have < width:
            take = min(rows, width - have)
            lefts.insert(0, shifted(lax.slice_in_dim(value, rows - take, rows, axis=dim), hop))
            rights.append(shifted(lax.slice_in_dim(value, 0, take, axis=dim), -hop))
            have += take
            hop += 1
        return jnp.concatenate(lefts, dim), jnp.concatenate(rights, dim)

    zs = gather(z, HZ, 0)
    lds = gather(ldt, HB, 1)
    seens = gather(obs, HZ, 1)
    return packed(zs[0], lds[0], seens[0]), packed(zs[1], lds[1], seens[1])


def local(dosage, allele_mean, snp_scale, band_next, ld_prev, band_prev, zscores, observed):
    samples, cols = dosage.shape
    rows = ld_prev.shape[0]
    n_smp = lax.axis_size("smp")
    ldt = ld_prev.T
    obs = observed.T
    line = ("snp", "pair")
    paired = rows >= HZ

    sent = pack(dosage, zscores, ldt, obs, paired)
    dos_o = exchange(sent[1], line, 1)
    dos_e = exchange(sent[0], line, 0)
    if paired:
        got_o = exchange(sent[3], ("smp",), 1)
        got_e = exchange(sent[2], ("smp",), 0)
    else:
        got_o, got_e = halos(zscores, ldt, obs, "smp")

    parts = cols // QW
    rot = parts == n_smp == 4 and zscores.shape[1] == LANE
    inv = 1.0 / (samples if rot else samples * n_smp)
    mean = allele_mean.reshape(-1, LANE)
    scale = snp_scale.reshape(-1, LANE)
    made = gram_parts(dosage, mean, scale, rot, inv)
    blocks = cross_parts(dos_e, dos_o, mean, scale, made, cols, rot, inv)
    if rot:

        def shift(value, by):
            return lax.ppermute(value, "smp", [(i, (i + by) % n_smp) for i in range(n_smp)])

        def swap(value, by):
            return lax.ppermute(value, "smp", [(i, i ^ by) for i in range(n_smp)])

        got = [shift(blocks[by], by) for by in (1, 2, 3)]
    w, mom = krylov(ldt, zscores, obs, got_e, got_o, band_prev, paired)
    if rot:
        mine = total_of(blocks[0], got, mom)
        ring = [swap(mine, by) if by else mine for by in RING]
        moms = []
    else:
        ring = list(lax.psum(tuple(blocks), "smp"))
        moms = [lax.psum(mom, "smp")]
    ldn, imputed = final(ring, moms, w, band_next, cols, rot)
    return ldn.T, imputed


def solution(mesh):
    return jax.shard_map(
        local,
        mesh=mesh,
        in_specs=(
            P(("grp", "smp"), ("snp", "pair")),
            P("grp"),
            P("grp"),
            P("grp"),
            P(("grp", "smp"), None),
            P("grp"),
            P(("grp", "smp"), ("snp", "pair")),
            P(("grp", "smp"), ("snp", "pair")),
        ),
        out_specs=(P(("grp", "snp", "pair"), None), P(("grp", "smp"), ("snp", "pair"))),
        check_vma=False,
    )
```

```python
import functools
import jax
import jax.numpy as jnp
from jax import lax
from jax.experimental import pallas as pl
from jax.experimental.pallas import tpu as pltpu
from jax.sharding import PartitionSpec as P

TILE = 64
BMAX = 2
TBLK = 64
ITERS = 3
RIDGE = 1.0
SPAN = 2 * BMAX + 1
REACH = TILE * BMAX
LANE = 128
QW = 256
HZ = ITERS * REACH
HB = (ITERS - 1) * REACH
TINY = 1e-6
VMEM = pl.BlockSpec(memory_space=pltpu.VMEM)


def params(mib):
    return pltpu.CompilerParams(vmem_limit_bytes=mib * 1024 * 1024)


def mask_table(band_ref, first_tile, tiles):
    total = band_ref.shape[1]
    lanes = (tiles + 2 * BMAX) * TILE
    shape = (total, lanes)
    tile = lax.broadcasted_iota(jnp.int32, shape, 1) // TILE + (first_tile - BMAX)
    chosen = tile == lax.broadcasted_iota(jnp.int32, shape, 0)
    given = jnp.broadcast_to(band_ref[...].astype(jnp.float32), (8, total)).astype(jnp.bfloat16)
    widths = dot(given, chosen.astype(jnp.float32).astype(jnp.bfloat16))[:1]
    here = widths[:, BMAX * TILE : (BMAX + tiles) * TILE]
    rows = []
    for q in range(-BMAX, BMAX + 1):
        if q % 2:
            beside = pltpu.roll(widths, (-q * TILE) % lanes, axis=1)[
                :, BMAX * TILE : (BMAX + tiles) * TILE
            ]
        else:
            beside = widths[:, (BMAX + q) * TILE : (BMAX + q + tiles) * TILE]
        rows.append((abs(q) <= jnp.minimum(here, beside)).astype(jnp.float32))
    return rows


def masks_at(table, block):
    return [row[:, block * LANE : (block + 1) * LANE] for row in table]


def low_lanes(shape):
    return lax.broadcasted_iota(jnp.int32, shape, 1) < TILE


def tdot(left, right):
    return lax.dot_general(
        left, right, (((0,), (0,)), ((), ())), preferred_element_type=jnp.float32
    )


def dot(left, right):
    return lax.dot_general(
        left, right, (((1,), (0,)), ((), ())), preferred_element_type=jnp.float32
    )


LEVELS = 32000.0
Z_LARGEST = 22.0
Z_ROOTS = 2
LARGEST = 36.0


def encode(value, largest=LARGEST, roots=3):
    size = jnp.minimum(jnp.abs(value) * (1.0 / largest), 1.0) + 1e-30
    for _ in range(roots):
        size = size * lax.rsqrt(size)
    code = size * LEVELS + 0.5
    return to_code(jnp.where(value < 0, -code, code))


def decode(code, largest=LARGEST, roots=3):
    value = from_code(code)
    size = value * (1.0 / LEVELS)
    for _ in range(roots):
        size = size * size
    size = size * largest
    return jnp.where(value < 0, -size, size)


def encode_exact(value):
    size = jnp.maximum(jnp.abs(value), 1e-30)
    power = jnp.clip(jnp.floor(jnp.log2(size)), -100.0, 120.0)
    scaled = value * jnp.exp2(-power) * 2.0**13
    high = jnp.round(scaled)
    low = jnp.round((scaled - high) * 2.0**14)
    return power, high, low


def decode_exact(power, high, low):
    return (high * 2.0**-13 + low * 2.0**-27) * jnp.exp2(power)


def to_code(value):
    return value.astype(jnp.int32).astype(jnp.int16)


def from_code(code):
    return code.astype(jnp.int32).astype(jnp.float32)


def line_index(axes):
    place = lax.axis_index(axes[0])
    for axis in axes[1:]:
        place = place * lax.axis_size(axis) + lax.axis_index(axis)
    return place


def in_hbm(value):
    return pltpu.with_memory_space_constraint(value, pltpu.HBM)


def halo_height(nb):
    height = HZ + HB // LANE * SPAN * TILE + HZ // LANE * nb
    return height + -height % 16


def pack_kernel(dos, z, ldt, obs, dos_e, dos_o, *rest):
    cols = dos.shape[1]
    rows = z.shape[0]
    sem = rest[-1]
    copies = []

    def start(source, target):
        copy = pltpu.make_async_copy(source, target, sem.at[len(copies)])
        copy.start()
        copies.append(copy)

    even = lax.rem(line_index(("snp", "pair")), 2) == 0
    to_e = pl.multiple_of(jnp.where(even, cols - LANE, 0), LANE)
    to_o = pl.multiple_of(jnp.where(even, 0, cols - LANE), LANE)
    halo = ()
    if len(rest) > 1:
        halo, (zs, lds, flags) = rest[:2], rest[2:5]
        even = lax.rem(lax.axis_index("smp"), 2) == 0
        for i, last in enumerate((even, jnp.logical_not(even))):
            row = pl.multiple_of(jnp.where(last, rows - HZ, 0), LANE)
            col = pl.multiple_of(jnp.where(last, rows - HB, 0), LANE)
            start(z.at[pl.ds(row, HZ), :], zs.at[i])
            start(ldt.at[:, pl.ds(col, HB)], lds.at[i])
            start(obs.at[:, pl.ds(row, HZ)], flags.at[i])
    start(dos.at[:, pl.ds(to_e, LANE)], dos_e)
    start(dos.at[:, pl.ds(to_o, LANE)], dos_o)
    for i, out in enumerate(halo):
        nb = obs.shape[0]
        for copy in copies[3 * i : 3 * i + 3]:
            copy.wait()
        out[0:HZ, : z.shape[1]] = encode(zs[i], Z_LARGEST, Z_ROOTS)
        base = HZ
        for j in range(HB // LANE):
            out[base : base + SPAN * TILE, :] = to_code(
                jnp.round(lds[i, :, j * LANE : (j + 1) * LANE] * LEVELS)
            )
            base += SPAN * TILE
        bits = [flags[i, :, j * LANE : (j + 1) * LANE] for j in range(HZ // LANE)]
        blank = out.shape[0] - base - nb * len(bits)
        bits.append(jnp.zeros((blank, LANE), jnp.int32))
        out[base:, :] = jnp.concatenate(bits, axis=0).astype(jnp.int16)
    for copy in copies[3 * len(halo) :]:
        copy.wait()


def pack(dosage, z, ldt, obs, with_halo):
    samples = dosage.shape[0]
    shapes = [jax.ShapeDtypeStruct((samples, LANE), dosage.dtype)] * 2
    copies = 2
    scratch = []
    if with_halo:
        shapes += [jax.ShapeDtypeStruct((halo_height(obs.shape[0]), LANE), jnp.int16)] * 2
        copies += 6
        scratch = [
            pltpu.VMEM((2, HZ, z.shape[1]), z.dtype),
            pltpu.VMEM((2, SPAN * TILE, HB), ldt.dtype),
            pltpu.VMEM((2, obs.shape[0], HZ), obs.dtype),
        ]
    far = pl.BlockSpec(memory_space=pltpu.HBM)
    return pl.pallas_call(
        pack_kernel,
        in_specs=[far] * 4,
        out_specs=[VMEM] * len(shapes),
        out_shape=shapes,
        scratch_shapes=scratch + [pltpu.SemaphoreType.DMA((copies,))],
        compiler_params=params(8),
        name="pack",
    )(in_hbm(dosage), in_hbm(z), in_hbm(ldt), in_hbm(obs))


def exchange(value, axes, phase):
    count = 1
    for axis in axes:
        count *= lax.axis_size(axis)
    if phase == 0 and lax.axis_size(axes[-1]) == 2 and len(axes) > 1:
        return lax.ppermute(value, axes[-1], [(0, 1), (1, 0)])
    pairs = []
    for i in range(phase, count - 1, 2):
        pairs += [(i, i + 1), (i + 1, i)]
    return lax.ppermute(value, axes, pairs)


DIAG = TILE // 2
RING = (0, 2, 3, 1)
NEAR = DIAG + BMAX * TILE


def quarter_at(step, first, parts):
    if isinstance(first, int):
        return (step + first) % parts
    return lax.rem(step + first, parts)


def tail_rows(parts):
    return TILE // parts


def standard(values, mean, scale, block):
    row = jnp.clip(block, 0, mean.shape[0] - 1)
    m = mean[pl.ds(row, 1), :]
    s = scale[pl.ds(row, 1), :]
    return ((values.astype(jnp.float32) - m) * s).astype(jnp.bfloat16)


def gram_kernel(parts, rot, inv, dos, mean, scale, *rest):
    outs, (head, last), normed = rest[:parts], rest[parts : parts + 2], rest[parts + 2]
    blocks = QW // LANE
    samples, cols = dos.shape
    base = line_index(("snp", "pair")) * (cols // LANE)
    first = lax.axis_index("smp") if rot else 0
    tail = tail_rows(parts)
    sub = lax.broadcasted_iota(jnp.int32, (TILE, LANE), 0)
    lane = lax.broadcasted_iota(jnp.int32, (TILE, LANE), 1)
    spot = lax.broadcasted_iota(jnp.int32, (tail, LANE), 0)
    low = low_lanes(((BMAX + 1) * TILE, LANE))

    def settle(g):
        block = quarter_at(g, first, parts) * blocks
        for b in range(blocks):
            at = block + b
            if rot:
                at = pl.multiple_of(at * LANE, LANE)
                values = dos[:, pl.ds(at, LANE)]
            else:
                values = dos[:, at * LANE : (at + 1) * LANE]
            normed[g, :, b * LANE : (b + 1) * LANE] = standard(
                values, mean, scale, base + block + b
            )

    settle(0)
    for g in range(parts):
        if g + 1 < parts:
            settle(g + 1)
        own = normed[g]
        top = tdot(own, own)
        bottom = tdot(normed[(g + 1) % parts, :, :LANE], own)
        pieces = []
        for b in range(blocks):
            cut = slice(b * LANE, (b + 1) * LANE)
            full = jnp.concatenate([top[b * LANE :, cut], bottom[:, cut]], axis=0)
            pieces.append(
                inv * jnp.where(low, full[: low.shape[0]], full[TILE : TILE + low.shape[0]])
            )
        folded = [
            jnp.where(sub <= lane, p[:TILE], pltpu.roll(p[:TILE], TILE, axis=1)) for p in pieces
        ]
        folded = jnp.where(lane < TILE, folded[0], pltpu.roll(folded[1], TILE, axis=1))
        diagonals = [
            jnp.sum(jnp.where(sub == lane - TILE, p[:TILE], 0.0), axis=0, keepdims=True)
            for p in pieces
        ]
        ends = jnp.where(spot == 0, diagonals[0], jnp.where(spot == 1, diagonals[1], 0.0))
        send = encode if rot and g > 0 else (lambda v: v)
        for b in range(blocks):
            cut = slice(b * LANE, (b + 1) * LANE)
            outs[g][:DIAG, cut] = send(folded[b * DIAG : (b + 1) * DIAG])
            outs[g][DIAG:NEAR, cut] = send(pieces[b][TILE:])
        outs[g][NEAR:, :LANE] = jnp.zeros((tail, LANE), outs[g].dtype)
        outs[g][NEAR:, LANE:] = send(ends)
    head[...] = normed[lax.rem(parts - first, parts), :, :LANE]
    last[...] = normed[parts - 1 - first, :, (blocks - 1) * LANE :]


def gram_parts(dosage, mean, scale, rot, inv):
    samples, cols = dosage.shape
    parts = cols // QW
    rows = NEAR + tail_rows(parts)
    kinds = [jnp.float32] + [jnp.int16 if rot else jnp.float32] * (parts - 1)
    shapes = [jax.ShapeDtypeStruct((rows, QW), kind) for kind in kinds]
    shapes += [jax.ShapeDtypeStruct((samples, LANE), jnp.bfloat16)] * 2
    return pl.pallas_call(
        functools.partial(gram_kernel, parts, rot, inv),
        in_specs=[VMEM] * 3,
        out_specs=[VMEM] * len(shapes),
        out_shape=shapes,
        scratch_shapes=[pltpu.VMEM((parts, samples, QW), jnp.bfloat16)],
        compiler_params=params(24),
        cost_estimate=pl.CostEstimate(
            flops=2 * samples * cols * (QW + LANE), bytes_accessed=dosage.size * 4, transcendentals=0
        ),
        name="gram",
    )(dosage, mean, scale)


def cross_kernel(parts, rot, inv, cols, head, last, got_e, got_o, mean, scale, *rest):
    ins, outs, (zero, one) = rest[:parts], rest[parts : 2 * parts], rest[-2:]
    blocks = QW // LANE
    tail = tail_rows(parts)
    place = line_index(("snp", "pair"))
    base = place * (cols // LANE)
    end = base + cols // LANE
    even = lax.rem(place, 2) == 0
    pick = lambda one, two: jnp.where(even, one[...], two[...])
    right = standard(pick(got_e, got_o), mean, scale, end)
    left = standard(pick(got_o, got_e), mean, scale, base - 1)
    ahead = inv * tdot(right, last[...])
    behind = inv * tdot(left, head[...])
    low = low_lanes((TILE, LANE))
    turned = pltpu.roll(behind[TILE:], TILE, axis=1)
    zero[...] = jnp.where(low, behind[:TILE], turned)
    one[...] = turned
    far = slice((blocks - 1) * LANE, blocks * LANE)
    first = lax.axis_index("smp") if rot else 0
    for i in range(parts):
        send = encode if rot and i > 0 else (lambda v: v)
        wide = (lambda v: v.astype(jnp.int32)) if rot and i > 0 else (lambda v: v)
        kind = outs[i].dtype
        outs[i][:NEAR, :] = ins[i][:NEAR, :]
        quarter = quarter_at(i, first, parts)
        share = pl.ds(pl.multiple_of(quarter * tail, 8) if rot else quarter * tail, tail)
        outs[i][NEAR:, :LANE] = send(zero[share, :])
        outs[i][NEAR:, LANE:] = jnp.where(
            low_lanes((tail, LANE)), wide(send(one[share, :])), wide(ins[i][NEAR:, LANE:])
        ).astype(kind)

        def join(i=i, send=send, wide=wide, kind=kind):
            next_one = slice(DIAG, DIAG + TILE)
            outs[i][next_one, far] = jnp.where(
                low, wide(ins[i][next_one, far]), wide(send(ahead[:TILE]))
            ).astype(kind)
            outs[i][DIAG + TILE : NEAR, far] = send(jnp.where(low, ahead[:TILE], ahead[TILE:]))

        if rot:
            pl.when(quarter == parts - 1)(join)
        elif i == parts - 1:
            join()


def cross_parts(got_e, got_o, mean, scale, made, cols, rot, inv):
    *blocks, head, last = made
    parts = len(blocks)
    height = NEAR + tail_rows(parts)
    return pl.pallas_call(
        functools.partial(cross_kernel, parts, rot, inv, cols),
        in_specs=[VMEM] * (6 + parts),
        out_specs=[VMEM] * parts,
        out_shape=[jax.ShapeDtypeStruct((height, QW), b.dtype) for b in blocks],
        scratch_shapes=[pltpu.VMEM((TILE, LANE), jnp.float32)] * 2,
        compiler_params=params(12),
        name="cross",
    )(head, last, got_e, got_o, mean, scale, *blocks)


def total_kernel(count, own, *rest):
    others, mom, out = rest[:-2], rest[-2], rest[-1]
    height = own.shape[0]
    total = own[...]
    for other in others:
        total = total + decode(other[...])
    out[0:height, :] = encode(total * (1.0 / count))
    power, high, low = encode_exact(mom[...])
    lanes = mom.shape[1]
    top = jnp.concatenate([power, low], axis=1)
    bottom = jnp.concatenate([high, jnp.zeros_like(low)], axis=1)
    out[height : height + 16, :] = to_code(jnp.concatenate([top, bottom], axis=0))


def total_of(own, others, mom):
    count = 1 + len(others)
    return pl.pallas_call(
        functools.partial(total_kernel, count),
        in_specs=[VMEM] * (count + 1),
        out_specs=VMEM,
        out_shape=jax.ShapeDtypeStruct((own.shape[0] + 16, own.shape[1]), jnp.int16),
        compiler_params=params(8),
        name="total",
    )(own, *others, mom)


def final_kernel(parts, rot, moments, band, w, *rest):
    ring = rest[:parts]
    moms = rest[parts : parts + moments]
    out_far, imputed_far, held, out, imputed, sem = rest[parts + moments :]
    blocks = QW // LANE
    tail = tail_rows(parts)
    height = NEAR + tail
    low = low_lanes((TILE, LANE))
    sub = lax.broadcasted_iota(jnp.int32, (TILE, LANE), 0)
    lane = lax.broadcasted_iota(jnp.int32, (TILE, LANE), 1)
    cols = out.shape[1]
    first_tile = line_index(("snp", "pair")) * (cols // TILE)
    table = mask_table(band, first_tile, cols // TILE)
    copies = []

    def ship(source, target):
        copy = pltpu.make_async_copy(source, target, sem.at[len(copies)])
        copy.start()
        copies.append(copy)

    def swap(value):
        return pltpu.roll(value, TILE, axis=1)

    if rot:
        k = lax.axis_index("smp")
        total = None
        for piece, by in zip(ring, RING):
            held[jnp.bitwise_xor(k, by)] = decode(piece[0:height, :])
            code = from_code(piece[height : height + 16, :])
            lanes = code.shape[1] // 2
            mom = decode_exact(code[:8, :lanes], code[8:, :lanes], code[:8, lanes:])
            total = mom if total is None else total + mom
    else:
        for by in range(parts):
            held[by] = ring[by][...]
        total = moms[0][...]
    solve(w, total, imputed)
    ship(imputed, imputed_far)
    for quarter in range(parts):
        fold = jnp.concatenate(
            [held[quarter, :DIAG, b * LANE : (b + 1) * LANE] for b in range(blocks)], axis=0
        )
        mirror = jnp.concatenate([fold, swap(fold)], axis=0).T[:TILE]
        for b in range(blocks):
            a = quarter * blocks + b
            cut = slice(b * LANE, (b + 1) * LANE)
            cols_here = slice(a * LANE, (a + 1) * LANE)
            masks = masks_at(table, a)
            here, there = (fold, mirror) if b == 0 else (swap(fold), swap(mirror))
            second = jnp.where(
                sub == lane - TILE,
                held[quarter, NEAR + b : NEAR + b + 1, LANE : 2 * LANE],
                swap(jnp.where(lane < sub, here, there)),
            )
            centre = jnp.where(low, jnp.where(sub <= lane, here, there), second)
            out[BMAX * TILE : (BMAX + 1) * TILE, cols_here] = centre * masks[BMAX]
            for q in range(1, BMAX + 1):
                out[(BMAX + q) * TILE : (BMAX + q + 1) * TILE, cols_here] = (
                    held[quarter, DIAG + (q - 1) * TILE : DIAG + q * TILE, cut] * masks[BMAX + q]
                )
            turned = held[quarter, DIAG:NEAR, cut].T
            rolled = swap(turned)
            if a == 0:
                cross = [
                    jnp.concatenate(
                        [held[j, NEAR:height, c * LANE : (c + 1) * LANE] for j in range(parts)],
                        axis=0,
                    )
                    for c in range(2)
                ]
                one_low, two_low, two_high = swap(cross[0]), cross[0], swap(cross[1])
            else:
                one_low, two_low, two_high = (
                    last_turned[TILE:], last_rolled[:TILE], last_turned[TILE:]
                )
            out[TILE : 2 * TILE, cols_here] = jnp.where(low, one_low, rolled[:TILE]) * masks[1]
            out[0:TILE, cols_here] = jnp.where(low, two_low, two_high) * masks[0]
            last_turned, last_rolled = turned, rolled
        block = slice(quarter * QW, (quarter + 1) * QW)
        ship(out.at[:, block], out_far.at[:, block])
    for copy in copies:
        copy.wait()


def final(ring, moms, w, band_next, cols, rot):
    parts = len(ring)
    shapes = [
        jax.ShapeDtypeStruct((SPAN * TILE, cols), jnp.float32),
        jax.ShapeDtypeStruct(w.shape[1:], jnp.float32),
    ]
    return pl.pallas_call(
        functools.partial(final_kernel, parts, rot, len(moms)),
        in_specs=[VMEM] * (2 + parts + len(moms)),
        out_specs=[pl.BlockSpec(memory_space=pltpu.HBM)] * 2,
        out_shape=shapes,
        scratch_shapes=[
            pltpu.VMEM((parts, NEAR + tail_rows(parts), QW), jnp.float32),
            pltpu.VMEM(shapes[0].shape, jnp.float32),
            pltpu.VMEM(shapes[1].shape, jnp.float32),
            pltpu.SemaphoreType.DMA((parts + 1,)),
        ],
        compiler_params=params(16),
        name="final",
    )(band_next.reshape(1, -1), w, *ring, *moms)


class Side:
    def __init__(self, flag, one, two):
        self.flag, self.one, self.two = flag, one, two

    def pick(self, at, convert):
        if self.flag is None:
            return self.one[at]
        return jnp.where(self.flag, convert(self.one[at]), convert(self.two[at]))

    def vector(self, at):
        return self.pick(at, lambda code: decode(code, Z_LARGEST, Z_ROOTS))

    def band(self, at):
        return self.pick(at, lambda code: from_code(code) * (1.0 / LEVELS))

    def flags(self, at):
        return self.pick(at, from_code)


def krylov_kernel(
    sb, paired, band, ldt, z, obs, got_o, got_e, w_out, mom_out,
    dh, dl, ucat, seen, u_prev, y
):
    rows = ldt.shape[1]
    traits = z.shape[1]
    own_blocks = rows // LANE
    zb = HZ // LANE
    bb = HB // LANE
    first_tile = lax.axis_index("smp") * (rows // TILE)
    even = lax.rem(lax.axis_index("smp"), 2) == 0 if paired else None
    halo_r = Side(even, got_e, got_o)
    halo_l = Side(even, got_o, got_e)
    nb = obs.shape[0]
    ld_rows = SPAN * TILE
    total_blocks = own_blocks + 2 * zb

    tail = (slice(HZ + bb * ld_rows, got_e.shape[0]), slice(None))
    flags_l, flags_r = halo_l.flags(tail), halo_r.flags(tail)

    for c in range(total_blocks):
        if c < zb:
            vec = halo_l.vector((slice(c * LANE, (c + 1) * LANE), slice(0, traits)))
            flags = [flags_l[c * nb + i : c * nb + i + 1, :] for i in range(nb)]
        elif c < zb + own_blocks:
            o = c - zb
            vec = z[o * LANE : (o + 1) * LANE, :]
            flags = [
                obs[i : i + 1, o * LANE : (o + 1) * LANE].astype(jnp.float32) for i in range(nb)
            ]
        else:
            o = c - zb - own_blocks
            vec = halo_r.vector((slice(o * LANE, (o + 1) * LANE), slice(0, traits)))
            flags = [flags_r[o * nb + i : o * nb + i + 1, :] for i in range(nb)]
        wide = jnp.concatenate(
            [jnp.broadcast_to(f, (TBLK, LANE)) for f in flags], axis=0
        )
        mask = wide.T
        here = slice(c * LANE, (c + 1) * LANE)
        seen[here, :] = mask
        start = mask * vec
        high = start.astype(jnp.bfloat16)
        u_prev[here, :] = start
        ucat[here, :traits] = high
        ucat[here, traits:] = (start - high.astype(jnp.float32)).astype(jnp.bfloat16)

    per = sb // LANE
    low = low_lanes((TILE, LANE))
    sub = lax.broadcasted_iota(jnp.int32, (TILE, LANE), 0)
    lane = lax.broadcasted_iota(jnp.int32, (TILE, LANE), 1)
    chunks = SPAN + 1
    table = mask_table(band, first_tile - HB // TILE, (rows + 2 * HB) // TILE)
    for c in range(own_blocks + 2 * bb):
        if c < bb:
            full = halo_l.band((slice(HZ + c * ld_rows, HZ + (c + 1) * ld_rows), slice(None)))
            get = lambda q, full=full: full[q * TILE : (q + 1) * TILE]
        elif c < bb + own_blocks:
            get = lambda q, c=c: ldt[q * TILE : (q + 1) * TILE, (c - bb) * LANE : (c - bb + 1) * LANE]
        else:
            o = c - bb - own_blocks
            full = halo_r.band((slice(HZ + o * ld_rows, HZ + (o + 1) * ld_rows), slice(None)))
            get = lambda q, full=full: full[q * TILE : (q + 1) * TILE]
        masks = masks_at(table, c)
        s, h = c // per, c % per
        cols = slice(h * LANE, (h + 1) * LANE)
        parts = [get(q) * masks[q] for q in range(SPAN)]
        zero = jnp.zeros((TILE, LANE), jnp.float32)
        for j in range(chunks):
            left = parts[j] if j < SPAN else zero
            right = parts[j - 1] if j >= 1 else zero
            value = jnp.where(low, left, right)
            if BMAX <= j < BMAX + 2:
                value = value - (sub + TILE * (j - BMAX) == lane).astype(jnp.float32)
            high = value.astype(jnp.bfloat16)
            at = slice(h * LANE + j * TILE, h * LANE + (j + 1) * TILE)
            dh[s, at, cols] = high
            dl[s, at, cols] = (value - high.astype(jnp.float32)).astype(jnp.bfloat16)
        for x in range(per):
            if x < h:
                at = slice(x * LANE, (x + 1) * LANE)
            elif x > h:
                at = slice((x + 2) * LANE, (x + 3) * LANE)
            else:
                continue
            blank = jnp.zeros((LANE, LANE), jnp.bfloat16)
            dh[s, at, cols] = blank
            dl[s, at, cols] = blank

    supers = (rows + 2 * HB) // sb
    window = sb + 2 * REACH

    def product(both, rest):
        return both[:, :traits] + both[:, traits:] + rest

    ext = total_blocks * LANE

    def apply(step):
        lo, hi = (step + 1) * REACH, ext - (step + 1) * REACH
        done = 0
        for s in range(supers):
            at = s * sb
            begin = max(REACH + at, lo - REACH)
            end = min(REACH + at + sb, hi + REACH)
            top, bottom = max(at, lo), min(at + window, hi)
            if begin >= end or top >= bottom:
                continue
            r = slice(top - at, bottom - at)
            c = slice(begin - at - REACH, end - at - REACH)
            vec = ucat[begin:end, :]
            part = product(dot(dh[s, r, c], vec), dot(dl[s, r, c], vec[:, :traits]))
            both = min(max(done - top, 0), bottom - top)
            if both:
                y[top : top + both, :] += part[:both]
            if both < bottom - top:
                y[top + both : bottom, :] = part[both:]
            done = max(done, bottom)

    own = slice(HZ, HZ + rows)
    sums = []
    for step in range(ITERS):
        apply(step)
        if step == 0:
            for edge_rows, edge_cols, s, target, source in (
                (slice(0, LANE), slice(0, LANE), 0, 1, 0),
                (
                    slice(window - LANE, window),
                    slice(sb - LANE, sb),
                    supers - 1,
                    total_blocks - 2,
                    total_blocks - 1,
                ),
            ):
                vec = ucat[source * LANE : (source + 1) * LANE, :]
                part = product(
                    tdot(dh[s, edge_rows, edge_cols], vec),
                    tdot(dl[s, edge_rows, edge_cols], vec[:, :traits]),
                )
                y[target * LANE : (target + 1) * LANE, :] += part
        u_own = u_prev[own, :]
        y_own = y[own, :]
        w_out[step] = u_own + y_own
        sums.append(jnp.sum(u_own * u_own, axis=0, keepdims=True))
        sums.append(jnp.sum(u_own * y_own, axis=0, keepdims=True))
        if step < ITERS - 1:
            edge = (step + 1) * REACH
            here = slice(edge, total_blocks * LANE - edge)
            nxt = seen[here, :] * y[here, :]
            high = nxt.astype(jnp.bfloat16)
            u_prev[here, :] = nxt
            ucat[here, :traits] = high
            ucat[here, traits:] = (nxt - high.astype(jnp.float32)).astype(jnp.bfloat16)
    mom_out[...] = jnp.concatenate(
        sums + [jnp.zeros((8 - len(sums), traits), jnp.float32)], axis=0
    )


def krylov(ldt, z, obs, got_e, got_o, band_prev, paired):
    rows, traits = z.shape
    wide = rows + 2 * HB
    sb = 2 * LANE if wide % (2 * LANE) == 0 else LANE
    ext = rows + 2 * HZ
    supers = wide // sb
    return pl.pallas_call(
        functools.partial(krylov_kernel, sb, paired),
        in_specs=[VMEM] * 6,
        out_specs=[VMEM, VMEM],
        out_shape=[
            jax.ShapeDtypeStruct((ITERS, rows, traits), jnp.float32),
            jax.ShapeDtypeStruct((8, traits), jnp.float32),
        ],
        scratch_shapes=[
            pltpu.VMEM((supers, sb + 2 * REACH, sb), jnp.bfloat16),
            pltpu.VMEM((supers, sb + 2 * REACH, sb), jnp.bfloat16),
            pltpu.VMEM((ext, 2 * traits), jnp.bfloat16),
            pltpu.VMEM((ext, traits), jnp.float32),
            pltpu.VMEM((ext, traits), jnp.float32),
            pltpu.VMEM((ext, traits), jnp.float32),
        ],
        compiler_params=params(28),
        cost_estimate=pl.CostEstimate(
            flops=ITERS * 6 * ext * SPAN * TILE * traits, bytes_accessed=ldt.size * 4, transcendentals=0
        ),
        name="krylov",
    )(band_prev.reshape(1, -1), ldt, z, obs, got_o, got_e)


def solve(w, mom, out):
    m = [mom[i : i + 1, :] for i in range(2 * ITERS)]
    shift = 1.0 + RIDGE
    h = [shift * m[i] + m[i + 1] for i in range(2 * ITERS - 1)]
    d0 = h[0]
    l10 = h[1] / d0
    l20 = h[2] / d0
    d1 = h[2] - l10 * h[1]
    t12 = h[3] - l20 * h[1]
    ok1 = d1 > TINY * h[2]
    r1 = jnp.where(ok1, 1.0 / jnp.where(ok1, d1, 1.0), 0.0)
    l21 = t12 * r1
    d2 = h[4] - l20 * h[2] - l21 * t12
    ok2 = ok1 & (d2 > TINY * h[4])
    r2 = jnp.where(ok2, 1.0 / jnp.where(ok2, d2, 1.0), 0.0)
    z0 = m[0]
    z1 = m[1] - l10 * z0
    z2 = m[2] - l20 * z0 - l21 * z1
    c2 = z2 * r2
    c1 = z1 * r1 - l21 * c2
    c0 = z0 / d0 - l10 * c1 - l20 * c2
    out[...] = c0 * w[0] + c1 * w[1] + c2 * w[2]


def packed(z, ldt, obs):
    z = jnp.pad(z, ((0, 0), (0, LANE - z.shape[1])))
    obs = obs.astype(jnp.float32)
    parts = [z]
    parts += [ldt[:, i : i + LANE] for i in range(0, ldt.shape[1], LANE)]
    parts += [obs[:, i : i + LANE] for i in range(0, obs.shape[1], LANE)]
    height = sum(p.shape[0] for p in parts)
    parts.append(jnp.zeros((-height % 16, LANE), jnp.float32))
    return jnp.concatenate(parts, axis=0)


def halos(z, ldt, obs, axis):
    count = lax.axis_size(axis)
    rows = z.shape[0]

    def shifted(value, by):
        pairs = [(i, i + by) for i in range(count) if 0 <= i + by < count]
        return lax.ppermute(value, axis, pairs)

    def gather(value, width, dim):
        lefts, rights = [], []
        hop, have = 1, 0
        while have < width:
            take = min(rows, width - have)
            lefts.insert(0, shifted(lax.slice_in_dim(value, rows - take, rows, axis=dim), hop))
            rights.append(shifted(lax.slice_in_dim(value, 0, take, axis=dim), -hop))
            have += take
            hop += 1
        return jnp.concatenate(lefts, dim), jnp.concatenate(rights, dim)

    zs = gather(z, HZ, 0)
    lds = gather(ldt, HB, 1)
    seens = gather(obs, HZ, 1)
    return packed(zs[0], lds[0], seens[0]), packed(zs[1], lds[1], seens[1])


def local(dosage, allele_mean, snp_scale, band_next, ld_prev, band_prev, zscores, observed):
    samples, cols = dosage.shape
    rows = ld_prev.shape[0]
    n_smp = lax.axis_size("smp")
    ldt = ld_prev.T
    obs = observed.T
    line = ("snp", "pair")
    paired = rows >= HZ

    sent = pack(dosage, zscores, ldt, obs, paired)
    dos_e = exchange(sent[0], line, 0)
    dos_o = exchange(sent[1], line, 1)
    if paired:
        got_o = exchange(sent[3], ("smp",), 1)
        got_e = exchange(sent[2], ("smp",), 0)
    else:
        got_o, got_e = halos(zscores, ldt, obs, "smp")

    parts = cols // QW
    rot = parts == n_smp == 4 and zscores.shape[1] == LANE
    inv = 1.0 / (samples if rot else samples * n_smp)
    mean = allele_mean.reshape(-1, LANE)
    scale = snp_scale.reshape(-1, LANE)
    made = gram_parts(dosage, mean, scale, rot, inv)
    blocks = cross_parts(dos_e, dos_o, mean, scale, made, cols, rot, inv)
    if rot:

        def shift(value, by):
            return lax.ppermute(value, "smp", [(i, (i + by) % n_smp) for i in range(n_smp)])

        def swap(value, by):
            return lax.ppermute(value, "smp", [(i, i ^ by) for i in range(n_smp)])

        got = [shift(blocks[by], by) for by in (1, 2, 3)]
    w, mom = krylov(ldt, zscores, obs, got_e, got_o, band_prev, paired)
    if rot:
        mine = total_of(blocks[0], got, mom)
        ring = [swap(mine, by) if by else mine for by in RING]
        moms = []
    else:
        ring = list(lax.psum(tuple(blocks), "smp"))
        moms = [lax.psum(mom, "smp")]
    ldn, imputed = final(ring, moms, w, band_next, cols, rot)
    return ldn.T, imputed


def solution(mesh):
    return jax.shard_map(
        local,
        mesh=mesh,
        in_specs=(
            P(("grp", "smp"), ("snp", "pair")),
            P("grp"),
            P("grp"),
            P("grp"),
            P(("grp", "smp"), None),
            P("grp"),
            P(("grp", "smp"), ("snp", "pair")),
            P(("grp", "smp"), ("snp", "pair")),
        ),
        out_specs=(P(("grp", "snp", "pair"), None), P(("grp", "smp"), ("snp", "pair"))),
        check_vma=False,
    )
```

```python
import functools
import jax
import jax.numpy as jnp
from jax import lax
from jax.experimental import pallas as pl
from jax.experimental.pallas import tpu as pltpu
from jax.sharding import PartitionSpec as P


TILE = 64
BMAX = 2
TBLK = 64
ITERS = 3
RIDGE = 1.0
SPAN = 2 * BMAX + 1
REACH = TILE * BMAX
LANE = 128
QW = 256
HZ = ITERS * REACH
HB = (ITERS - 1) * REACH
TINY = 1e-6
VMEM = pl.BlockSpec(memory_space=pltpu.VMEM)


def params(mib):
    return pltpu.CompilerParams(vmem_limit_bytes=mib * 1024 * 1024)


def mask_table(band_ref, first_tile, tiles):
    total = band_ref.shape[1]
    lanes = (tiles + 2 * BMAX) * TILE
    shape = (total, lanes)
    tile = lax.broadcasted_iota(jnp.int32, shape, 1) // TILE + (first_tile - BMAX)
    chosen = tile == lax.broadcasted_iota(jnp.int32, shape, 0)
    given = jnp.broadcast_to(band_ref[...].astype(jnp.float32), (8, total)).astype(jnp.bfloat16)
    widths = dot(given, chosen.astype(jnp.float32).astype(jnp.bfloat16))[:1]
    here = widths[:, BMAX * TILE : (BMAX + tiles) * TILE]
    rows = []
    for q in range(-BMAX, BMAX + 1):
        if q % 2:
            beside = pltpu.roll(widths, (-q * TILE) % lanes, axis=1)[
                :, BMAX * TILE : (BMAX + tiles) * TILE
            ]
        else:
            beside = widths[:, (BMAX + q) * TILE : (BMAX + q + tiles) * TILE]
        rows.append((abs(q) <= jnp.minimum(here, beside)).astype(jnp.float32))
    return rows


def masks_at(table, block):
    return [row[:, block * LANE : (block + 1) * LANE] for row in table]


def low_lanes(shape):
    return lax.broadcasted_iota(jnp.int32, shape, 1) < TILE


def tdot(left, right):
    return lax.dot_general(
        left, right, (((0,), (0,)), ((), ())), preferred_element_type=jnp.float32
    )


def dot(left, right):
    return lax.dot_general(
        left, right, (((1,), (0,)), ((), ())), preferred_element_type=jnp.float32
    )


LEVELS = 32000.0
Z_LARGEST = 22.0
Z_ROOTS = 2
LARGEST = 36.0


def encode(value, largest=LARGEST, roots=3):
    size = jnp.minimum(jnp.abs(value) * (1.0 / largest), 1.0) + 1e-30
    for _ in range(roots):
        size = size * lax.rsqrt(size)
    code = size * LEVELS + 0.5
    return to_code(jnp.where(value < 0, -code, code))


def decode(code, largest=LARGEST, roots=3):
    value = from_code(code)
    size = value * (1.0 / LEVELS)
    for _ in range(roots):
        size = size * size
    size = size * largest
    return jnp.where(value < 0, -size, size)


def encode_exact(value):
    size = jnp.maximum(jnp.abs(value), 1e-30)
    power = jnp.clip(jnp.floor(jnp.log2(size)), -100.0, 120.0)
    scaled = value * jnp.exp2(-power) * 2.0**13
    high = jnp.round(scaled)
    low = jnp.round((scaled - high) * 2.0**14)
    return power, high, low


def decode_exact(power, high, low):
    return (high * 2.0**-13 + low * 2.0**-27) * jnp.exp2(power)


def to_code(value):
    return value.astype(jnp.int32).astype(jnp.int16)


def from_code(code):
    return code.astype(jnp.int32).astype(jnp.float32)


def line_index(axes):
    place = lax.axis_index(axes[0])
    for axis in axes[1:]:
        place = place * lax.axis_size(axis) + lax.axis_index(axis)
    return place


def in_hbm(value):
    return pltpu.with_memory_space_constraint(value, pltpu.HBM)


def halo_height(nb):
    height = HZ + HB // LANE * SPAN * TILE + HZ // LANE * nb
    return height + -height % 16


def pack_kernel(dos, z, ldt, obs, dos_e, dos_o, *rest):
    cols = dos.shape[1]
    rows = z.shape[0]
    sem = rest[-1]
    copies = []

    def start(source, target):
        copy = pltpu.make_async_copy(source, target, sem.at[len(copies)])
        copy.start()
        copies.append(copy)

    even = lax.rem(line_index(("snp", "pair")), 2) == 0
    to_e = pl.multiple_of(jnp.where(even, cols - LANE, 0), LANE)
    to_o = pl.multiple_of(jnp.where(even, 0, cols - LANE), LANE)
    halo = ()
    if len(rest) > 1:
        halo, (zs, lds, flags) = rest[:2], rest[2:5]
        even = lax.rem(lax.axis_index("smp"), 2) == 0
        for i, last in enumerate((even, jnp.logical_not(even))):
            row = pl.multiple_of(jnp.where(last, rows - HZ, 0), LANE)
            col = pl.multiple_of(jnp.where(last, rows - HB, 0), LANE)
            start(z.at[pl.ds(row, HZ), :], zs.at[i])
            start(ldt.at[:, pl.ds(col, HB)], lds.at[i])
            start(obs.at[:, pl.ds(row, HZ)], flags.at[i])
    start(dos.at[:, pl.ds(to_e, LANE)], dos_e)
    start(dos.at[:, pl.ds(to_o, LANE)], dos_o)
    for i, out in enumerate(halo):
        nb = obs.shape[0]
        for copy in copies[3 * i : 3 * i + 3]:
            copy.wait()
        out[0:HZ, : z.shape[1]] = encode(zs[i], Z_LARGEST, Z_ROOTS)
        base = HZ
        for j in range(HB // LANE):
            out[base : base + SPAN * TILE, :] = to_code(
                jnp.round(lds[i, :, j * LANE : (j + 1) * LANE] * LEVELS)
            )
            base += SPAN * TILE
        bits = [flags[i, :, j * LANE : (j + 1) * LANE] for j in range(HZ // LANE)]
        blank = out.shape[0] - base - nb * len(bits)
        bits.append(jnp.zeros((blank, LANE), jnp.int32))
        out[base:, :] = jnp.concatenate(bits, axis=0).astype(jnp.int16)
    for copy in copies[3 * len(halo) :]:
        copy.wait()


def pack(dosage, z, ldt, obs, with_halo):
    samples = dosage.shape[0]
    shapes = [jax.ShapeDtypeStruct((samples, LANE), dosage.dtype)] * 2
    copies = 2
    scratch = []
    if with_halo:
        shapes += [jax.ShapeDtypeStruct((halo_height(obs.shape[0]), LANE), jnp.int16)] * 2
        copies += 6
        scratch = [
            pltpu.VMEM((2, HZ, z.shape[1]), z.dtype),
            pltpu.VMEM((2, SPAN * TILE, HB), ldt.dtype),
            pltpu.VMEM((2, obs.shape[0], HZ), obs.dtype),
        ]
    far = pl.BlockSpec(memory_space=pltpu.HBM)
    return pl.pallas_call(
        pack_kernel,
        in_specs=[far] * 4,
        out_specs=[VMEM] * len(shapes),
        out_shape=shapes,
        scratch_shapes=scratch + [pltpu.SemaphoreType.DMA((copies,))],
        compiler_params=params(8),
        name="pack",
    )(in_hbm(dosage), in_hbm(z), in_hbm(ldt), in_hbm(obs))


def exchange(value, axes, phase):
    count = 1
    for axis in axes:
        count *= lax.axis_size(axis)
    if phase == 0 and lax.axis_size(axes[-1]) == 2 and len(axes) > 1:
        return lax.ppermute(value, axes[-1], [(0, 1), (1, 0)])
    pairs = []
    for i in range(phase, count - 1, 2):
        pairs += [(i, i + 1), (i + 1, i)]
    return lax.ppermute(value, axes, pairs)


DIAG = TILE // 2
CUT = DIAG + TILE
RING = (0, 2, 3, 1)
NEAR = DIAG + BMAX * TILE


def quarter_at(step, first, parts):
    if isinstance(first, int):
        return (step + first) % parts
    return lax.rem(step + first, parts)


def tail_rows(parts):
    return TILE // parts


def standard(values, mean, scale, block):
    row = jnp.clip(block, 0, mean.shape[0] - 1)
    m = mean[pl.ds(row, 1), :]
    s = scale[pl.ds(row, 1), :]
    return ((values.astype(jnp.float32) - m) * s).astype(jnp.bfloat16)


def gram_kernel(parts, rot, inv, dos, mean, scale, *rest):
    outs, (head, last), normed = rest[:parts], rest[parts : parts + 2], rest[parts + 2]
    blocks = QW // LANE
    samples, cols = dos.shape
    base = line_index(("snp", "pair")) * (cols // LANE)
    first = lax.axis_index("smp") if rot else 0
    tail = tail_rows(parts)
    sub = lax.broadcasted_iota(jnp.int32, (TILE, LANE), 0)
    lane = lax.broadcasted_iota(jnp.int32, (TILE, LANE), 1)
    spot = lax.broadcasted_iota(jnp.int32, (tail, LANE), 0)
    low = low_lanes(((BMAX + 1) * TILE, LANE))

    def settle(g):
        block = quarter_at(g, first, parts) * blocks
        for b in range(blocks):
            at = block + b
            if rot:
                at = pl.multiple_of(at * LANE, LANE)
                values = dos[:, pl.ds(at, LANE)]
            else:
                values = dos[:, at * LANE : (at + 1) * LANE]
            normed[g, :, b * LANE : (b + 1) * LANE] = standard(
                values, mean, scale, base + block + b
            )

    settle(0)
    for g in range(parts):
        if g + 1 < parts:
            settle(g + 1)
        own = normed[g]
        top = tdot(own, own)
        bottom = tdot(normed[(g + 1) % parts, :, :LANE], own)
        pieces = []
        for b in range(blocks):
            cut = slice(b * LANE, (b + 1) * LANE)
            full = jnp.concatenate([top[b * LANE :, cut], bottom[:, cut]], axis=0)
            pieces.append(
                inv * jnp.where(low, full[: low.shape[0]], full[TILE : TILE + low.shape[0]])
            )
        folded = [
            jnp.where(sub <= lane, p[:TILE], pltpu.roll(p[:TILE], TILE, axis=1)) for p in pieces
        ]
        folded = jnp.where(lane < TILE, folded[0], pltpu.roll(folded[1], TILE, axis=1))
        diagonals = [
            jnp.sum(jnp.where(sub == lane - TILE, p[:TILE], 0.0), axis=0, keepdims=True)
            for p in pieces
        ]
        ends = jnp.where(spot == 0, diagonals[0], jnp.where(spot == 1, diagonals[1], 0.0))
        send = encode if rot and g > 0 else (lambda v: v)
        for b in range(blocks):
            cut = slice(b * LANE, (b + 1) * LANE)
            outs[g][:DIAG, cut] = send(folded[b * DIAG : (b + 1) * DIAG])
            outs[g][DIAG:NEAR, cut] = send(pieces[b][TILE:])
        outs[g][NEAR:, :LANE] = jnp.zeros((tail, LANE), outs[g].dtype)
        outs[g][NEAR:, LANE:] = send(ends)
    head[...] = normed[lax.rem(parts - first, parts), :, :LANE]
    last[...] = normed[parts - 1 - first, :, (blocks - 1) * LANE :]


def gram_parts(dosage, mean, scale, rot, inv):
    samples, cols = dosage.shape
    parts = cols // QW
    rows = NEAR + tail_rows(parts)
    kinds = [jnp.float32] + [jnp.int16 if rot else jnp.float32] * (parts - 1)
    shapes = [jax.ShapeDtypeStruct((rows, QW), kind) for kind in kinds]
    shapes += [jax.ShapeDtypeStruct((samples, LANE), jnp.bfloat16)] * 2
    return pl.pallas_call(
        functools.partial(gram_kernel, parts, rot, inv),
        in_specs=[VMEM] * 3,
        out_specs=[VMEM] * len(shapes),
        out_shape=shapes,
        scratch_shapes=[pltpu.VMEM((parts, samples, QW), jnp.bfloat16)],
        compiler_params=params(24),
        cost_estimate=pl.CostEstimate(
            flops=2 * samples * cols * (QW + LANE), bytes_accessed=dosage.size * 4, transcendentals=0
        ),
        name="gram",
    )(dosage, mean, scale)


def cross_kernel(parts, rot, inv, cols, head, last, got_e, got_o, mean, scale, *rest):
    ins, (zero, one) = rest[:parts], rest[-2:]
    tops, ends = rest[parts : 2 * parts], rest[2 * parts : 3 * parts]
    blocks = QW // LANE
    tail = tail_rows(parts)
    place = line_index(("snp", "pair"))
    base = place * (cols // LANE)
    end = base + cols // LANE
    even = lax.rem(place, 2) == 0
    pick = lambda one, two: jnp.where(even, one[...], two[...])
    right = standard(pick(got_e, got_o), mean, scale, end)
    left = standard(pick(got_o, got_e), mean, scale, base - 1)
    ahead = inv * tdot(right, last[...])
    behind = inv * tdot(left, head[...])
    low = low_lanes((TILE, LANE))
    turned = pltpu.roll(behind[TILE:], TILE, axis=1)
    zero[...] = jnp.where(low, behind[:TILE], turned)
    one[...] = turned
    far = slice((blocks - 1) * LANE, blocks * LANE)
    first = lax.axis_index("smp") if rot else 0
    for i in range(parts):
        send = encode if rot and i > 0 else (lambda v: v)
        wide = (lambda v: v.astype(jnp.int32)) if rot and i > 0 else (lambda v: v)
        kind = tops[i].dtype
        tops[i][...] = ins[i][:CUT, :]
        ends[i][: NEAR - CUT, :] = ins[i][CUT:NEAR, :]
        quarter = quarter_at(i, first, parts)
        share = pl.ds(pl.multiple_of(quarter * tail, 8) if rot else quarter * tail, tail)
        ends[i][NEAR - CUT :, :LANE] = send(zero[share, :])
        ends[i][NEAR - CUT :, LANE:] = jnp.where(
            low_lanes((tail, LANE)), wide(send(one[share, :])), wide(ins[i][NEAR:, LANE:])
        ).astype(kind)

        def join(i=i, send=send, wide=wide, kind=kind):
            next_one = slice(DIAG, DIAG + TILE)
            tops[i][next_one, far] = jnp.where(
                low, wide(ins[i][next_one, far]), wide(send(ahead[:TILE]))
            ).astype(kind)
            ends[i][: NEAR - CUT, far] = send(jnp.where(low, ahead[:TILE], ahead[TILE:]))

        if rot:
            pl.when(quarter == parts - 1)(join)
        elif i == parts - 1:
            join()


def cross_parts(got_e, got_o, mean, scale, made, cols, rot, inv):
    *blocks, head, last = made
    parts = len(blocks)
    height = NEAR + tail_rows(parts)
    return pl.pallas_call(
        functools.partial(cross_kernel, parts, rot, inv, cols),
        in_specs=[VMEM] * (6 + parts),
        out_specs=[VMEM] * (2 * parts),
        out_shape=[
            jax.ShapeDtypeStruct((rows, QW), b.dtype) for rows in (CUT, height - CUT) for b in blocks
        ],
        scratch_shapes=[pltpu.VMEM((TILE, LANE), jnp.float32)] * 2,
        compiler_params=params(12),
        name="cross",
    )(head, last, got_e, got_o, mean, scale, *blocks)


def total_kernel(count, own, *rest):
    others, mom, out = rest[: count - 1], rest[count - 1 : -1], rest[-1]
    height = own.shape[0]
    total = own[...]
    for other in others:
        total = total + decode(other[...])
    out[0:height, :] = encode(total * (1.0 / count))
    if mom:
        power, high, low = encode_exact(mom[0][...])
        top = jnp.concatenate([power, low], axis=1)
        bottom = jnp.concatenate([high, jnp.zeros_like(low)], axis=1)
        out[height : height + 16, :] = to_code(jnp.concatenate([top, bottom], axis=0))


def total_of(own, others, *mom):
    count = 1 + len(others)
    return pl.pallas_call(
        functools.partial(total_kernel, count),
        in_specs=[VMEM] * (count + len(mom)),
        out_specs=VMEM,
        out_shape=jax.ShapeDtypeStruct((own.shape[0] + 16 * len(mom), own.shape[1]), jnp.int16),
        compiler_params=params(8),
        name="total",
    )(own, *others, *mom)


def final_kernel(parts, rot, moments, band, w, *rest):
    ring = list(zip(rest[:parts], rest[parts : 2 * parts]))
    moms = rest[2 * parts : 2 * parts + moments]
    out_far, imputed_far, held, out, imputed, sem = rest[2 * parts + moments :]
    blocks = QW // LANE
    tail = tail_rows(parts)
    height = NEAR + tail
    low = low_lanes((TILE, LANE))
    sub = lax.broadcasted_iota(jnp.int32, (TILE, LANE), 0)
    lane = lax.broadcasted_iota(jnp.int32, (TILE, LANE), 1)
    cols = out.shape[1]
    first_tile = line_index(("snp", "pair")) * (cols // TILE)
    table = mask_table(band, first_tile, cols // TILE)
    copies = []

    def ship(source, target):
        copy = pltpu.make_async_copy(source, target, sem.at[len(copies)])
        copy.start()
        copies.append(copy)

    def swap(value):
        return pltpu.roll(value, TILE, axis=1)

    if rot:
        k = lax.axis_index("smp")
        total = None
        for (top, end), by in zip(ring, RING):
            quarter = jnp.bitwise_xor(k, by)
            held[quarter, :CUT] = decode(top[...])
            held[quarter, CUT:] = decode(end[: height - CUT, :])
            code = from_code(end[height - CUT :, :])
            lanes = code.shape[1] // 2
            mom = decode_exact(code[:8, :lanes], code[8:, :lanes], code[:8, lanes:])
            total = mom if total is None else total + mom
    else:
        for by in range(parts):
            held[by, :CUT] = ring[by][0][...]
            held[by, CUT:] = ring[by][1][...]
        total = moms[0][...]
    solve(w, total, imputed)
    ship(imputed, imputed_far)
    for quarter in range(parts):
        fold = jnp.concatenate(
            [held[quarter, :DIAG, b * LANE : (b + 1) * LANE] for b in range(blocks)], axis=0
        )
        mirror = jnp.concatenate([fold, swap(fold)], axis=0).T[:TILE]
        for b in range(blocks):
            a = quarter * blocks + b
            cut = slice(b * LANE, (b + 1) * LANE)
            cols_here = slice(a * LANE, (a + 1) * LANE)
            masks = masks_at(table, a)
            here, there = (fold, mirror) if b == 0 else (swap(fold), swap(mirror))
            second = jnp.where(
                sub == lane - TILE,
                held[quarter, NEAR + b : NEAR + b + 1, LANE : 2 * LANE],
                swap(jnp.where(lane < sub, here, there)),
            )
            centre = jnp.where(low, jnp.where(sub <= lane, here, there), second)
            out[BMAX * TILE : (BMAX + 1) * TILE, cols_here] = centre * masks[BMAX]
            for q in range(1, BMAX + 1):
                out[(BMAX + q) * TILE : (BMAX + q + 1) * TILE, cols_here] = (
                    held[quarter, DIAG + (q - 1) * TILE : DIAG + q * TILE, cut] * masks[BMAX + q]
                )
            turned = held[quarter, DIAG:NEAR, cut].T
            rolled = swap(turned)
            if a == 0:
                cross = [
                    jnp.concatenate(
                        [held[j, NEAR:height, c * LANE : (c + 1) * LANE] for j in range(parts)],
                        axis=0,
                    )
                    for c in range(2)
                ]
                one_low, two_low, two_high = swap(cross[0]), cross[0], swap(cross[1])
            else:
                one_low, two_low, two_high = (
                    last_turned[TILE:], last_rolled[:TILE], last_turned[TILE:]
                )
            out[TILE : 2 * TILE, cols_here] = jnp.where(low, one_low, rolled[:TILE]) * masks[1]
            out[0:TILE, cols_here] = jnp.where(low, two_low, two_high) * masks[0]
            last_turned, last_rolled = turned, rolled
        block = slice(quarter * QW, (quarter + 1) * QW)
        ship(out.at[:, block], out_far.at[:, block])
    for copy in copies:
        copy.wait()


def final(ring, moms, w, band_next, cols, rot):
    parts = len(ring) // 2
    shapes = [
        jax.ShapeDtypeStruct((SPAN * TILE, cols), jnp.float32),
        jax.ShapeDtypeStruct(w.shape[1:], jnp.float32),
    ]
    return pl.pallas_call(
        functools.partial(final_kernel, parts, rot, len(moms)),
        in_specs=[VMEM] * (2 + 2 * parts + len(moms)),
        out_specs=[pl.BlockSpec(memory_space=pltpu.HBM)] * 2,
        out_shape=shapes,
        scratch_shapes=[
            pltpu.VMEM((parts, NEAR + tail_rows(parts), QW), jnp.float32),
            pltpu.VMEM(shapes[0].shape, jnp.float32),
            pltpu.VMEM(shapes[1].shape, jnp.float32),
            pltpu.SemaphoreType.DMA((parts + 1,)),
        ],
        compiler_params=params(16),
        name="final",
    )(band_next.reshape(1, -1), w, *ring, *moms)


class Side:
    def __init__(self, flag, one, two):
        self.flag, self.one, self.two = flag, one, two

    def pick(self, at, convert):
        if self.flag is None:
            return self.one[at]
        return jnp.where(self.flag, convert(self.one[at]), convert(self.two[at]))

    def vector(self, at):
        return self.pick(at, lambda code: decode(code, Z_LARGEST, Z_ROOTS))

    def band(self, at):
        return self.pick(at, lambda code: from_code(code) * (1.0 / LEVELS))

    def flags(self, at):
        return self.pick(at, from_code)


def krylov_kernel(
    sb, paired, band, ldt, z, obs, got_o, got_e, w_out, mom_out,
    dh, dl, ucat, seen, u_prev, y
):
    rows = ldt.shape[1]
    traits = z.shape[1]
    own_blocks = rows // LANE
    zb = HZ // LANE
    bb = HB // LANE
    first_tile = lax.axis_index("smp") * (rows // TILE)
    even = lax.rem(lax.axis_index("smp"), 2) == 0 if paired else None
    halo_r = Side(even, got_e, got_o)
    halo_l = Side(even, got_o, got_e)
    nb = obs.shape[0]
    ld_rows = SPAN * TILE
    total_blocks = own_blocks + 2 * zb

    tail = (slice(HZ + bb * ld_rows, got_e.shape[0]), slice(None))
    flags_l, flags_r = halo_l.flags(tail), halo_r.flags(tail)

    for c in range(total_blocks):
        if c < zb:
            vec = halo_l.vector((slice(c * LANE, (c + 1) * LANE), slice(0, traits)))
            flags = [flags_l[c * nb + i : c * nb + i + 1, :] for i in range(nb)]
        elif c < zb + own_blocks:
            o = c - zb
            vec = z[o * LANE : (o + 1) * LANE, :]
            flags = [
                obs[i : i + 1, o * LANE : (o + 1) * LANE].astype(jnp.float32) for i in range(nb)
            ]
        else:
            o = c - zb - own_blocks
            vec = halo_r.vector((slice(o * LANE, (o + 1) * LANE), slice(0, traits)))
            flags = [flags_r[o * nb + i : o * nb + i + 1, :] for i in range(nb)]
        wide = jnp.concatenate(
            [jnp.broadcast_to(f, (TBLK, LANE)) for f in flags], axis=0
        )
        mask = wide.T
        here = slice(c * LANE, (c + 1) * LANE)
        seen[here, :] = mask
        start = mask * vec
        high = start.astype(jnp.bfloat16)
        u_prev[here, :] = start
        ucat[here, :traits] = high
        ucat[here, traits:] = (start - high.astype(jnp.float32)).astype(jnp.bfloat16)

    per = sb // LANE
    low = low_lanes((TILE, LANE))
    sub = lax.broadcasted_iota(jnp.int32, (TILE, LANE), 0)
    lane = lax.broadcasted_iota(jnp.int32, (TILE, LANE), 1)
    chunks = SPAN + 1
    table = mask_table(band, first_tile - HB // TILE, (rows + 2 * HB) // TILE)
    for c in range(own_blocks + 2 * bb):
        if c < bb:
            full = halo_l.band((slice(HZ + c * ld_rows, HZ + (c + 1) * ld_rows), slice(None)))
            get = lambda q, full=full: full[q * TILE : (q + 1) * TILE]
        elif c < bb + own_blocks:
            get = lambda q, c=c: ldt[q * TILE : (q + 1) * TILE, (c - bb) * LANE : (c - bb + 1) * LANE]
        else:
            o = c - bb - own_blocks
            full = halo_r.band((slice(HZ + o * ld_rows, HZ + (o + 1) * ld_rows), slice(None)))
            get = lambda q, full=full: full[q * TILE : (q + 1) * TILE]
        masks = masks_at(table, c)
        s, h = c // per, c % per
        cols = slice(h * LANE, (h + 1) * LANE)
        parts = [get(q) * masks[q] for q in range(SPAN)]
        zero = jnp.zeros((TILE, LANE), jnp.float32)
        for j in range(chunks):
            left = parts[j] if j < SPAN else zero
            right = parts[j - 1] if j >= 1 else zero
            value = jnp.where(low, left, right)
            if BMAX <= j < BMAX + 2:
                value = value - (sub + TILE * (j - BMAX) == lane).astype(jnp.float32)
            high = value.astype(jnp.bfloat16)
            at = slice(h * LANE + j * TILE, h * LANE + (j + 1) * TILE)
            dh[s, at, cols] = high
            dl[s, at, cols] = (value - high.astype(jnp.float32)).astype(jnp.bfloat16)
        for x in range(per):
            if x < h:
                at = slice(x * LANE, (x + 1) * LANE)
            elif x > h:
                at = slice((x + 2) * LANE, (x + 3) * LANE)
            else:
                continue
            blank = jnp.zeros((LANE, LANE), jnp.bfloat16)
            dh[s, at, cols] = blank
            dl[s, at, cols] = blank

    supers = (rows + 2 * HB) // sb
    window = sb + 2 * REACH

    def product(both, rest):
        return both[:, :traits] + both[:, traits:] + rest

    ext = total_blocks * LANE

    def apply(step):
        lo, hi = (step + 1) * REACH, ext - (step + 1) * REACH
        done = 0
        for s in range(supers):
            at = s * sb
            begin = max(REACH + at, lo - REACH)
            end = min(REACH + at + sb, hi + REACH)
            top, bottom = max(at, lo), min(at + window, hi)
            if begin >= end or top >= bottom:
                continue
            r = slice(top - at, bottom - at)
            c = slice(begin - at - REACH, end - at - REACH)
            vec = ucat[begin:end, :]
            part = product(dot(dh[s, r, c], vec), dot(dl[s, r, c], vec[:, :traits]))
            both = min(max(done - top, 0), bottom - top)
            if both:
                y[top : top + both, :] += part[:both]
            if both < bottom - top:
                y[top + both : bottom, :] = part[both:]
            done = max(done, bottom)

    own = slice(HZ, HZ + rows)
    sums = []
    for step in range(ITERS):
        apply(step)
        if step == 0:
            for edge_rows, edge_cols, s, target, source in (
                (slice(0, LANE), slice(0, LANE), 0, 1, 0),
                (
                    slice(window - LANE, window),
                    slice(sb - LANE, sb),
                    supers - 1,
                    total_blocks - 2,
                    total_blocks - 1,
                ),
            ):
                vec = ucat[source * LANE : (source + 1) * LANE, :]
                part = product(
                    tdot(dh[s, edge_rows, edge_cols], vec),
                    tdot(dl[s, edge_rows, edge_cols], vec[:, :traits]),
                )
                y[target * LANE : (target + 1) * LANE, :] += part
        u_own = u_prev[own, :]
        y_own = y[own, :]
        w_out[step] = u_own + y_own
        sums.append(jnp.sum(u_own * u_own, axis=0, keepdims=True))
        sums.append(jnp.sum(u_own * y_own, axis=0, keepdims=True))
        if step < ITERS - 1:
            edge = (step + 1) * REACH
            here = slice(edge, total_blocks * LANE - edge)
            nxt = seen[here, :] * y[here, :]
            high = nxt.astype(jnp.bfloat16)
            u_prev[here, :] = nxt
            ucat[here, :traits] = high
            ucat[here, traits:] = (nxt - high.astype(jnp.float32)).astype(jnp.bfloat16)
    mom_out[...] = jnp.concatenate(
        sums + [jnp.zeros((8 - len(sums), traits), jnp.float32)], axis=0
    )


def krylov(ldt, z, obs, got_e, got_o, band_prev, paired):
    rows, traits = z.shape
    wide = rows + 2 * HB
    sb = 2 * LANE if wide % (2 * LANE) == 0 else LANE
    ext = rows + 2 * HZ
    supers = wide // sb
    return pl.pallas_call(
        functools.partial(krylov_kernel, sb, paired),
        in_specs=[VMEM] * 6,
        out_specs=[VMEM, VMEM],
        out_shape=[
            jax.ShapeDtypeStruct((ITERS, rows, traits), jnp.float32),
            jax.ShapeDtypeStruct((8, traits), jnp.float32),
        ],
        scratch_shapes=[
            pltpu.VMEM((supers, sb + 2 * REACH, sb), jnp.bfloat16),
            pltpu.VMEM((supers, sb + 2 * REACH, sb), jnp.bfloat16),
            pltpu.VMEM((ext, 2 * traits), jnp.bfloat16),
            pltpu.VMEM((ext, traits), jnp.float32),
            pltpu.VMEM((ext, traits), jnp.float32),
            pltpu.VMEM((ext, traits), jnp.float32),
        ],
        compiler_params=params(28),
        cost_estimate=pl.CostEstimate(
            flops=ITERS * 6 * ext * SPAN * TILE * traits, bytes_accessed=ldt.size * 4, transcendentals=0
        ),
        name="krylov",
    )(band_prev.reshape(1, -1), ldt, z, obs, got_o, got_e)


def solve(w, mom, out):
    m = [mom[i : i + 1, :] for i in range(2 * ITERS)]
    shift = 1.0 + RIDGE
    h = [shift * m[i] + m[i + 1] for i in range(2 * ITERS - 1)]
    d0 = h[0]
    l10 = h[1] / d0
    l20 = h[2] / d0
    d1 = h[2] - l10 * h[1]
    t12 = h[3] - l20 * h[1]
    ok1 = d1 > TINY * h[2]
    r1 = jnp.where(ok1, 1.0 / jnp.where(ok1, d1, 1.0), 0.0)
    l21 = t12 * r1
    d2 = h[4] - l20 * h[2] - l21 * t12
    ok2 = ok1 & (d2 > TINY * h[4])
    r2 = jnp.where(ok2, 1.0 / jnp.where(ok2, d2, 1.0), 0.0)
    z0 = m[0]
    z1 = m[1] - l10 * z0
    z2 = m[2] - l20 * z0 - l21 * z1
    c2 = z2 * r2
    c1 = z1 * r1 - l21 * c2
    c0 = z0 / d0 - l10 * c1 - l20 * c2
    out[...] = c0 * w[0] + c1 * w[1] + c2 * w[2]


def packed(z, ldt, obs):
    z = jnp.pad(z, ((0, 0), (0, LANE - z.shape[1])))
    obs = obs.astype(jnp.float32)
    parts = [z]
    parts += [ldt[:, i : i + LANE] for i in range(0, ldt.shape[1], LANE)]
    parts += [obs[:, i : i + LANE] for i in range(0, obs.shape[1], LANE)]
    height = sum(p.shape[0] for p in parts)
    parts.append(jnp.zeros((-height % 16, LANE), jnp.float32))
    return jnp.concatenate(parts, axis=0)


def halos(z, ldt, obs, axis):
    count = lax.axis_size(axis)
    rows = z.shape[0]

    def shifted(value, by):
        pairs = [(i, i + by) for i in range(count) if 0 <= i + by < count]
        return lax.ppermute(value, axis, pairs)

    def gather(value, width, dim):
        lefts, rights = [], []
        hop, have = 1, 0
        while have < width:
            take = min(rows, width - have)
            lefts.insert(0, shifted(lax.slice_in_dim(value, rows - take, rows, axis=dim), hop))
            rights.append(shifted(lax.slice_in_dim(value, 0, take, axis=dim), -hop))
            have += take
            hop += 1
        return jnp.concatenate(lefts, dim), jnp.concatenate(rights, dim)

    zs = gather(z, HZ, 0)
    lds = gather(ldt, HB, 1)
    seens = gather(obs, HZ, 1)
    return packed(zs[0], lds[0], seens[0]), packed(zs[1], lds[1], seens[1])


def local(dosage, allele_mean, snp_scale, band_next, ld_prev, band_prev, zscores, observed):
    samples, cols = dosage.shape
    rows = ld_prev.shape[0]
    n_smp = lax.axis_size("smp")
    ldt = ld_prev.T
    obs = observed.T
    line = ("snp", "pair")
    paired = rows >= HZ

    sent = pack(dosage, zscores, ldt, obs, paired)
    dos_e = exchange(sent[0], line, 0)
    dos_o = exchange(sent[1], line, 1)
    if paired:
        got_o = exchange(sent[3], ("smp",), 1)
        got_e = exchange(sent[2], ("smp",), 0)
    else:
        got_o, got_e = halos(zscores, ldt, obs, "smp")

    parts = cols // QW
    rot = parts == n_smp == 4 and zscores.shape[1] == LANE
    inv = 1.0 / (samples if rot else samples * n_smp)
    mean = allele_mean.reshape(-1, LANE)
    scale = snp_scale.reshape(-1, LANE)
    made = gram_parts(dosage, mean, scale, rot, inv)
    blocks = cross_parts(dos_e, dos_o, mean, scale, made, cols, rot, inv)
    if rot:

        def shift(value, by):
            return lax.ppermute(value, "smp", [(i, (i + by) % n_smp) for i in range(n_smp)])

        def swap(value, by):
            return lax.ppermute(value, "smp", [(i, i ^ by) for i in range(n_smp)])

        tops, ends = blocks[:parts], blocks[parts:]
        got_tops = [shift(tops[by], by) for by in (1, 2, 3)]
        got_ends = [shift(ends[by], by) for by in (1, 2, 3)]
    w, mom = krylov(ldt, zscores, obs, got_e, got_o, band_prev, paired)
    if rot:
        mine = total_of(tops[0], got_tops)
        ring = [swap(mine, by) if by else mine for by in RING]
        mine = total_of(ends[0], got_ends, mom)
        ring += [swap(mine, by) if by else mine for by in RING]
        moms = []
    else:
        ring = list(lax.psum(tuple(blocks), "smp"))
        moms = [lax.psum(mom, "smp")]
    ldn, imputed = final(ring, moms, w, band_next, cols, rot)
    return ldn.T, imputed


def solution(mesh):
    return jax.shard_map(
        local,
        mesh=mesh,
        in_specs=(
            P(("grp", "smp"), ("snp", "pair")),
            P("grp"),
            P("grp"),
            P("grp"),
            P(("grp", "smp"), None),
            P("grp"),
            P(("grp", "smp"), ("snp", "pair")),
            P(("grp", "smp"), ("snp", "pair")),
        ),
        out_specs=(P(("grp", "snp", "pair"), None), P(("grp", "smp"), ("snp", "pair"))),
        check_vma=False,
    )
```

```python
import functools
import jax
import jax.numpy as jnp
from jax import lax
from jax.experimental import pallas as pl
from jax.experimental.pallas import tpu as pltpu
from jax.sharding import PartitionSpec as P

TILE = 64
BMAX = 2
TBLK = 64
ITERS = 3
RIDGE = 1.0
SPAN = 2 * BMAX + 1
REACH = TILE * BMAX
LANE = 128
QW = 256
HZ = ITERS * REACH
HB = (ITERS - 1) * REACH
TINY = 1e-6
VMEM = pl.BlockSpec(memory_space=pltpu.VMEM)


def params(mib):
    return pltpu.CompilerParams(vmem_limit_bytes=mib * 1024 * 1024)


def mask_table(band_ref, first_tile, tiles):
    total = band_ref.shape[1]
    lanes = (tiles + 2 * BMAX) * TILE
    shape = (total, lanes)
    tile = lax.broadcasted_iota(jnp.int32, shape, 1) // TILE + (first_tile - BMAX)
    chosen = tile == lax.broadcasted_iota(jnp.int32, shape, 0)
    given = jnp.broadcast_to(band_ref[...].astype(jnp.float32), (8, total)).astype(jnp.bfloat16)
    widths = dot(given, chosen.astype(jnp.float32).astype(jnp.bfloat16))[:1]
    here = widths[:, BMAX * TILE : (BMAX + tiles) * TILE]
    rows = []
    for q in range(-BMAX, BMAX + 1):
        if q % 2:
            beside = pltpu.roll(widths, (-q * TILE) % lanes, axis=1)[
                :, BMAX * TILE : (BMAX + tiles) * TILE
            ]
        else:
            beside = widths[:, (BMAX + q) * TILE : (BMAX + q + tiles) * TILE]
        rows.append((abs(q) <= jnp.minimum(here, beside)).astype(jnp.float32))
    return rows


def masks_at(table, block):
    return [row[:, block * LANE : (block + 1) * LANE] for row in table]


def low_lanes(shape):
    return lax.broadcasted_iota(jnp.int32, shape, 1) < TILE


def tdot(left, right):
    return lax.dot_general(
        left, right, (((0,), (0,)), ((), ())), preferred_element_type=jnp.float32
    )


def dot(left, right):
    return lax.dot_general(
        left, right, (((1,), (0,)), ((), ())), preferred_element_type=jnp.float32
    )


LEVELS = 32000.0
Z_LARGEST = 22.0
Z_ROOTS = 2
LARGEST = 36.0


def encode(value, largest=LARGEST, roots=3):
    size = jnp.minimum(jnp.abs(value) * (1.0 / largest), 1.0) + 1e-30
    for _ in range(roots):
        size = size * lax.rsqrt(size)
    code = size * LEVELS + 0.5
    return to_code(jnp.where(value < 0, -code, code))


def decode(code, largest=LARGEST, roots=3):
    return decoded(from_code(code), largest, roots)


def decoded(value, largest, roots):
    size = value * (1.0 / LEVELS)
    for _ in range(roots):
        size = size * size
    size = size * largest
    return jnp.where(value < 0, -size, size)


def encode_exact(value):
    size = jnp.maximum(jnp.abs(value), 1e-30)
    power = jnp.clip(jnp.floor(jnp.log2(size)), -100.0, 120.0)
    scaled = value * jnp.exp2(-power) * 2.0**13
    high = jnp.round(scaled)
    low = jnp.round((scaled - high) * 2.0**14)
    return power, high, low


def decode_exact(power, high, low):
    return (high * 2.0**-13 + low * 2.0**-27) * jnp.exp2(power)


def to_code(value):
    return value.astype(jnp.int32).astype(jnp.int16)


def from_code(code):
    return code.astype(jnp.int32).astype(jnp.float32)


def line_index(axes):
    place = lax.axis_index(axes[0])
    for axis in axes[1:]:
        place = place * lax.axis_size(axis) + lax.axis_index(axis)
    return place


def in_hbm(value):
    return pltpu.with_memory_space_constraint(value, pltpu.HBM)


def halo_height(nb):
    height = HZ + HB // LANE * SPAN * TILE + HZ // LANE * nb
    return height + -height % 16


def pack_kernel(dos, z, ldt, obs, dos_e, dos_o, *rest):
    cols = dos.shape[1]
    rows = z.shape[0]
    sem = rest[-1]
    copies = []

    def start(source, target):
        copy = pltpu.make_async_copy(source, target, sem.at[len(copies)])
        copy.start()
        copies.append(copy)

    even = lax.rem(line_index(("snp", "pair")), 2) == 0
    to_e = pl.multiple_of(jnp.where(even, cols - LANE, 0), LANE)
    to_o = pl.multiple_of(jnp.where(even, 0, cols - LANE), LANE)
    halo = ()
    if len(rest) > 1:
        halo, (zs, lds, flags) = rest[:2], rest[2:5]
        even = lax.rem(lax.axis_index("smp"), 2) == 0
        for i, last in enumerate((even, jnp.logical_not(even))):
            row = pl.multiple_of(jnp.where(last, rows - HZ, 0), LANE)
            col = pl.multiple_of(jnp.where(last, rows - HB, 0), LANE)
            start(z.at[pl.ds(row, HZ), :], zs.at[i])
            start(ldt.at[:, pl.ds(col, HB)], lds.at[i])
            start(obs.at[:, pl.ds(row, HZ)], flags.at[i])
    start(dos.at[:, pl.ds(to_e, LANE)], dos_e)
    start(dos.at[:, pl.ds(to_o, LANE)], dos_o)
    for i, out in enumerate(halo):
        nb = obs.shape[0]
        for copy in copies[3 * i : 3 * i + 3]:
            copy.wait()
        out[0:HZ, : z.shape[1]] = encode(zs[i], Z_LARGEST, Z_ROOTS)
        base = HZ
        for j in range(HB // LANE):
            out[base : base + SPAN * TILE, :] = to_code(
                jnp.round(lds[i, :, j * LANE : (j + 1) * LANE] * LEVELS)
            )
            base += SPAN * TILE
        bits = [flags[i, :, j * LANE : (j + 1) * LANE] for j in range(HZ // LANE)]
        blank = out.shape[0] - base - nb * len(bits)
        bits.append(jnp.zeros((blank, LANE), jnp.int32))
        out[base:, :] = jnp.concatenate(bits, axis=0).astype(jnp.int16)
    for copy in copies[3 * len(halo) :]:
        copy.wait()


def pack(dosage, z, ldt, obs, with_halo):
    samples = dosage.shape[0]
    shapes = [jax.ShapeDtypeStruct((samples, LANE), dosage.dtype)] * 2
    copies = 2
    scratch = []
    if with_halo:
        shapes += [jax.ShapeDtypeStruct((halo_height(obs.shape[0]), LANE), jnp.int16)] * 2
        copies += 6
        scratch = [
            pltpu.VMEM((2, HZ, z.shape[1]), z.dtype),
            pltpu.VMEM((2, SPAN * TILE, HB), ldt.dtype),
            pltpu.VMEM((2, obs.shape[0], HZ), obs.dtype),
        ]
    far = pl.BlockSpec(memory_space=pltpu.HBM)
    return pl.pallas_call(
        pack_kernel,
        in_specs=[far] * 4,
        out_specs=[VMEM] * len(shapes),
        out_shape=shapes,
        scratch_shapes=scratch + [pltpu.SemaphoreType.DMA((copies,))],
        compiler_params=params(8),
        name="pack",
    )(in_hbm(dosage), in_hbm(z), in_hbm(ldt), in_hbm(obs))


def exchange(value, axes, phase):
    count = 1
    for axis in axes:
        count *= lax.axis_size(axis)
    if phase == 0 and lax.axis_size(axes[-1]) == 2 and len(axes) > 1:
        return lax.ppermute(value, axes[-1], [(0, 1), (1, 0)])
    pairs = []
    for i in range(phase, count - 1, 2):
        pairs += [(i, i + 1), (i + 1, i)]
    return lax.ppermute(value, axes, pairs)


DIAG = TILE // 2
RING = (0, 2, 3, 1)
NEAR = DIAG + BMAX * TILE


def quarter_at(step, first, parts):
    if isinstance(first, int):
        return (step + first) % parts
    return lax.rem(step + first, parts)


def tail_rows(parts):
    return TILE // parts


def standard(values, mean, scale, block):
    row = jnp.clip(block, 0, mean.shape[0] - 1)
    m = mean[pl.ds(row, 1), :]
    s = scale[pl.ds(row, 1), :]
    return ((values.astype(jnp.float32) - m) * s).astype(jnp.bfloat16)


def gram_kernel(parts, rot, inv, dos, mean, scale, *rest):
    outs, (head, last), normed = rest[:parts], rest[parts : parts + 2], rest[parts + 2]
    blocks = QW // LANE
    samples, cols = dos.shape
    base = line_index(("snp", "pair")) * (cols // LANE)
    first = lax.axis_index("smp") if rot else 0
    tail = tail_rows(parts)
    sub = lax.broadcasted_iota(jnp.int32, (TILE, LANE), 0)
    lane = lax.broadcasted_iota(jnp.int32, (TILE, LANE), 1)
    spot = lax.broadcasted_iota(jnp.int32, (tail, LANE), 0)
    low = low_lanes(((BMAX + 1) * TILE, LANE))

    def settle(g):
        block = quarter_at(g, first, parts) * blocks
        for b in range(blocks):
            at = block + b
            if rot:
                at = pl.multiple_of(at * LANE, LANE)
                values = dos[:, pl.ds(at, LANE)]
            else:
                values = dos[:, at * LANE : (at + 1) * LANE]
            normed[g, :, b * LANE : (b + 1) * LANE] = standard(
                values, mean, scale, base + block + b
            )

    settle(0)
    for g in range(parts):
        if g + 1 < parts:
            settle(g + 1)
        own = normed[g]
        top = tdot(own, own)
        bottom = tdot(normed[(g + 1) % parts, :, :LANE], own)
        pieces = []
        for b in range(blocks):
            cut = slice(b * LANE, (b + 1) * LANE)
            full = jnp.concatenate([top[b * LANE :, cut], bottom[:, cut]], axis=0)
            pieces.append(
                inv * jnp.where(low, full[: low.shape[0]], full[TILE : TILE + low.shape[0]])
            )
        folded = [
            jnp.where(sub <= lane, p[:TILE], pltpu.roll(p[:TILE], TILE, axis=1)) for p in pieces
        ]
        folded = jnp.where(lane < TILE, folded[0], pltpu.roll(folded[1], TILE, axis=1))
        diagonals = [
            jnp.sum(jnp.where(sub == lane - TILE, p[:TILE], 0.0), axis=0, keepdims=True)
            for p in pieces
        ]
        ends = jnp.where(spot == 0, diagonals[0], jnp.where(spot == 1, diagonals[1], 0.0))
        send = encode if rot and g > 0 else (lambda v: v)
        for b in range(blocks):
            cut = slice(b * LANE, (b + 1) * LANE)
            outs[g][:DIAG, cut] = send(folded[b * DIAG : (b + 1) * DIAG])
            outs[g][DIAG:NEAR, cut] = send(pieces[b][TILE:])
        outs[g][NEAR:, :LANE] = jnp.zeros((tail, LANE), outs[g].dtype)
        outs[g][NEAR:, LANE:] = send(ends)
    head[...] = normed[lax.rem(parts - first, parts), :, :LANE]
    last[...] = normed[parts - 1 - first, :, (blocks - 1) * LANE :]


def gram_parts(dosage, mean, scale, rot, inv):
    samples, cols = dosage.shape
    parts = cols // QW
    rows = NEAR + tail_rows(parts)
    kinds = [jnp.float32] + [jnp.int16 if rot else jnp.float32] * (parts - 1)
    shapes = [jax.ShapeDtypeStruct((rows, QW), kind) for kind in kinds]
    shapes += [jax.ShapeDtypeStruct((samples, LANE), jnp.bfloat16)] * 2
    return pl.pallas_call(
        functools.partial(gram_kernel, parts, rot, inv),
        in_specs=[VMEM] * 3,
        out_specs=[VMEM] * len(shapes),
        out_shape=shapes,
        scratch_shapes=[pltpu.VMEM((parts, samples, QW), jnp.bfloat16)],
        compiler_params=params(24),
        cost_estimate=pl.CostEstimate(
            flops=2 * samples * cols * (QW + LANE), bytes_accessed=dosage.size * 4, transcendentals=0
        ),
        name="gram",
    )(dosage, mean, scale)


def cross_kernel(parts, rot, inv, cols, head, last, got_e, got_o, mean, scale, *rest):
    ins, outs, (zero, one) = rest[:parts], rest[parts : 2 * parts], rest[-2:]
    blocks = QW // LANE
    tail = tail_rows(parts)
    place = line_index(("snp", "pair"))
    base = place * (cols // LANE)
    end = base + cols // LANE
    even = lax.rem(place, 2) == 0
    pick = lambda one, two: jnp.where(even, one[...], two[...])
    right = standard(pick(got_e, got_o), mean, scale, end)
    left = standard(pick(got_o, got_e), mean, scale, base - 1)
    ahead = inv * tdot(right, last[...])
    behind = inv * tdot(left, head[...])
    low = low_lanes((TILE, LANE))
    turned = pltpu.roll(behind[TILE:], TILE, axis=1)
    zero[...] = jnp.where(low, behind[:TILE], turned)
    one[...] = turned
    far = slice((blocks - 1) * LANE, blocks * LANE)
    first = lax.axis_index("smp") if rot else 0
    for i in range(parts):
        send = encode if rot and i > 0 else (lambda v: v)
        wide = (lambda v: v.astype(jnp.int32)) if rot and i > 0 else (lambda v: v)
        kind = outs[i].dtype
        outs[i][:NEAR, :] = ins[i][:NEAR, :]
        quarter = quarter_at(i, first, parts)
        share = pl.ds(pl.multiple_of(quarter * tail, 8) if rot else quarter * tail, tail)
        outs[i][NEAR:, :LANE] = send(zero[share, :])
        outs[i][NEAR:, LANE:] = jnp.where(
            low_lanes((tail, LANE)), wide(send(one[share, :])), wide(ins[i][NEAR:, LANE:])
        ).astype(kind)

        def join(i=i, send=send, wide=wide, kind=kind):
            next_one = slice(DIAG, DIAG + TILE)
            outs[i][next_one, far] = jnp.where(
                low, wide(ins[i][next_one, far]), wide(send(ahead[:TILE]))
            ).astype(kind)
            outs[i][DIAG + TILE : NEAR, far] = send(jnp.where(low, ahead[:TILE], ahead[TILE:]))

        if rot:
            pl.when(quarter == parts - 1)(join)
        elif i == parts - 1:
            join()


def cross_parts(got_e, got_o, mean, scale, made, cols, rot, inv):
    *blocks, head, last = made
    parts = len(blocks)
    height = NEAR + tail_rows(parts)
    return pl.pallas_call(
        functools.partial(cross_kernel, parts, rot, inv, cols),
        in_specs=[VMEM] * (6 + parts),
        out_specs=[VMEM] * parts,
        out_shape=[jax.ShapeDtypeStruct((height, QW), b.dtype) for b in blocks],
        scratch_shapes=[pltpu.VMEM((TILE, LANE), jnp.float32)] * 2,
        compiler_params=params(12),
        name="cross",
    )(head, last, got_e, got_o, mean, scale, *blocks)


def total_kernel(count, own, *rest):
    others, mom, out = rest[:-2], rest[-2], rest[-1]
    height = own.shape[0]
    total = own[...]
    for other in others:
        total = total + decode(other[...])
    out[0:height, :] = encode(total * (1.0 / count))
    power, high, low = encode_exact(mom[...])
    lanes = mom.shape[1]
    top = jnp.concatenate([power, low], axis=1)
    bottom = jnp.concatenate([high, jnp.zeros_like(low)], axis=1)
    out[height : height + 16, :] = to_code(jnp.concatenate([top, bottom], axis=0))


def total_of(own, others, mom):
    count = 1 + len(others)
    return pl.pallas_call(
        functools.partial(total_kernel, count),
        in_specs=[VMEM] * (count + 1),
        out_specs=VMEM,
        out_shape=jax.ShapeDtypeStruct((own.shape[0] + 16, own.shape[1]), jnp.int16),
        compiler_params=params(8),
        name="total",
    )(own, *others, mom)


def final_kernel(parts, rot, moments, band, w, *rest):
    ring = rest[:parts]
    moms = rest[parts : parts + moments]
    out_far, imputed_far, held, out, imputed, sem = rest[parts + moments :]
    blocks = QW // LANE
    tail = tail_rows(parts)
    height = NEAR + tail
    low = low_lanes((TILE, LANE))
    sub = lax.broadcasted_iota(jnp.int32, (TILE, LANE), 0)
    lane = lax.broadcasted_iota(jnp.int32, (TILE, LANE), 1)
    cols = out.shape[1]
    first_tile = line_index(("snp", "pair")) * (cols // TILE)
    table = mask_table(band, first_tile, cols // TILE)
    copies = []

    def ship(source, target):
        copy = pltpu.make_async_copy(source, target, sem.at[len(copies)])
        copy.start()
        copies.append(copy)

    def swap(value):
        return pltpu.roll(value, TILE, axis=1)

    if rot:
        k = lax.axis_index("smp")
        total = None
        for piece, by in zip(ring, RING):
            held[jnp.bitwise_xor(k, by)] = decode(piece[0:height, :])
            code = from_code(piece[height : height + 16, :])
            lanes = code.shape[1] // 2
            mom = decode_exact(code[:8, :lanes], code[8:, :lanes], code[:8, lanes:])
            total = mom if total is None else total + mom
    else:
        for by in range(parts):
            held[by] = ring[by][...]
        total = moms[0][...]
    solve(w, total, imputed)
    ship(imputed, imputed_far)
    for quarter in range(parts):
        fold = jnp.concatenate(
            [held[quarter, :DIAG, b * LANE : (b + 1) * LANE] for b in range(blocks)], axis=0
        )
        mirror = jnp.concatenate([fold, swap(fold)], axis=0).T[:TILE]
        for b in range(blocks):
            a = quarter * blocks + b
            cut = slice(b * LANE, (b + 1) * LANE)
            cols_here = slice(a * LANE, (a + 1) * LANE)
            masks = masks_at(table, a)
            here, there = (fold, mirror) if b == 0 else (swap(fold), swap(mirror))
            second = jnp.where(
                sub == lane - TILE,
                held[quarter, NEAR + b : NEAR + b + 1, LANE : 2 * LANE],
                swap(jnp.where(lane < sub, here, there)),
            )
            centre = jnp.where(low, jnp.where(sub <= lane, here, there), second)
            out[BMAX * TILE : (BMAX + 1) * TILE, cols_here] = centre * masks[BMAX]
            for q in range(1, BMAX + 1):
                out[(BMAX + q) * TILE : (BMAX + q + 1) * TILE, cols_here] = (
                    held[quarter, DIAG + (q - 1) * TILE : DIAG + q * TILE, cut] * masks[BMAX + q]
                )
            turned = held[quarter, DIAG:NEAR, cut].T
            rolled = swap(turned)
            if a == 0:
                cross = [
                    jnp.concatenate(
                        [held[j, NEAR:height, c * LANE : (c + 1) * LANE] for j in range(parts)],
                        axis=0,
                    )
                    for c in range(2)
                ]
                one_low, two_low, two_high = swap(cross[0]), cross[0], swap(cross[1])
            else:
                one_low, two_low, two_high = (
                    last_turned[TILE:], last_rolled[:TILE], last_turned[TILE:]
                )
            out[TILE : 2 * TILE, cols_here] = jnp.where(low, one_low, rolled[:TILE]) * masks[1]
            out[0:TILE, cols_here] = jnp.where(low, two_low, two_high) * masks[0]
            last_turned, last_rolled = turned, rolled
        block = slice(quarter * QW, (quarter + 1) * QW)
        ship(out.at[:, block], out_far.at[:, block])
    for copy in copies:
        copy.wait()


def final(ring, moms, w, band_next, cols, rot):
    parts = len(ring)
    shapes = [
        jax.ShapeDtypeStruct((SPAN * TILE, cols), jnp.float32),
        jax.ShapeDtypeStruct(w.shape[1:], jnp.float32),
    ]
    return pl.pallas_call(
        functools.partial(final_kernel, parts, rot, len(moms)),
        in_specs=[VMEM] * (2 + parts + len(moms)),
        out_specs=[pl.BlockSpec(memory_space=pltpu.HBM)] * 2,
        out_shape=shapes,
        scratch_shapes=[
            pltpu.VMEM((parts, NEAR + tail_rows(parts), QW), jnp.float32),
            pltpu.VMEM(shapes[0].shape, jnp.float32),
            pltpu.VMEM(shapes[1].shape, jnp.float32),
            pltpu.SemaphoreType.DMA((parts + 1,)),
        ],
        compiler_params=params(16),
        name="final",
    )(band_next.reshape(1, -1), w, *ring, *moms)


class Side:
    def __init__(self, flag, one, two):
        self.flag, self.one, self.two = flag, one, two

    def pick(self, at, convert):
        if self.flag is None:
            return self.one[at]
        return convert(jnp.where(self.flag, from_code(self.one[at]), from_code(self.two[at])))

    def vector(self, at):
        return self.pick(at, lambda value: decoded(value, Z_LARGEST, Z_ROOTS))

    def band(self, at):
        return self.pick(at, lambda value: value * (1.0 / LEVELS))

    def flags(self, at):
        return self.pick(at, lambda value: value)


def krylov_kernel(
    sb, paired, band, ldt, z, obs, got_o, got_e, w_out, mom_out,
    dh, dl, ucat, seen, u_prev, y
):
    rows = ldt.shape[1]
    traits = z.shape[1]
    own_blocks = rows // LANE
    zb = HZ // LANE
    bb = HB // LANE
    first_tile = lax.axis_index("smp") * (rows // TILE)
    even = lax.rem(lax.axis_index("smp"), 2) == 0 if paired else None
    halo_r = Side(even, got_e, got_o)
    halo_l = Side(even, got_o, got_e)
    nb = obs.shape[0]
    ld_rows = SPAN * TILE
    total_blocks = own_blocks + 2 * zb

    tail = (slice(HZ + bb * ld_rows, got_e.shape[0]), slice(None))
    flags_l, flags_r = halo_l.flags(tail), halo_r.flags(tail)

    for c in range(total_blocks):
        if c < zb:
            vec = halo_l.vector((slice(c * LANE, (c + 1) * LANE), slice(0, traits)))
            flags = [flags_l[c * nb + i : c * nb + i + 1, :] for i in range(nb)]
        elif c < zb + own_blocks:
            o = c - zb
            vec = z[o * LANE : (o + 1) * LANE, :]
            flags = [
                obs[i : i + 1, o * LANE : (o + 1) * LANE].astype(jnp.float32) for i in range(nb)
            ]
        else:
            o = c - zb - own_blocks
            vec = halo_r.vector((slice(o * LANE, (o + 1) * LANE), slice(0, traits)))
            flags = [flags_r[o * nb + i : o * nb + i + 1, :] for i in range(nb)]
        wide = jnp.concatenate(
            [jnp.broadcast_to(f, (TBLK, LANE)) for f in flags], axis=0
        )
        mask = wide.T
        here = slice(c * LANE, (c + 1) * LANE)
        seen[here, :] = mask
        start = mask * vec
        high = start.astype(jnp.bfloat16)
        u_prev[here, :] = start
        ucat[here, :traits] = high
        ucat[here, traits:] = (start - high.astype(jnp.float32)).astype(jnp.bfloat16)

    per = sb // LANE
    low = low_lanes((TILE, LANE))
    sub = lax.broadcasted_iota(jnp.int32, (TILE, LANE), 0)
    lane = lax.broadcasted_iota(jnp.int32, (TILE, LANE), 1)
    chunks = SPAN + 1
    table = mask_table(band, first_tile - HB // TILE, (rows + 2 * HB) // TILE)
    for c in range(own_blocks + 2 * bb):
        if c < bb:
            full = halo_l.band((slice(HZ + c * ld_rows, HZ + (c + 1) * ld_rows), slice(None)))
            get = lambda q, full=full: full[q * TILE : (q + 1) * TILE]
        elif c < bb + own_blocks:
            get = lambda q, c=c: ldt[q * TILE : (q + 1) * TILE, (c - bb) * LANE : (c - bb + 1) * LANE]
        else:
            o = c - bb - own_blocks
            full = halo_r.band((slice(HZ + o * ld_rows, HZ + (o + 1) * ld_rows), slice(None)))
            get = lambda q, full=full: full[q * TILE : (q + 1) * TILE]
        masks = masks_at(table, c)
        s, h = c // per, c % per
        cols = slice(h * LANE, (h + 1) * LANE)
        parts = [get(q) * masks[q] for q in range(SPAN)]
        zero = jnp.zeros((TILE, LANE), jnp.float32)
        for j in range(chunks):
            left = parts[j] if j < SPAN else zero
            right = parts[j - 1] if j >= 1 else zero
            value = jnp.where(low, left, right)
            if BMAX <= j < BMAX + 2:
                value = value - (sub + TILE * (j - BMAX) == lane).astype(jnp.float32)
            high = value.astype(jnp.bfloat16)
            at = slice(h * LANE + j * TILE, h * LANE + (j + 1) * TILE)
            dh[s, at, cols] = high
            dl[s, at, cols] = (value - high.astype(jnp.float32)).astype(jnp.bfloat16)
        for x in range(per):
            if x < h:
                at = slice(x * LANE, (x + 1) * LANE)
            elif x > h:
                at = slice((x + 2) * LANE, (x + 3) * LANE)
            else:
                continue
            blank = jnp.zeros((LANE, LANE), jnp.bfloat16)
            dh[s, at, cols] = blank
            dl[s, at, cols] = blank

    supers = (rows + 2 * HB) // sb
    window = sb + 2 * REACH

    def product(both, rest):
        return both[:, :traits] + both[:, traits:] + rest

    ext = total_blocks * LANE

    def apply(step):
        lo, hi = (step + 1) * REACH, ext - (step + 1) * REACH
        done = 0
        for s in range(supers):
            at = s * sb
            begin = max(REACH + at, lo - REACH)
            end = min(REACH + at + sb, hi + REACH)
            top, bottom = max(at, lo), min(at + window, hi)
            if begin >= end or top >= bottom:
                continue
            r = slice(top - at, bottom - at)
            c = slice(begin - at - REACH, end - at - REACH)
            vec = ucat[begin:end, :]
            part = product(dot(dh[s, r, c], vec), dot(dl[s, r, c], vec[:, :traits]))
            both = min(max(done - top, 0), bottom - top)
            if both:
                y[top : top + both, :] += part[:both]
            if both < bottom - top:
                y[top + both : bottom, :] = part[both:]
            done = max(done, bottom)

    own = slice(HZ, HZ + rows)
    sums = []
    for step in range(ITERS):
        apply(step)
        if step == 0:
            for edge_rows, edge_cols, s, target, source in (
                (slice(0, LANE), slice(0, LANE), 0, 1, 0),
                (
                    slice(window - LANE, window),
                    slice(sb - LANE, sb),
                    supers - 1,
                    total_blocks - 2,
                    total_blocks - 1,
                ),
            ):
                vec = ucat[source * LANE : (source + 1) * LANE, :]
                part = product(
                    tdot(dh[s, edge_rows, edge_cols], vec),
                    tdot(dl[s, edge_rows, edge_cols], vec[:, :traits]),
                )
                y[target * LANE : (target + 1) * LANE, :] += part
        u_own = u_prev[own, :]
        y_own = y[own, :]
        w_out[step] = u_own + y_own
        sums.append(jnp.sum(u_own * u_own, axis=0, keepdims=True))
        sums.append(jnp.sum(u_own * y_own, axis=0, keepdims=True))
        if step < ITERS - 1:
            edge = (step + 1) * REACH
            here = slice(edge, total_blocks * LANE - edge)
            nxt = seen[here, :] * y[here, :]
            high = nxt.astype(jnp.bfloat16)
            u_prev[here, :] = nxt
            ucat[here, :traits] = high
            ucat[here, traits:] = (nxt - high.astype(jnp.float32)).astype(jnp.bfloat16)
    mom_out[...] = jnp.concatenate(
        sums + [jnp.zeros((8 - len(sums), traits), jnp.float32)], axis=0
    )


def krylov(ldt, z, obs, got_e, got_o, band_prev, paired):
    rows, traits = z.shape
    wide = rows + 2 * HB
    sb = 2 * LANE if wide % (2 * LANE) == 0 else LANE
    ext = rows + 2 * HZ
    supers = wide // sb
    return pl.pallas_call(
        functools.partial(krylov_kernel, sb, paired),
        in_specs=[VMEM] * 6,
        out_specs=[VMEM, VMEM],
        out_shape=[
            jax.ShapeDtypeStruct((ITERS, rows, traits), jnp.float32),
            jax.ShapeDtypeStruct((8, traits), jnp.float32),
        ],
        scratch_shapes=[
            pltpu.VMEM((supers, sb + 2 * REACH, sb), jnp.bfloat16),
            pltpu.VMEM((supers, sb + 2 * REACH, sb), jnp.bfloat16),
            pltpu.VMEM((ext, 2 * traits), jnp.bfloat16),
            pltpu.VMEM((ext, traits), jnp.float32),
            pltpu.VMEM((ext, traits), jnp.float32),
            pltpu.VMEM((ext, traits), jnp.float32),
        ],
        compiler_params=params(28),
        cost_estimate=pl.CostEstimate(
            flops=ITERS * 6 * ext * SPAN * TILE * traits, bytes_accessed=ldt.size * 4, transcendentals=0
        ),
        name="krylov",
    )(band_prev.reshape(1, -1), ldt, z, obs, got_o, got_e)


def solve(w, mom, out):
    m = [mom[i : i + 1, :] for i in range(2 * ITERS)]
    shift = 1.0 + RIDGE
    h = [shift * m[i] + m[i + 1] for i in range(2 * ITERS - 1)]
    d0 = h[0]
    l10 = h[1] / d0
    l20 = h[2] / d0
    d1 = h[2] - l10 * h[1]
    t12 = h[3] - l20 * h[1]
    ok1 = d1 > TINY * h[2]
    r1 = jnp.where(ok1, 1.0 / jnp.where(ok1, d1, 1.0), 0.0)
    l21 = t12 * r1
    d2 = h[4] - l20 * h[2] - l21 * t12
    ok2 = ok1 & (d2 > TINY * h[4])
    r2 = jnp.where(ok2, 1.0 / jnp.where(ok2, d2, 1.0), 0.0)
    z0 = m[0]
    z1 = m[1] - l10 * z0
    z2 = m[2] - l20 * z0 - l21 * z1
    c2 = z2 * r2
    c1 = z1 * r1 - l21 * c2
    c0 = z0 / d0 - l10 * c1 - l20 * c2
    out[...] = c0 * w[0] + c1 * w[1] + c2 * w[2]


def packed(z, ldt, obs):
    z = jnp.pad(z, ((0, 0), (0, LANE - z.shape[1])))
    obs = obs.astype(jnp.float32)
    parts = [z]
    parts += [ldt[:, i : i + LANE] for i in range(0, ldt.shape[1], LANE)]
    parts += [obs[:, i : i + LANE] for i in range(0, obs.shape[1], LANE)]
    height = sum(p.shape[0] for p in parts)
    parts.append(jnp.zeros((-height % 16, LANE), jnp.float32))
    return jnp.concatenate(parts, axis=0)


def halos(z, ldt, obs, axis):
    count = lax.axis_size(axis)
    rows = z.shape[0]

    def shifted(value, by):
        pairs = [(i, i + by) for i in range(count) if 0 <= i + by < count]
        return lax.ppermute(value, axis, pairs)

    def gather(value, width, dim):
        lefts, rights = [], []
        hop, have = 1, 0
        while have < width:
            take = min(rows, width - have)
            lefts.insert(0, shifted(lax.slice_in_dim(value, rows - take, rows, axis=dim), hop))
            rights.append(shifted(lax.slice_in_dim(value, 0, take, axis=dim), -hop))
            have += take
            hop += 1
        return jnp.concatenate(lefts, dim), jnp.concatenate(rights, dim)

    zs = gather(z, HZ, 0)
    lds = gather(ldt, HB, 1)
    seens = gather(obs, HZ, 1)
    return packed(zs[0], lds[0], seens[0]), packed(zs[1], lds[1], seens[1])


def local(dosage, allele_mean, snp_scale, band_next, ld_prev, band_prev, zscores, observed):
    samples, cols = dosage.shape
    rows = ld_prev.shape[0]
    n_smp = lax.axis_size("smp")
    ldt = ld_prev.T
    obs = observed.T
    line = ("snp", "pair")
    paired = rows >= HZ

    sent = pack(dosage, zscores, ldt, obs, paired)
    dos_e = exchange(sent[0], line, 0)
    dos_o = exchange(sent[1], line, 1)
    if paired:
        got_o = exchange(sent[3], ("smp",), 1)
        got_e = exchange(sent[2], ("smp",), 0)
    else:
        got_o, got_e = halos(zscores, ldt, obs, "smp")

    parts = cols // QW
    rot = parts == n_smp == 4 and zscores.shape[1] == LANE
    inv = 1.0 / (samples if rot else samples * n_smp)
    mean = allele_mean.reshape(-1, LANE)
    scale = snp_scale.reshape(-1, LANE)
    made = gram_parts(dosage, mean, scale, rot, inv)
    blocks = cross_parts(dos_e, dos_o, mean, scale, made, cols, rot, inv)
    if rot:

        def shift(value, by):
            return lax.ppermute(value, "smp", [(i, (i + by) % n_smp) for i in range(n_smp)])

        def swap(value, by):
            return lax.ppermute(value, "smp", [(i, i ^ by) for i in range(n_smp)])

        got = [shift(blocks[by], by) for by in (1, 3, 2)]
    w, mom = krylov(ldt, zscores, obs, got_e, got_o, band_prev, paired)
    if rot:
        mine = total_of(blocks[0], got, mom)
        ring = [swap(mine, by) if by else mine for by in RING]
        moms = []
    else:
        ring = list(lax.psum(tuple(blocks), "smp"))
        moms = [lax.psum(mom, "smp")]
    ldn, imputed = final(ring, moms, w, band_next, cols, rot)
    return ldn.T, imputed


def solution(mesh):
    return jax.shard_map(
        local,
        mesh=mesh,
        in_specs=(
            P(("grp", "smp"), ("snp", "pair")),
            P("grp"),
            P("grp"),
            P("grp"),
            P(("grp", "smp"), None),
            P("grp"),
            P(("grp", "smp"), ("snp", "pair")),
            P(("grp", "smp"), ("snp", "pair")),
        ),
        out_specs=(P(("grp", "snp", "pair"), None), P(("grp", "smp"), ("snp", "pair"))),
        check_vma=False,
    )
```

```python
import functools
import jax
import jax.numpy as jnp
from jax import lax
from jax.experimental import pallas as pl
from jax.experimental.pallas import tpu as pltpu
from jax.sharding import PartitionSpec as P

TILE = 64
BMAX = 2
TBLK = 64
ITERS = 3
RIDGE = 1.0
SPAN = 2 * BMAX + 1
REACH = TILE * BMAX
LANE = 128
QW = 256
HZ = ITERS * REACH
HB = (ITERS - 1) * REACH
TINY = 1e-6
VMEM = pl.BlockSpec(memory_space=pltpu.VMEM)


def params(mib):
    return pltpu.CompilerParams(vmem_limit_bytes=mib * 1024 * 1024)


def mask_table(band_ref, first_tile, tiles):
    total = band_ref.shape[1]
    lanes = (tiles + 2 * BMAX) * TILE
    shape = (total, lanes)
    tile = lax.broadcasted_iota(jnp.int32, shape, 1) // TILE + (first_tile - BMAX)
    chosen = tile == lax.broadcasted_iota(jnp.int32, shape, 0)
    given = jnp.broadcast_to(band_ref[...].astype(jnp.float32), (8, total)).astype(jnp.bfloat16)
    widths = dot(given, chosen.astype(jnp.float32).astype(jnp.bfloat16))[:1]
    here = widths[:, BMAX * TILE : (BMAX + tiles) * TILE]
    rows = []
    for q in range(-BMAX, BMAX + 1):
        if q % 2:
            beside = pltpu.roll(widths, (-q * TILE) % lanes, axis=1)[
                :, BMAX * TILE : (BMAX + tiles) * TILE
            ]
        else:
            beside = widths[:, (BMAX + q) * TILE : (BMAX + q + tiles) * TILE]
        rows.append((abs(q) <= jnp.minimum(here, beside)).astype(jnp.float32))
    return rows


def masks_at(table, block):
    return [row[:, block * LANE : (block + 1) * LANE] for row in table]


def low_lanes(shape):
    return lax.broadcasted_iota(jnp.int32, shape, 1) < TILE


def tdot(left, right):
    return lax.dot_general(
        left, right, (((0,), (0,)), ((), ())), preferred_element_type=jnp.float32
    )


def dot(left, right):
    return lax.dot_general(
        left, right, (((1,), (0,)), ((), ())), preferred_element_type=jnp.float32
    )


LEVELS = 32000.0
Z_LARGEST = 22.0
Z_ROOTS = 2
LARGEST = 36.0


def encode(value, largest=LARGEST, roots=3):
    size = jnp.minimum(jnp.abs(value) * (1.0 / largest), 1.0) + 1e-30
    for _ in range(roots):
        size = size * lax.rsqrt(size)
    code = size * LEVELS + 0.5
    return to_code(jnp.where(value < 0, -code, code))


def decode(code, largest=LARGEST, roots=3):
    return decoded(from_code(code), largest, roots)


def decoded(value, largest, roots):
    size = value * (1.0 / LEVELS)
    for _ in range(roots):
        size = size * size
    size = size * largest
    return jnp.where(value < 0, -size, size)


def encode_exact(value):
    size = jnp.maximum(jnp.abs(value), 1e-30)
    power = jnp.clip(jnp.floor(jnp.log2(size)), -100.0, 120.0)
    scaled = value * jnp.exp2(-power) * 2.0**13
    high = jnp.round(scaled)
    low = jnp.round((scaled - high) * 2.0**14)
    return power, high, low


def decode_exact(power, high, low):
    return (high * 2.0**-13 + low * 2.0**-27) * jnp.exp2(power)


def to_code(value):
    return value.astype(jnp.int32).astype(jnp.int16)


def from_code(code):
    return code.astype(jnp.int32).astype(jnp.float32)


def line_index(axes):
    place = lax.axis_index(axes[0])
    for axis in axes[1:]:
        place = place * lax.axis_size(axis) + lax.axis_index(axis)
    return place


def in_hbm(value):
    return pltpu.with_memory_space_constraint(value, pltpu.HBM)


def halo_height(nb):
    height = HZ + HB // LANE * SPAN * TILE + HZ // LANE * nb
    return height + -height % 16


def pack_kernel(dos, z, ldt, obs, dos_e, dos_o, *rest):
    cols = dos.shape[1]
    rows = z.shape[0]
    sem = rest[-1]
    copies = []

    def start(source, target):
        copy = pltpu.make_async_copy(source, target, sem.at[len(copies)])
        copy.start()
        copies.append(copy)

    even = lax.rem(line_index(("snp", "pair")), 2) == 0
    to_e = pl.multiple_of(jnp.where(even, cols - LANE, 0), LANE)
    to_o = pl.multiple_of(jnp.where(even, 0, cols - LANE), LANE)
    halo = ()
    if len(rest) > 1:
        halo, (zs, lds, flags) = rest[:2], rest[2:5]
        even = lax.rem(lax.axis_index("smp"), 2) == 0
        for i, last in enumerate((even, jnp.logical_not(even))):
            row = pl.multiple_of(jnp.where(last, rows - HZ, 0), LANE)
            col = pl.multiple_of(jnp.where(last, rows - HB, 0), LANE)
            start(z.at[pl.ds(row, HZ), :], zs.at[i])
            start(ldt.at[:, pl.ds(col, HB)], lds.at[i])
            start(obs.at[:, pl.ds(row, HZ)], flags.at[i])
    start(dos.at[:, pl.ds(to_e, LANE)], dos_e)
    start(dos.at[:, pl.ds(to_o, LANE)], dos_o)
    for i, out in enumerate(halo):
        nb = obs.shape[0]
        for copy in copies[3 * i : 3 * i + 3]:
            copy.wait()
        out[0:HZ, : z.shape[1]] = encode(zs[i], Z_LARGEST, Z_ROOTS)
        base = HZ
        for j in range(HB // LANE):
            out[base : base + SPAN * TILE, :] = to_code(
                jnp.round(lds[i, :, j * LANE : (j + 1) * LANE] * LEVELS)
            )
            base += SPAN * TILE
        bits = [flags[i, :, j * LANE : (j + 1) * LANE] for j in range(HZ // LANE)]
        blank = out.shape[0] - base - nb * len(bits)
        bits.append(jnp.zeros((blank, LANE), jnp.int32))
        out[base:, :] = jnp.concatenate(bits, axis=0).astype(jnp.int16)
    for copy in copies[3 * len(halo) :]:
        copy.wait()


def pack(dosage, z, ldt, obs, with_halo):
    samples = dosage.shape[0]
    shapes = [jax.ShapeDtypeStruct((samples, LANE), dosage.dtype)] * 2
    copies = 2
    scratch = []
    if with_halo:
        shapes += [jax.ShapeDtypeStruct((halo_height(obs.shape[0]), LANE), jnp.int16)] * 2
        copies += 6
        scratch = [
            pltpu.VMEM((2, HZ, z.shape[1]), z.dtype),
            pltpu.VMEM((2, SPAN * TILE, HB), ldt.dtype),
            pltpu.VMEM((2, obs.shape[0], HZ), obs.dtype),
        ]
    far = pl.BlockSpec(memory_space=pltpu.HBM)
    return pl.pallas_call(
        pack_kernel,
        in_specs=[far] * 4,
        out_specs=[VMEM] * len(shapes),
        out_shape=shapes,
        scratch_shapes=scratch + [pltpu.SemaphoreType.DMA((copies,))],
        compiler_params=params(8),
        name="pack",
    )(in_hbm(dosage), in_hbm(z), in_hbm(ldt), in_hbm(obs))


def exchange(value, axes, phase):
    count = 1
    for axis in axes:
        count *= lax.axis_size(axis)
    if phase == 0 and lax.axis_size(axes[-1]) == 2 and len(axes) > 1:
        return lax.ppermute(value, axes[-1], [(0, 1), (1, 0)])
    pairs = []
    for i in range(phase, count - 1, 2):
        pairs += [(i, i + 1), (i + 1, i)]
    return lax.ppermute(value, axes, pairs)


DIAG = TILE // 2
RING = (0, 2, 3, 1)
NEAR = DIAG + BMAX * TILE


def quarter_at(step, first, parts):
    if isinstance(first, int):
        return (step + first) % parts
    return lax.rem(step + first, parts)


def tail_rows(parts):
    return TILE // parts


def standard(values, mean, scale, block):
    row = jnp.clip(block, 0, mean.shape[0] - 1)
    m = mean[pl.ds(row, 1), :]
    s = scale[pl.ds(row, 1), :]
    return ((values.astype(jnp.float32) - m) * s).astype(jnp.bfloat16)


def gram_kernel(parts, rot, inv, dos, mean, scale, *rest):
    outs, (head, last), normed = rest[:parts], rest[parts : parts + 2], rest[parts + 2]
    blocks = QW // LANE
    samples, cols = dos.shape
    base = line_index(("snp", "pair")) * (cols // LANE)
    first = lax.axis_index("smp") if rot else 0
    tail = tail_rows(parts)
    sub = lax.broadcasted_iota(jnp.int32, (TILE, LANE), 0)
    lane = lax.broadcasted_iota(jnp.int32, (TILE, LANE), 1)
    spot = lax.broadcasted_iota(jnp.int32, (tail, LANE), 0)
    low = low_lanes(((BMAX + 1) * TILE, LANE))

    def settle(g):
        block = quarter_at(g, first, parts) * blocks
        for b in range(blocks):
            at = block + b
            if rot:
                at = pl.multiple_of(at * LANE, LANE)
                values = dos[:, pl.ds(at, LANE)]
            else:
                values = dos[:, at * LANE : (at + 1) * LANE]
            normed[g, :, b * LANE : (b + 1) * LANE] = standard(
                values, mean, scale, base + block + b
            )

    settle(0)
    for g in range(parts):
        if g + 1 < parts:
            settle(g + 1)
        own = normed[g]
        top = tdot(own, own)
        bottom = tdot(normed[(g + 1) % parts, :, :LANE], own)
        pieces = []
        for b in range(blocks):
            cut = slice(b * LANE, (b + 1) * LANE)
            full = jnp.concatenate([top[b * LANE :, cut], bottom[:, cut]], axis=0)
            pieces.append(
                inv * jnp.where(low, full[: low.shape[0]], full[TILE : TILE + low.shape[0]])
            )
        folded = [
            jnp.where(sub <= lane, p[:TILE], pltpu.roll(p[:TILE], TILE, axis=1)) for p in pieces
        ]
        folded = jnp.where(lane < TILE, folded[0], pltpu.roll(folded[1], TILE, axis=1))
        diagonals = [
            jnp.sum(jnp.where(sub == lane - TILE, p[:TILE], 0.0), axis=0, keepdims=True)
            for p in pieces
        ]
        ends = jnp.where(spot == 0, diagonals[0], jnp.where(spot == 1, diagonals[1], 0.0))
        send = encode if rot and g > 0 else (lambda v: v)
        for b in range(blocks):
            cut = slice(b * LANE, (b + 1) * LANE)
            outs[g][:DIAG, cut] = send(folded[b * DIAG : (b + 1) * DIAG])
            outs[g][DIAG:NEAR, cut] = send(pieces[b][TILE:])
        outs[g][NEAR:, :LANE] = jnp.zeros((tail, LANE), outs[g].dtype)
        outs[g][NEAR:, LANE:] = send(ends)
    head[...] = normed[lax.rem(parts - first, parts), :, :LANE]
    last[...] = normed[parts - 1 - first, :, (blocks - 1) * LANE :]


def gram_parts(dosage, mean, scale, rot, inv):
    samples, cols = dosage.shape
    parts = cols // QW
    rows = NEAR + tail_rows(parts)
    kinds = [jnp.float32] + [jnp.int16 if rot else jnp.float32] * (parts - 1)
    shapes = [jax.ShapeDtypeStruct((rows, QW), kind) for kind in kinds]
    shapes += [jax.ShapeDtypeStruct((samples, LANE), jnp.bfloat16)] * 2
    return pl.pallas_call(
        functools.partial(gram_kernel, parts, rot, inv),
        in_specs=[VMEM] * 3,
        out_specs=[VMEM] * len(shapes),
        out_shape=shapes,
        scratch_shapes=[pltpu.VMEM((parts, samples, QW), jnp.bfloat16)],
        compiler_params=params(24),
        cost_estimate=pl.CostEstimate(
            flops=2 * samples * cols * (QW + LANE), bytes_accessed=dosage.size * 4, transcendentals=0
        ),
        name="gram",
    )(dosage, mean, scale)


def cross_kernel(parts, rot, inv, cols, head, last, got_e, got_o, mean, scale, *rest):
    ins, outs, (zero, one) = rest[:parts], rest[parts : 2 * parts], rest[-2:]
    blocks = QW // LANE
    tail = tail_rows(parts)
    place = line_index(("snp", "pair"))
    base = place * (cols // LANE)
    end = base + cols // LANE
    even = lax.rem(place, 2) == 0
    pick = lambda one, two: jnp.where(even, one[...], two[...])
    right = standard(pick(got_e, got_o), mean, scale, end)
    left = standard(pick(got_o, got_e), mean, scale, base - 1)
    ahead = inv * tdot(right, last[...])
    behind = inv * tdot(left, head[...])
    low = low_lanes((TILE, LANE))
    turned = pltpu.roll(behind[TILE:], TILE, axis=1)
    zero[...] = jnp.where(low, behind[:TILE], turned)
    one[...] = turned
    far = slice((blocks - 1) * LANE, blocks * LANE)
    first = lax.axis_index("smp") if rot else 0
    for i in range(parts):
        send = encode if rot and i > 0 else (lambda v: v)
        wide = (lambda v: v.astype(jnp.int32)) if rot and i > 0 else (lambda v: v)
        kind = outs[i].dtype
        outs[i][:NEAR, :] = ins[i][:NEAR, :]
        quarter = quarter_at(i, first, parts)
        share = pl.ds(pl.multiple_of(quarter * tail, 8) if rot else quarter * tail, tail)
        outs[i][NEAR:, :LANE] = send(zero[share, :])
        outs[i][NEAR:, LANE:] = jnp.where(
            low_lanes((tail, LANE)), wide(send(one[share, :])), wide(ins[i][NEAR:, LANE:])
        ).astype(kind)

        def join(i=i, send=send, wide=wide, kind=kind):
            next_one = slice(DIAG, DIAG + TILE)
            outs[i][next_one, far] = jnp.where(
                low, wide(ins[i][next_one, far]), wide(send(ahead[:TILE]))
            ).astype(kind)
            outs[i][DIAG + TILE : NEAR, far] = send(jnp.where(low, ahead[:TILE], ahead[TILE:]))

        if rot:
            pl.when(quarter == parts - 1)(join)
        elif i == parts - 1:
            join()


def cross_parts(got_e, got_o, mean, scale, made, cols, rot, inv):
    *blocks, head, last = made
    parts = len(blocks)
    height = NEAR + tail_rows(parts)
    return pl.pallas_call(
        functools.partial(cross_kernel, parts, rot, inv, cols),
        in_specs=[VMEM] * (6 + parts),
        out_specs=[VMEM] * parts,
        out_shape=[jax.ShapeDtypeStruct((height, QW), b.dtype) for b in blocks],
        scratch_shapes=[pltpu.VMEM((TILE, LANE), jnp.float32)] * 2,
        compiler_params=params(12),
        name="cross",
    )(head, last, got_e, got_o, mean, scale, *blocks)


def total_kernel(count, own, *rest):
    others, mom, out = rest[:-2], rest[-2], rest[-1]
    height = own.shape[0]
    total = own[...]
    for other in others:
        total = total + decode(other[...])
    out[0:height, :] = encode(total * (1.0 / count))
    power, high, low = encode_exact(mom[...])
    lanes = mom.shape[1]
    top = jnp.concatenate([power, low], axis=1)
    bottom = jnp.concatenate([high, jnp.zeros_like(low)], axis=1)
    out[height : height + 16, :] = to_code(jnp.concatenate([top, bottom], axis=0))


def total_of(own, others, mom):
    count = 1 + len(others)
    return pl.pallas_call(
        functools.partial(total_kernel, count),
        in_specs=[VMEM] * (count + 1),
        out_specs=VMEM,
        out_shape=jax.ShapeDtypeStruct((own.shape[0] + 16, own.shape[1]), jnp.int16),
        compiler_params=params(8),
        name="total",
    )(own, *others, mom)


def final_kernel(parts, rot, moments, band, w, *rest):
    ring = rest[:parts]
    moms = rest[parts : parts + moments]
    out_far, imputed_far, held, out, imputed, sem = rest[parts + moments :]
    blocks = QW // LANE
    tail = tail_rows(parts)
    height = NEAR + tail
    low = low_lanes((TILE, LANE))
    sub = lax.broadcasted_iota(jnp.int32, (TILE, LANE), 0)
    lane = lax.broadcasted_iota(jnp.int32, (TILE, LANE), 1)
    cols = out.shape[1]
    first_tile = line_index(("snp", "pair")) * (cols // TILE)
    table = mask_table(band, first_tile, cols // TILE)
    copies = []

    def ship(source, target):
        copy = pltpu.make_async_copy(source, target, sem.at[len(copies)])
        copy.start()
        copies.append(copy)

    def swap(value):
        return pltpu.roll(value, TILE, axis=1)

    if rot:
        k = lax.axis_index("smp")
        total = None
        for piece, by in zip(ring, RING):
            held[jnp.bitwise_xor(k, by)] = decode(piece[0:height, :])
            code = from_code(piece[height : height + 16, :])
            lanes = code.shape[1] // 2
            mom = decode_exact(code[:8, :lanes], code[8:, :lanes], code[:8, lanes:])
            total = mom if total is None else total + mom
    else:
        for by in range(parts):
            held[by] = ring[by][...]
        total = moms[0][...]
    solve(w, total, imputed)
    ship(imputed, imputed_far)
    for quarter in range(parts):
        fold = jnp.concatenate(
            [held[quarter, :DIAG, b * LANE : (b + 1) * LANE] for b in range(blocks)], axis=0
        )
        mirror = jnp.concatenate([fold, swap(fold)], axis=0).T[:TILE]
        for b in range(blocks):
            a = quarter * blocks + b
            cut = slice(b * LANE, (b + 1) * LANE)
            cols_here = slice(a * LANE, (a + 1) * LANE)
            masks = masks_at(table, a)
            here, there = (fold, mirror) if b == 0 else (swap(fold), swap(mirror))
            second = jnp.where(
                sub == lane - TILE,
                held[quarter, NEAR + b : NEAR + b + 1, LANE : 2 * LANE],
                swap(jnp.where(lane < sub, here, there)),
            )
            centre = jnp.where(low, jnp.where(sub <= lane, here, there), second)
            out[BMAX * TILE : (BMAX + 1) * TILE, cols_here] = centre * masks[BMAX]
            for q in range(1, BMAX + 1):
                out[(BMAX + q) * TILE : (BMAX + q + 1) * TILE, cols_here] = (
                    held[quarter, DIAG + (q - 1) * TILE : DIAG + q * TILE, cut] * masks[BMAX + q]
                )
            turned = held[quarter, DIAG:NEAR, cut].T
            rolled = swap(turned)
            if a == 0:
                cross = [
                    jnp.concatenate(
                        [held[j, NEAR:height, c * LANE : (c + 1) * LANE] for j in range(parts)],
                        axis=0,
                    )
                    for c in range(2)
                ]
                one_low, two_low, two_high = swap(cross[0]), cross[0], swap(cross[1])
            else:
                one_low, two_low, two_high = (
                    last_turned[TILE:], last_rolled[:TILE], last_turned[TILE:]
                )
            out[TILE : 2 * TILE, cols_here] = jnp.where(low, one_low, rolled[:TILE]) * masks[1]
            out[0:TILE, cols_here] = jnp.where(low, two_low, two_high) * masks[0]
            last_turned, last_rolled = turned, rolled
        block = slice(quarter * QW, (quarter + 1) * QW)
        ship(out.at[:, block], out_far.at[:, block])
    for copy in copies:
        copy.wait()


def final(ring, moms, w, band_next, cols, rot):
    parts = len(ring)
    shapes = [
        jax.ShapeDtypeStruct((SPAN * TILE, cols), jnp.float32),
        jax.ShapeDtypeStruct(w.shape[1:], jnp.float32),
    ]
    return pl.pallas_call(
        functools.partial(final_kernel, parts, rot, len(moms)),
        in_specs=[VMEM] * (2 + parts + len(moms)),
        out_specs=[pl.BlockSpec(memory_space=pltpu.HBM)] * 2,
        out_shape=shapes,
        scratch_shapes=[
            pltpu.VMEM((parts, NEAR + tail_rows(parts), QW), jnp.float32),
            pltpu.VMEM(shapes[0].shape, jnp.float32),
            pltpu.VMEM(shapes[1].shape, jnp.float32),
            pltpu.SemaphoreType.DMA((parts + 1,)),
        ],
        compiler_params=params(16),
        name="final",
    )(band_next.reshape(1, -1), w, *ring, *moms)


class Side:
    def __init__(self, flag, one, two):
        self.flag, self.one, self.two = flag, one, two

    def pick(self, at, convert):
        if self.flag is None:
            return self.one[at]
        return convert(jnp.where(self.flag, from_code(self.one[at]), from_code(self.two[at])))

    def vector(self, at):
        return self.pick(at, lambda value: decoded(value, Z_LARGEST, Z_ROOTS))

    def band(self, at):
        return self.pick(at, lambda value: value * (1.0 / LEVELS))

    def flags(self, at):
        return self.pick(at, lambda value: value)


def krylov_kernel(
    sb, paired, band, ldt, z, obs, got_o, got_e, w_out, mom_out,
    dh, dl, ucat, seen, u_prev, y
):
    rows = ldt.shape[1]
    traits = z.shape[1]
    own_blocks = rows // LANE
    zb = HZ // LANE
    bb = HB // LANE
    first_tile = lax.axis_index("smp") * (rows // TILE)
    even = lax.rem(lax.axis_index("smp"), 2) == 0 if paired else None
    halo_r = Side(even, got_e, got_o)
    halo_l = Side(even, got_o, got_e)
    nb = obs.shape[0]
    ld_rows = SPAN * TILE
    total_blocks = own_blocks + 2 * zb

    tail = (slice(HZ + bb * ld_rows, got_e.shape[0]), slice(None))
    flags_l, flags_r = halo_l.flags(tail), halo_r.flags(tail)

    for c in range(total_blocks):
        if c < zb:
            vec = halo_l.vector((slice(c * LANE, (c + 1) * LANE), slice(0, traits)))
            flags = [flags_l[c * nb + i : c * nb + i + 1, :] for i in range(nb)]
        elif c < zb + own_blocks:
            o = c - zb
            vec = z[o * LANE : (o + 1) * LANE, :]
            flags = [
                obs[i : i + 1, o * LANE : (o + 1) * LANE].astype(jnp.float32) for i in range(nb)
            ]
        else:
            o = c - zb - own_blocks
            vec = halo_r.vector((slice(o * LANE, (o + 1) * LANE), slice(0, traits)))
            flags = [flags_r[o * nb + i : o * nb + i + 1, :] for i in range(nb)]
        wide = jnp.concatenate(
            [jnp.broadcast_to(f, (TBLK, LANE)) for f in flags], axis=0
        )
        mask = wide.T
        here = slice(c * LANE, (c + 1) * LANE)
        seen[here, :] = mask
        start = mask * vec
        high = start.astype(jnp.bfloat16)
        u_prev[here, :] = start
        ucat[here, :traits] = high
        ucat[here, traits:] = (start - high.astype(jnp.float32)).astype(jnp.bfloat16)

    per = sb // LANE
    low = low_lanes((TILE, LANE))
    sub = lax.broadcasted_iota(jnp.int32, (TILE, LANE), 0)
    lane = lax.broadcasted_iota(jnp.int32, (TILE, LANE), 1)
    chunks = SPAN + 1
    table = mask_table(band, first_tile - HB // TILE, (rows + 2 * HB) // TILE)
    for c in range(own_blocks + 2 * bb):
        if c < bb:
            full = halo_l.band((slice(HZ + c * ld_rows, HZ + (c + 1) * ld_rows), slice(None)))
            get = lambda q, full=full: full[q * TILE : (q + 1) * TILE]
        elif c < bb + own_blocks:
            get = lambda q, c=c: ldt[q * TILE : (q + 1) * TILE, (c - bb) * LANE : (c - bb + 1) * LANE]
        else:
            o = c - bb - own_blocks
            full = halo_r.band((slice(HZ + o * ld_rows, HZ + (o + 1) * ld_rows), slice(None)))
            get = lambda q, full=full: full[q * TILE : (q + 1) * TILE]
        masks = masks_at(table, c)
        s, h = c // per, c % per
        cols = slice(h * LANE, (h + 1) * LANE)
        parts = [get(q) * masks[q] for q in range(SPAN)]
        zero = jnp.zeros((TILE, LANE), jnp.float32)
        for j in range(chunks):
            left = parts[j] if j < SPAN else zero
            right = parts[j - 1] if j >= 1 else zero
            value = jnp.where(low, left, right)
            if BMAX <= j < BMAX + 2:
                value = value - (sub + TILE * (j - BMAX) == lane).astype(jnp.float32)
            high = value.astype(jnp.bfloat16)
            at = slice(h * LANE + j * TILE, h * LANE + (j + 1) * TILE)
            dh[s, at, cols] = high
            dl[s, at, cols] = (value - high.astype(jnp.float32)).astype(jnp.bfloat16)
        for x in range(per):
            if x < h:
                at = slice(x * LANE, (x + 1) * LANE)
            elif x > h:
                at = slice((x + 2) * LANE, (x + 3) * LANE)
            else:
                continue
            blank = jnp.zeros((LANE, LANE), jnp.bfloat16)
            dh[s, at, cols] = blank
            dl[s, at, cols] = blank

    supers = (rows + 2 * HB) // sb
    window = sb + 2 * REACH

    def product(both, rest):
        return both[:, :traits] + both[:, traits:] + rest

    ext = total_blocks * LANE

    def apply(step):
        lo, hi = (step + 1) * REACH, ext - (step + 1) * REACH
        done = 0
        for s in range(supers):
            at = s * sb
            begin = max(REACH + at, lo - REACH)
            end = min(REACH + at + sb, hi + REACH)
            top, bottom = max(at, lo), min(at + window, hi)
            if begin >= end or top >= bottom:
                continue
            r = slice(top - at, bottom - at)
            c = slice(begin - at - REACH, end - at - REACH)
            vec = ucat[begin:end, :]
            part = product(dot(dh[s, r, c], vec), dot(dl[s, r, c], vec[:, :traits]))
            both = min(max(done - top, 0), bottom - top)
            if both:
                y[top : top + both, :] += part[:both]
            if both < bottom - top:
                y[top + both : bottom, :] = part[both:]
            done = max(done, bottom)

    own = slice(HZ, HZ + rows)
    sums = []
    for step in range(ITERS):
        apply(step)
        if step == 0:
            for edge_rows, edge_cols, s, target, source in (
                (slice(0, LANE), slice(0, LANE), 0, 1, 0),
                (
                    slice(window - LANE, window),
                    slice(sb - LANE, sb),
                    supers - 1,
                    total_blocks - 2,
                    total_blocks - 1,
                ),
            ):
                vec = ucat[source * LANE : (source + 1) * LANE, :]
                part = product(
                    tdot(dh[s, edge_rows, edge_cols], vec),
                    tdot(dl[s, edge_rows, edge_cols], vec[:, :traits]),
                )
                y[target * LANE : (target + 1) * LANE, :] += part
        u_own = u_prev[own, :]
        y_own = y[own, :]
        w_out[step] = u_own + y_own
        sums.append(jnp.sum(u_own * u_own, axis=0, keepdims=True))
        sums.append(jnp.sum(u_own * y_own, axis=0, keepdims=True))
        if step < ITERS - 1:
            edge = (step + 1) * REACH
            here = slice(edge, total_blocks * LANE - edge)
            nxt = seen[here, :] * y[here, :]
            high = nxt.astype(jnp.bfloat16)
            u_prev[here, :] = nxt
            ucat[here, :traits] = high
            ucat[here, traits:] = (nxt - high.astype(jnp.float32)).astype(jnp.bfloat16)
    mom_out[...] = jnp.concatenate(
        sums + [jnp.zeros((8 - len(sums), traits), jnp.float32)], axis=0
    )


def krylov(ldt, z, obs, got_e, got_o, band_prev, paired):
    rows, traits = z.shape
    wide = rows + 2 * HB
    sb = 2 * LANE if wide % (2 * LANE) == 0 else LANE
    ext = rows + 2 * HZ
    supers = wide // sb
    return pl.pallas_call(
        functools.partial(krylov_kernel, sb, paired),
        in_specs=[VMEM] * 6,
        out_specs=[VMEM, VMEM],
        out_shape=[
            jax.ShapeDtypeStruct((ITERS, rows, traits), jnp.float32),
            jax.ShapeDtypeStruct((8, traits), jnp.float32),
        ],
        scratch_shapes=[
            pltpu.VMEM((supers, sb + 2 * REACH, sb), jnp.bfloat16),
            pltpu.VMEM((supers, sb + 2 * REACH, sb), jnp.bfloat16),
            pltpu.VMEM((ext, 2 * traits), jnp.bfloat16),
            pltpu.VMEM((ext, traits), jnp.float32),
            pltpu.VMEM((ext, traits), jnp.float32),
            pltpu.VMEM((ext, traits), jnp.float32),
        ],
        compiler_params=params(28),
        cost_estimate=pl.CostEstimate(
            flops=ITERS * 6 * ext * SPAN * TILE * traits, bytes_accessed=ldt.size * 4, transcendentals=0
        ),
        name="krylov",
    )(band_prev.reshape(1, -1), ldt, z, obs, got_o, got_e)


def solve(w, mom, out):
    m = [mom[i : i + 1, :] for i in range(2 * ITERS)]
    shift = 1.0 + RIDGE
    h = [shift * m[i] + m[i + 1] for i in range(2 * ITERS - 1)]
    d0 = h[0]
    l10 = h[1] / d0
    l20 = h[2] / d0
    d1 = h[2] - l10 * h[1]
    t12 = h[3] - l20 * h[1]
    ok1 = d1 > TINY * h[2]
    r1 = jnp.where(ok1, 1.0 / jnp.where(ok1, d1, 1.0), 0.0)
    l21 = t12 * r1
    d2 = h[4] - l20 * h[2] - l21 * t12
    ok2 = ok1 & (d2 > TINY * h[4])
    r2 = jnp.where(ok2, 1.0 / jnp.where(ok2, d2, 1.0), 0.0)
    z0 = m[0]
    z1 = m[1] - l10 * z0
    z2 = m[2] - l20 * z0 - l21 * z1
    c2 = z2 * r2
    c1 = z1 * r1 - l21 * c2
    c0 = z0 / d0 - l10 * c1 - l20 * c2
    out[...] = c0 * w[0] + c1 * w[1] + c2 * w[2]


def packed(z, ldt, obs):
    z = jnp.pad(z, ((0, 0), (0, LANE - z.shape[1])))
    obs = obs.astype(jnp.float32)
    parts = [z]
    parts += [ldt[:, i : i + LANE] for i in range(0, ldt.shape[1], LANE)]
    parts += [obs[:, i : i + LANE] for i in range(0, obs.shape[1], LANE)]
    height = sum(p.shape[0] for p in parts)
    parts.append(jnp.zeros((-height % 16, LANE), jnp.float32))
    return jnp.concatenate(parts, axis=0)


def halos(z, ldt, obs, axis):
    count = lax.axis_size(axis)
    rows = z.shape[0]

    def shifted(value, by):
        pairs = [(i, i + by) for i in range(count) if 0 <= i + by < count]
        return lax.ppermute(value, axis, pairs)

    def gather(value, width, dim):
        lefts, rights = [], []
        hop, have = 1, 0
        while have < width:
            take = min(rows, width - have)
            lefts.insert(0, shifted(lax.slice_in_dim(value, rows - take, rows, axis=dim), hop))
            rights.append(shifted(lax.slice_in_dim(value, 0, take, axis=dim), -hop))
            have += take
            hop += 1
        return jnp.concatenate(lefts, dim), jnp.concatenate(rights, dim)

    zs = gather(z, HZ, 0)
    lds = gather(ldt, HB, 1)
    seens = gather(obs, HZ, 1)
    return packed(zs[0], lds[0], seens[0]), packed(zs[1], lds[1], seens[1])


def local(dosage, allele_mean, snp_scale, band_next, ld_prev, band_prev, zscores, observed):
    samples, cols = dosage.shape
    rows = ld_prev.shape[0]
    n_smp = lax.axis_size("smp")
    ldt = ld_prev.T
    obs = observed.T
    line = ("snp", "pair")
    paired = rows >= HZ

    sent = pack(dosage, zscores, ldt, obs, paired)
    dos_e = exchange(sent[0], line, 0)
    dos_o = exchange(sent[1], line, 1)
    if paired:
        got_o = exchange(sent[3], ("smp",), 1)
        got_e = exchange(sent[2], ("smp",), 0)
    else:
        got_o, got_e = halos(zscores, ldt, obs, "smp")

    parts = cols // QW
    rot = parts == n_smp == 4 and zscores.shape[1] == LANE
    inv = 1.0 / (samples if rot else samples * n_smp)
    mean = allele_mean.reshape(-1, LANE)
    scale = snp_scale.reshape(-1, LANE)
    made = gram_parts(dosage, mean, scale, rot, inv)
    blocks = cross_parts(dos_e, dos_o, mean, scale, made, cols, rot, inv)
    if rot:

        def shift(value, by):
            return lax.ppermute(value, "smp", [(i, (i + by) % n_smp) for i in range(n_smp)])

        def swap(value, by):
            return lax.ppermute(value, "smp", [(i, i ^ by) for i in range(n_smp)])

        got = [shift(blocks[by], by) for by in (3, 2, 1)]
    w, mom = krylov(ldt, zscores, obs, got_e, got_o, band_prev, paired)
    if rot:
        mine = total_of(blocks[0], got, mom)
        ring = [swap(mine, by) if by else mine for by in RING]
        moms = []
    else:
        ring = list(lax.psum(tuple(blocks), "smp"))
        moms = [lax.psum(mom, "smp")]
    ldn, imputed = final(ring, moms, w, band_next, cols, rot)
    return ldn.T, imputed


def solution(mesh):
    return jax.shard_map(
        local,
        mesh=mesh,
        in_specs=(
            P(("grp", "smp"), ("snp", "pair")),
            P("grp"),
            P("grp"),
            P("grp"),
            P(("grp", "smp"), None),
            P("grp"),
            P(("grp", "smp"), ("snp", "pair")),
            P(("grp", "smp"), ("snp", "pair")),
        ),
        out_specs=(P(("grp", "snp", "pair"), None), P(("grp", "smp"), ("snp", "pair"))),
        check_vma=False,
    )
```
